32 devices in a mesh: dp: 16 (over z, x, core), tensor: 2 (over y).
Axes of the slice: x: 2, y: 2, z: 4, core: 2. Of those that a mesh axis runs over, the one named last changes fastest.
Arguments:
- block_input: bfloat16 [32, 1024, 768], P('dp', 'tensor'), may hold values from -6 to 6
- skip_values: bfloat16 [32, 1024, 384], P('dp', None, 'tensor'), may hold values from -6 to 6
- segment_ids: int32 [32, 1024], P('dp'), may hold values from 0 to 7, never falling along the last dimension, each value on 1 to 256 neighbouring positions
- row_fill: int32 [32], P('dp'), may hold values from 512 to 1024, as said below
- query_weight: bfloat16 [768, 768], P(None, 'tensor'), may hold values from -0.21875 to 0.21875
- query_bias: float32 [768], P('tensor'), may hold values from -3 to 3
- key_weight: bfloat16 [768, 768], P(None, 'tensor'), may hold values from -0.21875 to 0.21875
- value_weight: bfloat16 [768, 384], P(None, 'tensor'), may hold values from -0.21875 to 0.21875
- value_bias: float32 [384], P('tensor'), may hold values from -3 to 3
- out_weight: bfloat16 [768, 768], P('tensor'), may hold values from -0.625 to 0.625
- out_bias: float32 [768], replicated, may hold values from -2 to 2
- up_weight: bfloat16 [768, 3072], P(None, 'tensor'), may hold values from -0.21875 to 0.21875
- up_bias: float32 [3072], P('tensor'), may hold values from -3 to 3
- down_weight: bfloat16 [3072, 768], P('tensor'), may hold values from -0.109375 to 0.109375
- down_bias: float32 [768], replicated, may hold values from -2 to 2
- first_gain: float32 [768], replicated, may hold values from 0.1 to 1.9
- first_shift: float32 [768], replicated, may hold values from -2 to 2
- second_gain: float32 [768], replicated, may hold values from 0.1 to 1.9
- second_shift: float32 [768], replicated, may hold values from -2 to 2
- cotangent: bfloat16 [32, 1024, 768], P('dp', 'tensor'), may hold values from -6 to 6
Outputs:
- block_output: float32 [32, 1024, 768], P('dp', 'tensor')
- input_grad: float32 [32, 1024, 768], P('dp', 'tensor')
- skip_grad: float32 [32, 1024, 384], P('dp', None, 'tensor')
- query_weight_grad: float32 [768, 768], P(None, 'tensor')
- query_bias_grad: float32 [768], P('tensor')
- key_weight_grad: float32 [768, 768], P(None, 'tensor')
- value_weight_grad: float32 [768, 384], P(None, 'tensor')
- value_bias_grad: float32 [384], P('tensor')
- out_weight_grad: float32 [768, 768], P('tensor')
- out_bias_grad: float32 [768], replicated
- up_weight_grad: float32 [768, 3072], P(None, 'tensor')
- up_bias_grad: float32 [3072], P('tensor')
- down_weight_grad: float32 [3072, 768], P('tensor')
- down_bias_grad: float32 [768], replicated
- first_gain_grad: float32 [768], replicated
- first_shift_grad: float32 [768], replicated
- second_gain_grad: float32 [768], replicated
- second_shift_grad: float32 [768], replicated
The draws below stay inside these ranges and needn't reach their ends.
Inputs may be any that keep to these rules, and one draw needn't show every extreme that they name: `row_fill`: row 0 is filled to 1024 in every draw; positions at or after a row's fill are padding that no other position sees.
All inputs are finite; a program needn't handle non-finite values.
Results may differ from the reference program's by a relative error of at most 0.012.
The reference program's roundings to bfloat16 on the way count: a program that leaves them out, or rounds other values in their place, can miss the bound.
Values may be sent and summed in bfloat16 or wider, within the bound.
No kernel may reach another device: no remote copies, remote signals or barrier semaphores. Data moves between devices by JAX's collectives and lax.ppermute only.
A program may use at most 256 MiB of HBM per device.

```python
import math
import jax
import jax.numpy as jnp
import numpy as np
from jax import lax

D = 768
HEADS = 12
DH = 64
FF = 3072
ROW_LEN = 1024
ROWS = 32


def draw_row_fill(key, part):
    filled = jax.random.randint(key, (ROWS,), ROW_LEN // 2, ROW_LEN + 1, dtype=jnp.int32)
    return filled.at[0].set(ROW_LEN)


def level_of(rng, shape, split, low, top_value):
    loudness = 1.0
    for axis_at, shards_of in split:
        steps = jax.random.uniform(jax.random.fold_in(jax.random.fold_in(rng, 6), axis_at), (shards_of,), jnp.float32, low / len(split), top_value / len(split))
        loudness = loudness * jnp.repeat(jnp.exp(steps), shape[axis_at] // shards_of).reshape((-1,) + (1,) * (len(shape) - 1 - axis_at))
    return loudness


def length_profile(count, total, reach, lean):
    loads = [(1 << 20) // math.isqrt(rank ** lean) + 1 for rank in range(2, count + 1)]
    spare, holding = total - reach - (count - 1), [1] * (count - 1)
    while spare > 0:
        movable = [i for i in range(count - 1) if holding[i] < reach]
        mass, left = sum([loads[i] for i in movable]), spare
        for i in movable:
            more = min(reach - holding[i], max(1, left * loads[i] // mass), spare)
            holding[i] = holding[i] + more
            spare = spare - more
    return np.array([reach] + holding)


def ragged_sizes(own_key, amount, total, bound, slope):
    if amount == 2:
        one = jax.random.randint(own_key, (), max(1, total - bound), min(bound, total - 1) + 1)
        return jnp.stack([one, total - one])
    tallies = jnp.asarray(length_profile(amount, total, bound, slope), jnp.int32)
    couples = (amount - 1) // 2
    source_of, sink = tallies[1:1 + 2 * couples:2], tallies[2:2 + 2 * couples:2]
    margin = jnp.minimum(source_of - 1, bound - sink)
    passed = jax.random.randint(jax.random.fold_in(own_key, 1), (couples,), 0, 1 << 20) % (margin + 1)
    tallies = tallies.at[1:1 + 2 * couples:2].set(source_of - passed).at[2:2 + 2 * couples:2].set(sink + passed)
    return tallies[jax.random.permutation(jax.random.fold_in(own_key, 2), amount)]


def bell_draw(key, shape, scale, bound, shards=(), kind=jnp.bfloat16):
    array = jax.random.normal(key, shape, jnp.float32) * scale
    if len(shards) > 0:
        array = level_of(key, shape, shards, -0.22, 0.18) * array
    return jnp.clip(array, min=-bound, max=bound).astype(kind)


def setup_inputs(seed: int = 0) -> dict:
    key_of = jax.random.split(jax.random.key(seed), 21)
    return {
        "block_input": bell_draw(key_of[0], (ROWS, ROW_LEN, D), 1.0, 6.0, ((0, 16), (1, 2))),
        "skip_values": bell_draw(key_of[1], (ROWS, ROW_LEN, HEADS // 2 * DH), 1.0, 6.0, ((0, 16), (2, 2))),
        "segment_ids": jax.vmap(lambda own: jnp.searchsorted(jnp.cumsum(ragged_sizes(own, 8, ROW_LEN, ROW_LEN // 4, 1)), jnp.arange(ROW_LEN), side="right"))(jax.random.split(key_of[2], ROWS)).reshape((ROWS, ROW_LEN)).astype(jnp.int32),
        "row_fill": draw_row_fill(jax.random.fold_in(key_of[20], 71), 0),
        "query_weight": bell_draw(key_of[4], (D, HEADS * DH), D ** -0.5, 0.21875, ((1, 2),)),
        "query_bias": bell_draw(key_of[5], (HEADS * DH,), 0.5, 3.0, ((0, 2),), jnp.float32),
        "key_weight": bell_draw(key_of[6], (D, HEADS * DH), D ** -0.5, 0.21875, ((1, 2),)),
        "value_weight": bell_draw(key_of[7], (D, HEADS // 2 * DH), D ** -0.5, 0.21875, ((1, 2),)),
        "value_bias": bell_draw(key_of[8], (HEADS // 2 * DH,), 0.5, 3.0, ((0, 2),), jnp.float32),
        "out_weight": bell_draw(key_of[9], (HEADS * DH, D), (HEADS * DH // 8) ** -0.5, 0.625, ((0, 2),)),
        "out_bias": bell_draw(key_of[10], (D,), 0.3, 2.0, (), jnp.float32),
        "up_weight": bell_draw(key_of[11], (D, FF), D ** -0.5, 0.21875, ((1, 2),)),
        "up_bias": bell_draw(key_of[12], (FF,), 0.5, 3.0, ((0, 2),), jnp.float32),
        "down_weight": bell_draw(key_of[13], (FF, D), FF ** -0.5, 0.109375, ((0, 2),)),
        "down_bias": bell_draw(key_of[14], (D,), 0.3, 2.0, (), jnp.float32),
        "first_gain": jnp.clip(1.0 + 0.18 * jax.random.normal(key_of[15], (D,), jnp.float32), 0.1, 1.9),
        "first_shift": bell_draw(key_of[16], (D,), 0.3, 2.0, (), jnp.float32),
        "second_gain": jnp.clip(1.0 + 0.18 * jax.random.normal(key_of[17], (D,), jnp.float32), 0.1, 1.9),
        "second_shift": bell_draw(key_of[18], (D,), 0.3, 2.0, (), jnp.float32),
        "cotangent": bell_draw(key_of[19], (ROWS, ROW_LEN, D), 1.0, 6.0, ((0, 16), (1, 2))),
    }


@jax.custom_vjp
def low(v):
    return lax.optimization_barrier(v.astype(jnp.bfloat16)).astype(jnp.float32)

@jax.custom_vjp
def low_back(v):
    return v

def low_keep(v):
    return (low(v), None)

def low_pass(kept, grad):
    return (grad,)

def back_keep(v):
    return (v, None)

def back_low(kept, grad):
    return (low(grad),)
low.defvjp(low_keep, low_pass)
low_back.defvjp(back_keep, back_low)

def layer_norm(values, gain_row, shift_row):
    center = values - lax.optimization_barrier(jnp.mean(values, axis=-1, keepdims=True))
    variance = lax.optimization_barrier(jnp.mean(center * center, axis=-1, keepdims=True))
    return center * lax.rsqrt(variance + 1e-05) * gain_row + shift_row

def rounded(values):
    return low(low_back(values))

def matmul_hi(left_side, right_side):
    return jnp.dot(left_side, right_side, precision=lax.Precision.HIGHEST)

def row_layer(weights, row_input, row_skip, row_segment, fill_value):
    query_weight, query_bias, key_weight, value_weight, value_bias, out_weight, out_bias, up_weight, up_bias, down_weight, down_bias, first_gain, first_shift, second_gain, second_shift = weights
    position = jnp.arange(ROW_LEN, dtype=jnp.int32)
    normed = low(layer_norm(row_input, first_gain, first_shift))
    queries = rounded(matmul_hi(normed, query_weight) + query_bias).reshape(ROW_LEN, HEADS, DH)
    keys_all = rounded(matmul_hi(normed, key_weight)).reshape(ROW_LEN, HEADS, DH)
    fresh_values = rounded(matmul_hi(normed, value_weight) + value_bias).reshape(ROW_LEN, HEADS // 2, DH)
    reused = row_skip.reshape(ROW_LEN, HEADS // 2, DH)
    values_all = jnp.stack([fresh_values, reused], axis=2).reshape(ROW_LEN, HEADS, DH)
    allowed = (row_segment[:, None] == row_segment[None, :]) & (position[None, :] <= position[:, None]) & ((position[None, :] < fill_value) | (position[None, :] == position[:, None]))
    scores = low_back(jnp.einsum('ihd,jhd->hij', queries, keys_all, precision=lax.Precision.HIGHEST) * DH ** (-0.5))
    scores = jnp.where(allowed[None], scores, -1000000000.0)
    probability = jax.nn.softmax(scores, axis=-1)
    head_mixed = rounded(jnp.einsum('hij,jhd->ihd', low(probability), values_all, precision=lax.Precision.HIGHEST)).reshape(ROW_LEN, HEADS * DH)
    hidden = row_input + low_back(matmul_hi(head_mixed, out_weight) + out_bias)
    normed_two = low(layer_norm(hidden, second_gain, second_shift))
    upward = low_back(matmul_hi(normed_two, up_weight) + up_bias)
    activated = low(jax.nn.gelu(upward, approximate=True))
    return hidden + low_back(matmul_hi(activated, down_weight) + down_bias)

def reference(block_input, skip_values, segment_ids, row_fill, query_weight, query_bias, key_weight, value_weight, value_bias, out_weight, out_bias, up_weight, up_bias, down_weight, down_bias, first_gain, first_shift, second_gain, second_shift, cotangent):
    weights = tuple((element.astype(jnp.float32) for element in (query_weight, query_bias, key_weight, value_weight, value_bias, out_weight, out_bias, up_weight, up_bias, down_weight, down_bias, first_gain, first_shift, second_gain, second_shift)))
    inputs = block_input.astype(jnp.float32)
    skipped = skip_values.astype(jnp.float32)

    def forward(weight_set, input_set, skip_set):

        def one_row(element):
            return row_layer(weight_set, element[0], element[1], element[2], element[3])
        return lax.map(jax.checkpoint(one_row), (input_set, skip_set, segment_ids, row_fill))
    output, pullback = jax.vjp(forward, weights, inputs, skipped)
    grad_weights, grad_input, grad_skip = pullback(cotangent.astype(jnp.float32))
    return (output, grad_input, grad_skip, grad_weights[0], grad_weights[1], grad_weights[2], grad_weights[3], grad_weights[4], grad_weights[5], grad_weights[6], grad_weights[7], grad_weights[8], grad_weights[9], grad_weights[10], grad_weights[11], grad_weights[12], grad_weights[13], grad_weights[14])
```

```python
import functools

import jax
import jax.numpy as jnp
from jax import lax
from jax.experimental import pallas as pl
from jax.experimental.pallas import tpu as pltpu
from jax.sharding import PartitionSpec as P

DH = 64
BF = jnp.bfloat16
F32 = jnp.float32
SPAN = 256
QB = 128
WIN = SPAN + QB
TH = 256
RC = 256
NEG = -1000000000.0


def layer_norm(values, gain_row, shift_row):
    center = values - jnp.mean(values, axis=-1, keepdims=True)
    variance = jnp.mean(center * center, axis=-1, keepdims=True)
    return center * lax.rsqrt(variance + 1e-05) * gain_row + shift_row


def dot_nn(a, b):
    return lax.dot_general(a, b, (((1,), (0,)), ((), ())), preferred_element_type=F32)


def dot_nt(a, b):
    return lax.dot_general(a, b, (((1,), (1,)), ((), ())), preferred_element_type=F32)


def dot_tn(a, b):
    return lax.dot_general(a, b, (((0,), (0,)), ((), ())), preferred_element_type=F32)


def split_pair(block, low_lane):
    zero = jnp.zeros_like(block)
    return jnp.concatenate(
        [jnp.where(low_lane, block, zero), jnp.where(low_lane, zero, block)], axis=0
    )


def window_bias(kseg_ref, qseg_ref, start):
    key_at = lax.broadcasted_iota(jnp.int32, (WIN, QB), 0)
    query_at = lax.broadcasted_iota(jnp.int32, (WIN, QB), 1) + SPAN
    kseg = kseg_ref[0, start : start + WIN, :]
    qseg = qseg_ref[0, :, start : start + QB]
    allowed = ((kseg == qseg) & (key_at <= query_at)) | (key_at == query_at)
    bias = jnp.where(allowed, 0.0, NEG).astype(F32)
    return jnp.concatenate([bias, bias], axis=1)


def fill_keys(k_s, v_s, ko_ref, kh_ref, fo_ref, fh_ref, so_ref, sh_ref):
    span = kh_ref.shape[0]
    length = ko_ref.shape[0]
    for pair in range(2):
        cols = slice(pair * 128, pair * 128 + 128)
        k_s[pair, :span] = kh_ref[:, cols]
        k_s[pair, span:] = ko_ref[:, cols]
        for at, size, f_ref, s_ref in ((0, span, fh_ref, sh_ref), (span, length, fo_ref, so_ref)):
            fresh = f_ref[...]
            reused = s_ref[...]
            low = lax.broadcasted_iota(jnp.int32, (size, 128), 1) < DH
            if pair == 0:
                both = jnp.where(low, fresh, pltpu.roll(reused.astype(F32), DH, 1).astype(BF))
            else:
                both = jnp.where(low, pltpu.roll(fresh.astype(F32), DH, 1).astype(BF), reused)
            v_s[pair, at : at + size] = both


def attend_forward_kernel(
    q_ref, ko_ref, kh_ref, fo_ref, fh_ref, so_ref, sh_ref, kseg_ref, qseg_ref, o_ref, lse_ref, k_s, v_s
):
    fill_keys(k_s, v_s, ko_ref, kh_ref, fo_ref, fh_ref, so_ref, sh_ref)
    low = lax.broadcasted_iota(jnp.int32, (QB, 128), 1) < DH
    turned = [v_s[pair].T for pair in range(2)]
    for start in range(0, q_ref.shape[0], QB):
        bias = window_bias(kseg_ref, qseg_ref, start)
        for pair in range(2):
            cols = slice(pair * 128, pair * 128 + 128)
            queries = split_pair(q_ref[start : start + QB, cols], low)
            scores = dot_nt(k_s[pair, start : start + WIN], queries) + bias
            largest = jnp.max(scores, axis=0, keepdims=True)
            expon = jnp.exp(scores - largest)
            total = jnp.sum(expon, axis=0, keepdims=True)
            probs = (expon * (1.0 / total)).astype(BF)
            out = dot_nn(turned[pair][:, start : start + WIN], probs)
            out = jnp.concatenate([out[:DH, :QB], out[DH:, QB:]], axis=0)
            o_ref[start : start + QB, cols] = out.T.astype(BF)
            sums = largest + jnp.log(total)
            lse_ref[0, 0, 2 * pair : 2 * pair + 1, start : start + QB] = sums[:, :QB]
            lse_ref[0, 0, 2 * pair + 1 : 2 * pair + 2, start : start + QB] = sums[:, QB:]


def attend_backward_kernel(
    q_ref,
    ko_ref,
    kh_ref,
    fo_ref,
    fh_ref,
    so_ref,
    sh_ref,
    kseg_ref,
    qseg_ref,
    lse_ref,
    g_ref,
    dq_ref,
    dko_ref,
    dkh_ref,
    dfo_ref,
    dfh_ref,
    dso_ref,
    dsh_ref,
    k_s,
    v_s,
    dk_s,
    dv_s,
):
    fill_keys(k_s, v_s, ko_ref, kh_ref, fo_ref, fh_ref, so_ref, sh_ref)
    span = kh_ref.shape[0]
    length = ko_ref.shape[0]
    low = lax.broadcasted_iota(jnp.int32, (QB, 128), 1) < DH
    turned = [k_s[pair].T for pair in range(2)]
    dk_s[...] = jnp.zeros_like(dk_s)
    dv_s[...] = jnp.zeros_like(dv_s)
    for start in range(0, length, QB):
        bias = window_bias(kseg_ref, qseg_ref, start)
        rows = slice(start, start + QB)
        win = slice(start, start + WIN)
        for pair in range(2):
            cols = slice(pair * 128, pair * 128 + 128)
            queries = split_pair(q_ref[rows, cols], low)
            grads = split_pair(g_ref[rows, cols], low)
            sums = jnp.concatenate(
                [
                    lse_ref[0, 0, 2 * pair : 2 * pair + 1, rows],
                    lse_ref[0, 0, 2 * pair + 1 : 2 * pair + 2, rows],
                ],
                axis=1,
            )
            scores = dot_nt(k_s[pair, win], queries) + bias
            probs = jnp.exp(scores - sums)
            prob_grad = dot_nt(v_s[pair, win], grads)
            row_total = jnp.sum(probs * prob_grad, axis=0, keepdims=True)
            score_grad = (probs * (prob_grad - row_total)).astype(BF)
            dv_s[pair, win] += dot_nn(probs.astype(BF), grads)
            dk_s[pair, win] += dot_nn(score_grad, queries)
            out = dot_nn(turned[pair][:, win], score_grad)
            out = jnp.concatenate([out[:DH, :QB], out[DH:, QB:]], axis=0)
            dq_ref[rows, cols] = (out.T * (DH**-0.5)).astype(BF)
    for pair in range(2):
        cols = slice(pair * 128, pair * 128 + 128)
        dkh_ref[:, cols] = dk_s[pair, :span].astype(BF)
        dko_ref[:, cols] = dk_s[pair, span:].astype(BF)
    for at, size, f_ref, s_ref in ((0, span, dfh_ref, dsh_ref), (span, length, dfo_ref, dso_ref)):
        rows = slice(at, at + size)
        low = lax.broadcasted_iota(jnp.int32, (size, 128), 1) < DH
        first, second = dv_s[0, rows], dv_s[1, rows]
        f_ref[...] = jnp.where(low, first, pltpu.roll(second, DH, 1)).astype(BF)
        s_ref[...] = jnp.where(low, pltpu.roll(first, DH, 1), second).astype(BF)


def attention_specs(rows, length, heads):
    width = heads * DH
    quads = width // 256
    q_spec = pl.BlockSpec((length, 256), lambda r, j: (r, j))
    ko_spec = pl.BlockSpec((length, 256), lambda r, j: (r, quads + j))
    kh_spec = pl.BlockSpec((SPAN, 256), lambda r, j: (r, j))
    fo_spec = pl.BlockSpec((length, 128), lambda r, j: (r, 4 * quads + j))
    fh_spec = pl.BlockSpec((SPAN, 128), lambda r, j: (r, 2 * quads + j))
    so_spec = pl.BlockSpec((length, 128), lambda r, j: (r, j))
    sh_spec = pl.BlockSpec((SPAN, 128), lambda r, j: (r, j))
    kseg_spec = pl.BlockSpec((1, SPAN + length, 1), lambda r, j: (r, 0, 0))
    qseg_spec = pl.BlockSpec((1, 1, length), lambda r, j: (r, 0, 0))
    lse_spec = pl.BlockSpec((1, 1, 4, length), lambda r, j: (r, j, 0, 0))
    ins = [q_spec, ko_spec, kh_spec, fo_spec, fh_spec, so_spec, sh_spec, kseg_spec, qseg_spec]
    return quads, ins, lse_spec


def attend_forward(qkv, kv_halo, skip_own, skip_halo, kseg, qseg, rows, length, heads):
    quads, ins, lse_spec = attention_specs(rows, length, heads)
    pairs = rows * heads * length * WIN
    return pl.pallas_call(
        attend_forward_kernel,
        grid=(rows, quads),
        in_specs=ins,
        out_specs=[pl.BlockSpec((length, 256), lambda r, j: (r, j)), lse_spec],
        out_shape=[
            jax.ShapeDtypeStruct((rows * length, heads * DH), BF),
            jax.ShapeDtypeStruct((rows, quads, 4, length), F32),
        ],
        scratch_shapes=[
            pltpu.VMEM((2, SPAN + length, 128), BF),
            pltpu.VMEM((2, SPAN + length, 128), BF),
        ],
        cost_estimate=pl.CostEstimate(
            flops=pairs * DH * 16, bytes_accessed=10 << 20, transcendentals=pairs
        ),
        name="attend_forward",
    )(qkv, qkv, kv_halo, qkv, kv_halo, skip_own, skip_halo, kseg, qseg)


def attend_backward(
    qkv, kv_halo, skip_own, skip_halo, kseg, qseg, sums, grads, rows, length, heads
):
    quads, ins, lse_spec = attention_specs(rows, length, heads)
    pairs = rows * heads * length * WIN
    own = pl.BlockSpec((length, 256), lambda r, j: (r, j))
    halo = pl.BlockSpec((SPAN, 256), lambda r, j: (r, j))
    own_half = pl.BlockSpec((length, 128), lambda r, j: (r, j))
    halo_half = pl.BlockSpec((SPAN, 128), lambda r, j: (r, j))
    width = heads * DH

    def shape(count, columns):
        return jax.ShapeDtypeStruct((rows * count, columns), BF)

    return pl.pallas_call(
        attend_backward_kernel,
        grid=(rows, quads),
        in_specs=ins + [lse_spec, own],
        out_specs=[own, own, halo, own_half, halo_half, own_half, halo_half],
        out_shape=[
            shape(length, width),
            shape(length, width),
            shape(SPAN, width),
            shape(length, width // 2),
            shape(SPAN, width // 2),
            shape(length, width // 2),
            shape(SPAN, width // 2),
        ],
        scratch_shapes=[
            pltpu.VMEM((2, SPAN + length, 128), BF),
            pltpu.VMEM((2, SPAN + length, 128), BF),
            pltpu.VMEM((2, SPAN + length, 128), F32),
            pltpu.VMEM((2, SPAN + length, 128), F32),
        ],
        cost_estimate=pl.CostEstimate(
            flops=pairs * DH * 40, bytes_accessed=18 << 20, transcendentals=pairs
        ),
        name="attend_backward",
    )(qkv, qkv, kv_halo, qkv, kv_halo, skip_own, skip_halo, kseg, qseg, sums, grads)


def feed_kernel(
    core_ref,
    n_ref,
    g_ref,
    ua_ref,
    ub_ref,
    ba_ref,
    bb_ref,
    da_ref,
    db_ref,
    wua_ref,
    wub_ref,
    wda_ref,
    wdb_ref,
    ga_ref,
    gb_ref,
    down_ref,
    second_ref,
    turned_s,
    act_s,
    upg_s,
):
    step = pl.program_id(0)
    half = pl.num_programs(0) // 2
    first = step < half

    @pl.when(step == 0)
    def _():
        turned_s[...] = n_ref[...].T
        down_ref[...] = jnp.zeros_like(down_ref)
        second_ref[...] = jnp.zeros_like(second_ref)

    up_tile = jnp.where(first, ua_ref[...], ub_ref[...])
    down_tile = jnp.where(first, da_ref[...], db_ref[...])
    bias = jnp.where(first, ba_ref[...], bb_ref[...])
    root = 0.7978845608028654
    for start in range(0, n_ref.shape[0], RC):
        rows = slice(start, start + RC)
        upward = dot_nn(n_ref[rows, :], up_tile) + bias
        act_grad = dot_nt(g_ref[rows, :], down_tile)
        square = upward * upward
        bent = jnp.tanh(root * upward * (1.0 + 0.044715 * square))
        gate = 0.5 * (1.0 + bent)
        slope = gate + 0.5 * root * upward * (1.0 - bent * bent) * (1.0 + 0.134145 * square)
        act = (upward * gate).astype(BF)
        upg = (act_grad * slope).astype(BF)
        act_s[rows, :] = act
        upg_s[rows, :] = upg
        down_ref[rows, :] += dot_nn(act, down_tile)
        second_ref[rows, :] += dot_nt(upg, up_tile)
    up_weight_grad = dot_nn(turned_s[...], upg_s[...]).astype(BF)
    down_weight_grad = dot_tn(act_s[...], g_ref[...]).astype(BF)
    bias_grad = jnp.sum(upg_s[...].astype(F32), axis=0, keepdims=True)

    @pl.when(first)
    def _():
        wua_ref[...] = up_weight_grad
        wda_ref[...] = down_weight_grad
        ga_ref[...] = bias_grad

    @pl.when(jnp.logical_not(first))
    def _():
        wub_ref[...] = up_weight_grad
        wdb_ref[...] = down_weight_grad
        gb_ref[...] = bias_grad


def feed(core, normed, grads, up_a, up_b, bias_a, bias_b, down_a, down_b, whole):
    tokens, width = normed.shape
    piece = up_a.shape[1] // 2 if whole else up_a.shape[1]
    tiles = piece // TH

    def a_at(i, c):
        at = jnp.minimum(i, tiles - 1)
        return at + (1 - c[0]) * tiles if whole else at

    def b_at(i, c):
        at = jnp.maximum(i - tiles, 0)
        return at + c[0] * tiles if whole else at

    def out_a(i, c):
        return jnp.minimum(i, tiles - 1)

    def out_b(i, c):
        return jnp.maximum(i - tiles, 0)

    resident = pl.BlockSpec((tokens, width), lambda i, c: (0, 0))
    once = pl.BlockSpec((tokens, width), lambda i, c: (0, 0))
    in_specs = [
        resident,
        resident,
        pl.BlockSpec((width, TH), lambda i, c: (0, a_at(i, c))),
        pl.BlockSpec((width, TH), lambda i, c: (0, b_at(i, c))),
        pl.BlockSpec((1, TH), lambda i, c: (0, a_at(i, c))),
        pl.BlockSpec((1, TH), lambda i, c: (0, b_at(i, c))),
        pl.BlockSpec((TH, width), lambda i, c: (a_at(i, c), 0)),
        pl.BlockSpec((TH, width), lambda i, c: (b_at(i, c), 0)),
    ]
    out_specs = [
        pl.BlockSpec((width, TH), lambda i, c: (0, out_a(i, c))),
        pl.BlockSpec((width, TH), lambda i, c: (0, out_b(i, c))),
        pl.BlockSpec((TH, width), lambda i, c: (out_a(i, c), 0)),
        pl.BlockSpec((TH, width), lambda i, c: (out_b(i, c), 0)),
        pl.BlockSpec((1, TH), lambda i, c: (0, out_a(i, c))),
        pl.BlockSpec((1, TH), lambda i, c: (0, out_b(i, c))),
        once,
        once,
    ]
    out_shape = [
        jax.ShapeDtypeStruct((width, piece), BF),
        jax.ShapeDtypeStruct((width, piece), BF),
        jax.ShapeDtypeStruct((piece, width), BF),
        jax.ShapeDtypeStruct((piece, width), BF),
        jax.ShapeDtypeStruct((1, piece), F32),
        jax.ShapeDtypeStruct((1, piece), F32),
        jax.ShapeDtypeStruct((tokens, width), F32),
        jax.ShapeDtypeStruct((tokens, width), F32),
    ]
    return pl.pallas_call(
        feed_kernel,
        grid_spec=pltpu.PrefetchScalarGridSpec(
            num_scalar_prefetch=1,
            grid=(2 * tiles,),
            in_specs=in_specs,
            out_specs=out_specs,
            scratch_shapes=[
                pltpu.VMEM((width, tokens), BF),
                pltpu.VMEM((tokens, TH), BF),
                pltpu.VMEM((tokens, TH), BF),
            ],
        ),
        out_shape=out_shape,
        compiler_params=pltpu.CompilerParams(vmem_limit_bytes=56 << 20),
        cost_estimate=pl.CostEstimate(
            flops=24 * tokens * width * piece,
            bytes_accessed=20 << 20,
            transcendentals=2 * tokens * piece,
        ),
        name="feed",
    )(core, normed, grads, up_a, up_b, bias_a, bias_b, down_a, down_b)


def swap_perm(count):
    return [(i, i ^ 1) for i in range(count)]


class Ring:
    def __init__(self, count):
        self.count = count
        chips = count // 2
        self.factors = []
        if (chips.bit_length() - 1) % 2:
            self.factors.append(2)
            chips //= 2
        while chips > 1:
            self.factors.append(4)
            chips //= 4
        self.index = lax.axis_index("dp")
        self.core = self.index % 2

    def swap_core(self, value):
        return lax.ppermute(value, "dp", swap_perm(self.count))

    def shift(self, value, stride, factor, by):
        perm = []
        for i in range(self.count):
            digit = (i // stride) % factor
            perm.append((i, i + (((digit + by) % factor) - digit) * stride))
        return lax.ppermute(value, "dp", perm)

    def stages(self):
        stride = 2
        for factor in self.factors:
            yield stride, factor, (self.index // stride) % factor
            stride *= factor

    def sum_chips(self, value):
        stages = list(self.stages())
        for stride, factor, digit in stages:
            rows = value.shape[0] // factor
            total = lax.dynamic_slice_in_dim(value, digit * rows, rows, 0).astype(F32)
            for by in range(1, factor):
                part = lax.dynamic_slice_in_dim(value, ((digit + by) % factor) * rows, rows, 0)
                total = total + self.shift(part, stride, factor, by).astype(F32)
            value = total.astype(BF)
        for stride, factor, digit in reversed(stages):
            parts = [value] + [self.shift(value, stride, factor, by) for by in range(1, factor)]
            value = jnp.concatenate(
                [lax.select_n((digit - at) % factor, *parts)
                 if factor > 2 else jnp.where(digit == at, parts[0], parts[1])
                 for at in range(factor)],
                axis=0,
            )
        return value

    def sum_small(self, value):
        value = value + self.swap_core(value)
        for stride, factor, digit in self.stages():
            total = value
            for by in range(1, factor):
                total = total + self.shift(value, stride, factor, by)
            value = total
        return value


def swap_tensor(value):
    return lax.ppermute(value, "tensor", [(0, 1), (1, 0)])


def own_half(value, at, axis):
    size = value.shape[axis] // 2
    return lax.dynamic_slice_in_dim(value, at * size, size, axis)


def in_order(core, mine, other, axis):
    return jnp.concatenate(
        [jnp.where(core == 0, mine, other), jnp.where(core == 0, other, mine)], axis=axis
    )


def on_device(
    dp_count,
    block_input,
    skip_values,
    segment_ids,
    row_fill,
    query_weight,
    query_bias,
    key_weight,
    value_weight,
    value_bias,
    out_weight,
    out_bias,
    up_weight,
    up_bias,
    down_weight,
    down_bias,
    first_gain,
    first_shift,
    second_gain,
    second_shift,
    cotangent,
):
    ring = Ring(dp_count)
    core = ring.core
    side = lax.axis_index("tensor")
    rows, length, width = block_input.shape
    tokens = rows * length
    local = query_weight.shape[1]
    local_half = local // 2
    heads = 2 * local // DH
    hidden_local = up_weight.shape[1]

    share_input = block_input.astype(F32)
    normed = layer_norm(share_input, first_gain, first_shift).astype(BF)
    normed_halo = lax.ppermute(normed[:, length - SPAN :], "tensor", [(0, 1)])
    normed = normed.reshape(tokens, width)
    normed_halo = normed_halo.reshape(rows * SPAN, width)

    def fetch(weight, axis):
        mine = swap_tensor(own_half(weight, core, axis))
        return mine, ring.swap_core(mine)

    qkv_own = jnp.concatenate([query_weight, key_weight, value_weight], axis=1)
    qkv_other = in_order(core, *fetch(qkv_own, 0), 0)
    cuts = (0, local, 2 * local, 2 * local + local_half)
    qkv_weight = jnp.concatenate(
        [
            piece[:, cuts[n] : cuts[n + 1]]
            for n in range(3)
            for piece in (qkv_own, qkv_other)
        ],
        axis=1,
    )
    small_other = swap_tensor(jnp.concatenate([query_bias, value_bias, up_bias]))
    query_bias_all = jnp.concatenate([query_bias, small_other[:local]])
    value_bias_all = jnp.concatenate([value_bias, small_other[local : local + local_half]])
    up_bias_other = small_other[local + local_half :]

    skip_mid = skip_values[:, length - SPAN : length]
    skip_send = jnp.concatenate(
        [skip_mid, lax.dynamic_slice_in_dim(skip_values, (1 - side) * length, length, 1)], axis=1
    )
    skip_got = swap_tensor(skip_send)
    skip_own = jnp.concatenate(
        [lax.dynamic_slice_in_dim(skip_values, side * length, length, 1), skip_got[:, SPAN:]],
        axis=2,
    ).reshape(tokens, local)
    skip_halo = jnp.concatenate([skip_mid, skip_got[:, :SPAN]], axis=2).reshape(rows * SPAN, local)

    position = jnp.arange(segment_ids.shape[1], dtype=jnp.int32)
    usable = jnp.where(position[None] < row_fill[:, None], segment_ids, -1)
    query_seg = lax.dynamic_slice_in_dim(segment_ids, side * length, length, 1)
    key_seg = jnp.concatenate(
        [
            jnp.where(side == 0, -1, usable[:, length - SPAN : length]),
            lax.dynamic_slice_in_dim(usable, side * length, length, 1),
        ],
        axis=1,
    )
    query_seg = query_seg.reshape(rows, 1, length)
    key_seg = key_seg.reshape(rows, SPAN + length, 1)

    scale = jnp.concatenate([jnp.full((2 * local,), DH**-0.5, F32), jnp.ones((3 * local,), F32)])
    qkv_bias = jnp.concatenate([query_bias_all, jnp.zeros((2 * local,), F32), value_bias_all])
    qkv = ((dot_nn(normed, qkv_weight) + qkv_bias) * scale).astype(BF)
    kv_halo = (dot_nn(normed_halo, qkv_weight[:, 2 * local :]) + qkv_bias[2 * local :]).astype(BF)
    mixed, sums = attend_forward(
        qkv, kv_halo, skip_own, skip_halo, key_seg, query_seg, rows, length, heads
    )
    out_other = in_order(core, *fetch(out_weight, 0), 0)
    out_all = jnp.concatenate([out_weight, out_other], axis=0)
    hidden = share_input.reshape(tokens, width) + (dot_nn(mixed, out_all) + out_bias)
    normed_two = layer_norm(hidden, second_gain, second_shift).astype(BF)

    out_grad = cotangent.reshape(tokens, width)
    core_at = core.reshape(1).astype(jnp.int32)
    up_mine, up_theirs = fetch(up_weight, 1)
    down_mine, down_theirs = fetch(down_weight, 0)
    bias_row = up_bias.reshape(1, hidden_local)
    (up_l2, up_l1, down_l2, down_l1, bias_l2, bias_l1, down_sum_l, second_sum_l) = feed(
        core_at, normed_two, out_grad, up_weight, up_weight, bias_row, bias_row,
        down_weight, down_weight, True,
    )
    (up_r2, up_r1, down_r2, down_r1, bias_r2, bias_r1, down_sum_r, second_sum_r) = feed(
        core_at, normed_two, out_grad, up_theirs, up_mine,
        own_half(up_bias_other, 1 - core, 0).reshape(1, -1),
        own_half(up_bias_other, core, 0).reshape(1, -1),
        down_theirs, down_mine, False,
    )
    block_output = hidden + (down_sum_l + down_sum_r + down_bias)
    cot = out_grad.astype(F32)
    down_bias_grad = jnp.sum(cot, axis=0)
    second_grad = second_sum_l + second_sum_r
    _, second_pull = jax.vjp(layer_norm, hidden, second_gain, second_shift)
    hidden_part, second_gain_grad, second_shift_grad = second_pull(second_grad)
    hidden_grad = cot + hidden_part
    hidden_low = hidden_grad.astype(BF)
    out_bias_grad = jnp.sum(hidden_low.astype(F32), axis=0)

    def sum_pieces(l1, l2, r1, r2):
        r1 = (r1.astype(F32) + ring.swap_core(r2).astype(F32)).astype(BF)
        l1 = l1.astype(F32) + ring.swap_core(l2).astype(F32)
        mine = ring.sum_chips((l1 + swap_tensor(r1).astype(F32)).astype(BF))
        return mine.astype(F32), ring.swap_core(mine).astype(F32)

    up_weight_grad = in_order(core, *sum_pieces(up_l1, up_l2, up_r1, up_r2), 1)
    down_weight_grad = in_order(core, *sum_pieces(down_l1, down_l2, down_r1, down_r2), 0)

    mixed_grad = dot_nt(hidden_low, out_all).astype(BF)
    out_grad_all = dot_tn(mixed, hidden_low).astype(BF)

    def cut(value, axis):
        return own_half(value, core, axis), own_half(value, 1 - core, axis)

    out_weight_grad = in_order(
        core, *sum_pieces(*cut(out_grad_all[:local], 1), *cut(out_grad_all[local:], 1)), 1
    )

    (query_g, key_g, key_g_halo, fresh_g, fresh_g_halo, skip_g, skip_g_halo) = attend_backward(
        qkv, kv_halo, skip_own, skip_halo, key_seg, query_seg, sums, mixed_grad, rows, length, heads
    )
    first_halo = dot_nt(key_g_halo, qkv_weight[:, 2 * local : 4 * local]) + dot_nt(
        fresh_g_halo, qkv_weight[:, 4 * local :]
    )
    first_got = lax.ppermute(first_halo.astype(BF), "tensor", [(1, 0)])
    first_grad = (
        dot_nt(query_g, qkv_weight[:, : 2 * local])
        + dot_nt(key_g, qkv_weight[:, 2 * local : 4 * local])
        + dot_nt(fresh_g, qkv_weight[:, 4 * local :])
    )
    first_grad = first_grad.reshape(rows, length, width) + jnp.pad(
        first_got.astype(F32).reshape(rows, SPAN, width), ((0, 0), (length - SPAN, 0), (0, 0))
    )
    _, first_pull = jax.vjp(layer_norm, share_input, first_gain, first_shift)
    input_part, first_gain_grad, first_shift_grad = first_pull(first_grad)
    input_grad = hidden_grad.reshape(rows, length, width) + input_part

    query_w = dot_tn(normed, query_g)
    key_w = dot_tn(normed, key_g) + dot_tn(normed_halo, key_g_halo)
    fresh_w = dot_tn(normed, fresh_g) + dot_tn(normed_halo, fresh_g_halo)
    own_w = jnp.concatenate([query_w[:, :local], key_w[:, :local], fresh_w[:, :local_half]], axis=1)
    other_w = jnp.concatenate([query_w[:, local:], key_w[:, local:], fresh_w[:, local_half:]], axis=1)
    qkv_grad = in_order(
        core, *sum_pieces(*cut(own_w.astype(BF), 0), *cut(other_w.astype(BF), 0)), 0
    )

    skip_g = skip_g.reshape(rows, length, local)
    skip_g_halo = skip_g_halo.reshape(rows, SPAN, local)
    got = swap_tensor(
        jnp.concatenate([skip_g_halo[:, :, local_half:], skip_g[:, :, local_half:]], axis=1)
    ).astype(F32)
    mine = skip_g[:, :, :local_half].astype(F32)
    extra = skip_g_halo[:, :, :local_half].astype(F32) + got[:, :SPAN]
    low = jnp.where(side == 0, mine, got[:, SPAN:])
    high = jnp.where(side == 0, got[:, SPAN:], mine)
    low = jnp.concatenate([low[:, : length - SPAN], low[:, length - SPAN :] + extra], axis=1)
    skip_grad = jnp.concatenate([low, high], axis=1)

    query_b = jnp.sum(query_g.astype(F32), axis=0)
    fresh_b = jnp.sum(fresh_g.astype(F32), axis=0) + jnp.sum(fresh_g_halo.astype(F32), axis=0)
    up_b_own = in_order(core, bias_l1[0], bias_l2[0], 0)
    up_b_other = in_order(core, bias_r1[0], bias_r2[0], 0)
    common = jnp.concatenate(
        [
            out_bias_grad,
            down_bias_grad,
            first_gain_grad,
            first_shift_grad,
            second_gain_grad,
            second_shift_grad,
        ]
    )
    own_small = jnp.concatenate([common, query_b[:local], fresh_b[:local_half], up_b_own])
    other_small = jnp.concatenate([common, query_b[local:], fresh_b[local_half:], up_b_other])
    small = ring.sum_small(own_small + swap_tensor(other_small))
    common = [small[n * width : (n + 1) * width] for n in range(6)]
    at = 6 * width

    return (
        block_output.reshape(rows, length, width),
        input_grad,
        skip_grad,
        qkv_grad[:, :local],
        small[at : at + local],
        qkv_grad[:, local : 2 * local],
        qkv_grad[:, 2 * local :],
        small[at + local : at + local + local_half],
        out_weight_grad,
        common[0],
        up_weight_grad,
        small[at + local + local_half :],
        down_weight_grad,
        common[1],
        common[2],
        common[3],
        common[4],
        common[5],
    )


def solution(mesh):
    in_specs = (
        P("dp", "tensor", None),
        P("dp", None, "tensor"),
        P("dp", None),
        P("dp"),
        P(None, "tensor"),
        P("tensor"),
        P(None, "tensor"),
        P(None, "tensor"),
        P("tensor"),
        P("tensor", None),
        P(),
        P(None, "tensor"),
        P("tensor"),
        P("tensor", None),
        P(),
        P(),
        P(),
        P(),
        P(),
        P("dp", "tensor", None),
    )
    out_specs = (
        P("dp", "tensor", None),
        P("dp", "tensor", None),
        P("dp", None, "tensor"),
        P(None, "tensor"),
        P("tensor"),
        P(None, "tensor"),
        P(None, "tensor"),
        P("tensor"),
        P("tensor", None),
        P(),
        P(None, "tensor"),
        P("tensor"),
        P("tensor", None),
        P(),
        P(),
        P(),
        P(),
        P(),
    )
    return jax.shard_map(
        functools.partial(on_device, mesh.shape["dp"]),
        mesh=mesh,
        in_specs=in_specs,
        out_specs=out_specs,
        check_vma=False,
    )
```

```python
import functools
import itertools

import jax
import jax.numpy as jnp
from jax import lax
from jax.experimental import pallas as pl
from jax.experimental.pallas import tpu as pltpu
from jax.sharding import PartitionSpec as P

DH = 64
BF = jnp.bfloat16
F32 = jnp.float32
SPAN = 256
QB = 128
WIN = SPAN + QB
TH = 256
RC = 256
NEG = -1000000000.0
COST = pl.CostEstimate(flops=1 << 20, bytes_accessed=1 << 20, transcendentals=0)


def dot_nn(a, b):
    return lax.dot_general(a, b, (((1,), (0,)), ((), ())), preferred_element_type=F32)


def dot_nt(a, b):
    return lax.dot_general(a, b, (((1,), (1,)), ((), ())), preferred_element_type=F32)


def dot_tn(a, b):
    return lax.dot_general(a, b, (((0,), (0,)), ((), ())), preferred_element_type=F32)


def split_pair(block, low_lane):
    zero = jnp.zeros_like(block)
    return jnp.concatenate(
        [jnp.where(low_lane, block, zero), jnp.where(low_lane, zero, block)], axis=0
    )


def window_bias(kseg_ref, qseg_ref, start):
    key_at = lax.broadcasted_iota(jnp.int32, (WIN, QB), 0)
    query_at = lax.broadcasted_iota(jnp.int32, (WIN, QB), 1) + SPAN
    kseg = kseg_ref[0, start : start + WIN, :]
    qseg = qseg_ref[0, :, start : start + QB]
    allowed = ((kseg == qseg) & (key_at <= query_at)) | (key_at == query_at)
    bias = jnp.where(allowed, 0.0, NEG).astype(F32)
    return jnp.concatenate([bias, bias], axis=1)


def pair_values(x_ref, s_ref, t_s, pairs):
    base = 4 * pairs * DH
    for at in range(0, pairs, 2):
        fresh = x_ref[:, base + at * DH : base + at * DH + 128].T
        for pair in range(at, min(at + 2, pairs)):
            t_s[pair, :DH, :] = fresh[(pair - at) * DH : (pair - at + 1) * DH, :]
            t_s[pair, DH:, :] = s_ref[pair * DH : (pair + 1) * DH, :]


def attend_forward_kernel(pairs, x_ref, s_ref, kseg_ref, qseg_ref, o_ref, lse_ref, t_s):
    o_blocks = o_ref.shape[0] // QB
    pair_values(x_ref, s_ref, t_s, pairs)

    low = lax.broadcasted_iota(jnp.int32, (QB, 128), 1) < DH
    for block, pair in itertools.product(range(o_blocks), range(pairs)):
        start = block * QB
        if pair == 0:
            bias = window_bias(kseg_ref, qseg_ref, start)
        win = slice(start, start + WIN)
        rows = slice(start + SPAN, start + SPAN + QB)
        here = slice(start, start + QB)
        cols = slice(pair * 128, pair * 128 + 128)
        key_cols = slice((pairs + pair) * 128, (pairs + pair) * 128 + 128)
        queries = split_pair(x_ref[rows, cols], low)
        scores = dot_nt(x_ref[win, key_cols], queries) + bias
        largest = jnp.max(scores, axis=0, keepdims=True)
        expon = jnp.exp(scores - largest)
        total = jnp.sum(expon, axis=0, keepdims=True)
        probs = (expon * (1.0 / total)).astype(BF)
        out = dot_nn(t_s[pair, :, win], probs)
        out = jnp.concatenate([out[:DH, :QB], out[DH:, QB:]], axis=0)
        o_ref[here, cols] = out.T.astype(BF)
        lse_ref[0, block, pair : pair + 1, :] = largest + jnp.log(total)


def attend_backward_kernel(
    pairs, x_ref, s_ref, kseg_ref, qseg_ref, lse_ref, g_ref, dx_ref, ds_ref, v_s, t_s, dk_s, dv_s
):
    o_blocks = g_ref.shape[0] // QB
    pair_values(x_ref, s_ref, t_s, pairs)
    for pair in range(pairs):
        v_s[pair] = t_s[pair].T
        key_cols = slice((pairs + pair) * 128, (pairs + pair) * 128 + 128)
        t_s[pair] = x_ref[:, key_cols].T
    dk_s[...] = jnp.zeros_like(dk_s)
    dv_s[...] = jnp.zeros_like(dv_s)
    dx_ref[:SPAN, : pairs * 128] = jnp.zeros((SPAN, pairs * 128), BF)

    low = lax.broadcasted_iota(jnp.int32, (QB, 128), 1) < DH
    for block, pair in itertools.product(range(o_blocks), range(pairs)):
        start = block * QB
        if pair == 0:
            bias = window_bias(kseg_ref, qseg_ref, start)
        win = slice(start, start + WIN)
        rows = slice(start + SPAN, start + SPAN + QB)
        here = slice(start, start + QB)
        cols = slice(pair * 128, pair * 128 + 128)
        key_cols = slice((pairs + pair) * 128, (pairs + pair) * 128 + 128)
        queries = split_pair(x_ref[rows, cols], low)
        grads = split_pair(g_ref[here, cols], low)
        scores = dot_nt(x_ref[win, key_cols], queries) + bias
        probs = jnp.exp(scores - lse_ref[0, block, pair : pair + 1, :])
        prob_grad = dot_nt(v_s[pair, win], grads)
        row_total = jnp.sum(probs * prob_grad, axis=0, keepdims=True)
        score_grad = (probs * (prob_grad - row_total)).astype(BF)
        dv_s[pair, win] += dot_nn(probs.astype(BF), grads)
        dk_s[pair, win] += dot_nn(score_grad, queries)
        out = dot_nn(t_s[pair, :, win], score_grad)
        out = jnp.concatenate([out[:DH, :QB], out[DH:, QB:]], axis=0)
        dx_ref[rows, cols] = (out.T * (DH**-0.5)).astype(BF)

    base = 4 * pairs * DH
    low_all = lax.broadcasted_iota(jnp.int32, (x_ref.shape[0], 128), 1) < DH
    for pair in range(pairs):
        key_cols = slice((pairs + pair) * 128, (pairs + pair) * 128 + 128)
        dx_ref[:, key_cols] = dk_s[pair].astype(BF)
        ds_ref[pair * DH : (pair + 1) * DH, :] = dv_s[pair].astype(BF).T[DH:, :]
    for at in range(0, pairs, 2):
        second = pltpu.roll(dv_s[at + 1], DH, 1) if at + 1 < pairs else jnp.zeros_like(dv_s[at])
        dx_ref[:, base + at * DH : base + at * DH + 128] = jnp.where(
            low_all, dv_s[at], second
        ).astype(BF)


def attention_specs(rows, blocks, columns, pairs):
    extended = SPAN + blocks * QB
    x_spec = pl.BlockSpec((extended, columns), lambda r: (r, 0))
    s_spec = pl.BlockSpec((pairs * DH, extended), lambda r: (r, 0))
    kseg_spec = pl.BlockSpec((1, extended, 1), lambda r: (r, 0, 0))
    qseg_spec = pl.BlockSpec((1, 1, blocks * QB), lambda r: (r, 0, 0))
    o_spec = pl.BlockSpec((blocks * QB, pairs * 128), lambda r: (r, 0))
    lse_spec = pl.BlockSpec((1, blocks, pairs, 2 * QB), lambda r: (r, 0, 0, 0))
    return extended, x_spec, s_spec, kseg_spec, qseg_spec, o_spec, lse_spec


def attend_forward(extended_qkv, skip, kseg, qseg):
    rows, blocks, pairs = qseg.shape[0], qseg.shape[2] // QB, skip.shape[0] // DH // qseg.shape[0]
    columns = extended_qkv.shape[1]
    extended, x_spec, s_spec, kseg_spec, qseg_spec, o_spec, lse_spec = attention_specs(
        rows, blocks, columns, pairs
    )
    return pl.pallas_call(
        functools.partial(attend_forward_kernel, pairs),
        grid=(rows,),
        in_specs=[x_spec, s_spec, kseg_spec, qseg_spec],
        out_specs=[o_spec, lse_spec],
        out_shape=[
            jax.ShapeDtypeStruct((rows * blocks * QB, pairs * 128), BF),
            jax.ShapeDtypeStruct((rows, blocks, pairs, 2 * QB), F32),
        ],
        scratch_shapes=[
            pltpu.VMEM((pairs, 128, extended), BF),
        ],
        cost_estimate=COST,
        name="attend_forward",
    )(extended_qkv, skip, kseg, qseg)


def attend_backward(extended_qkv, skip, kseg, qseg, sums, grads):
    rows, blocks, pairs = qseg.shape[0], qseg.shape[2] // QB, skip.shape[0] // DH // qseg.shape[0]
    columns = extended_qkv.shape[1]
    extended, x_spec, s_spec, kseg_spec, qseg_spec, o_spec, lse_spec = attention_specs(
        rows, blocks, columns, pairs
    )
    return pl.pallas_call(
        functools.partial(attend_backward_kernel, pairs),
        grid=(rows,),
        in_specs=[x_spec, s_spec, kseg_spec, qseg_spec, lse_spec, o_spec],
        out_specs=[x_spec, s_spec],
        out_shape=[
            jax.ShapeDtypeStruct((rows * extended, columns), BF),
            jax.ShapeDtypeStruct((rows * pairs * DH, extended), BF),
        ],
        scratch_shapes=[
            pltpu.VMEM((pairs, extended, 128), BF),
            pltpu.VMEM((pairs, 128, extended), BF),
            pltpu.VMEM((pairs, extended, 128), F32),
            pltpu.VMEM((pairs, extended, 128), F32),
        ],
        cost_estimate=COST,
        name="attend_backward",
    )(extended_qkv, skip, kseg, qseg, sums, grads)


def feed_kernel(
    core_ref,
    n_ref,
    g_ref,
    ua_ref,
    ub_ref,
    ba_ref,
    bb_ref,
    da_ref,
    db_ref,
    wua_ref,
    wub_ref,
    wda_ref,
    wdb_ref,
    ga_ref,
    gb_ref,
    down_ref,
    second_ref,
    turned_s,
    act_s,
    upg_s,
):
    step = pl.program_id(0)
    half = pl.num_programs(0) // 2
    first = step < half

    @pl.when(step == 0)
    def _():
        turned_s[...] = n_ref[...].T
        down_ref[...] = jnp.zeros_like(down_ref)
        second_ref[...] = jnp.zeros_like(second_ref)

    up_tile = jnp.where(first, ua_ref[...], ub_ref[...])
    down_tile = jnp.where(first, da_ref[...], db_ref[...])
    bias = jnp.where(first, ba_ref[...], bb_ref[...])
    root = 0.7978845608028654
    for start in range(0, n_ref.shape[0], RC):
        rows = slice(start, start + RC)
        upward = dot_nn(n_ref[rows, :], up_tile) + bias
        act_grad = dot_nt(g_ref[rows, :], down_tile)
        square = upward * upward
        bent = jnp.tanh(root * upward * (1.0 + 0.044715 * square))
        gate = 0.5 * (1.0 + bent)
        slope = gate + 0.5 * root * upward * (1.0 - bent * bent) * (1.0 + 0.134145 * square)
        act = (upward * gate).astype(BF)
        upg = (act_grad * slope).astype(BF)
        act_s[rows, :] = act
        upg_s[rows, :] = upg
        down_ref[rows, :] += dot_nn(act, down_tile)
        second_ref[rows, :] += dot_nt(upg, up_tile)
    up_weight_grad = dot_nn(turned_s[...], upg_s[...]).astype(BF)
    down_weight_grad = dot_tn(act_s[...], g_ref[...]).astype(BF)
    bias_grad = jnp.sum(upg_s[...].astype(F32), axis=0, keepdims=True)

    @pl.when(first)
    def _():
        wua_ref[...] = up_weight_grad
        wda_ref[...] = down_weight_grad
        ga_ref[...] = bias_grad

    @pl.when(jnp.logical_not(first))
    def _():
        wub_ref[...] = up_weight_grad
        wdb_ref[...] = down_weight_grad
        gb_ref[...] = bias_grad


def feed(at, normed, grads, up_a, up_b, bias, down_a, down_b, whole):
    tokens, width = normed.shape
    piece = up_a.shape[1] // 2 if whole else up_a.shape[1]
    tiles = piece // TH

    def a_at(i, c):
        at = jnp.minimum(i, tiles - 1)
        return at + (1 - c[0]) * tiles if whole else at

    def b_at(i, c):
        at = jnp.maximum(i - tiles, 0)
        return at + c[0] * tiles if whole else at

    def out_a(i, c):
        return jnp.minimum(i, tiles - 1)

    def out_b(i, c):
        return jnp.maximum(i - tiles, 0)

    resident = pl.BlockSpec((tokens, width), lambda i, c: (0, 0))
    once = pl.BlockSpec((tokens, width), lambda i, c: (0, 0))
    in_specs = [
        resident,
        resident,
        pl.BlockSpec((width, TH), lambda i, c: (0, a_at(i, c))),
        pl.BlockSpec((width, TH), lambda i, c: (0, b_at(i, c))),
        pl.BlockSpec((1, TH), lambda i, c: (0, out_a(i, c) + (1 - c[0]) * tiles)),
        pl.BlockSpec((1, TH), lambda i, c: (0, out_b(i, c) + c[0] * tiles)),
        pl.BlockSpec((TH, width), lambda i, c: (a_at(i, c), 0)),
        pl.BlockSpec((TH, width), lambda i, c: (b_at(i, c), 0)),
    ]
    out_specs = [
        pl.BlockSpec((width, TH), lambda i, c: (0, out_a(i, c))),
        pl.BlockSpec((width, TH), lambda i, c: (0, out_b(i, c))),
        pl.BlockSpec((TH, width), lambda i, c: (out_a(i, c), 0)),
        pl.BlockSpec((TH, width), lambda i, c: (out_b(i, c), 0)),
        pl.BlockSpec((1, TH), lambda i, c: (0, out_a(i, c))),
        pl.BlockSpec((1, TH), lambda i, c: (0, out_b(i, c))),
        once,
        once,
    ]
    out_shape = [
        jax.ShapeDtypeStruct((width, piece), BF),
        jax.ShapeDtypeStruct((width, piece), BF),
        jax.ShapeDtypeStruct((piece, width), BF),
        jax.ShapeDtypeStruct((piece, width), BF),
        jax.ShapeDtypeStruct((1, piece), F32),
        jax.ShapeDtypeStruct((1, piece), F32),
        jax.ShapeDtypeStruct((tokens, width), F32),
        jax.ShapeDtypeStruct((tokens, width), F32),
    ]
    return pl.pallas_call(
        feed_kernel,
        grid_spec=pltpu.PrefetchScalarGridSpec(
            num_scalar_prefetch=1,
            grid=(2 * tiles,),
            in_specs=in_specs,
            out_specs=out_specs,
            scratch_shapes=[
                pltpu.VMEM((width, tokens), BF),
                pltpu.VMEM((tokens, TH), BF),
                pltpu.VMEM((tokens, TH), BF),
            ],
        ),
        out_shape=out_shape,
        compiler_params=pltpu.CompilerParams(vmem_limit_bytes=56 << 20),
        cost_estimate=COST,
        name="feed",
    )(at, normed, grads, up_a, up_b, bias, bias, down_a, down_b)


def norm_rows(values, gain_row, shift_row):
    center = values - jnp.mean(values, axis=-1, keepdims=True)
    variance = jnp.mean(center * center, axis=-1, keepdims=True)
    return center * lax.rsqrt(variance + 1e-05) * gain_row + shift_row


def whole_spec(value):
    zeros = (0,) * value.ndim
    return pl.BlockSpec(value.shape, lambda *_: zeros)


def open_kernel(
    at_ref, qw_ref, kw_ref, vw_ref, x_ref, s_ref, w_ref, w_send_ref, halo_ref, s_send_ref, s_own_ref
):
    side = at_ref[1]
    rows, length, width = x_ref.shape
    local, half = qw_ref.shape[1], vw_ref.shape[0]
    depth = w_send_ref.shape[0]
    cut = pl.ds(pl.multiple_of(at_ref[2] * depth, depth), depth)
    w_ref[:, :local] = qw_ref[...]
    w_ref[:, local : 2 * local] = kw_ref[...]
    w_ref[:, 2 * local : 2 * local + half] = vw_ref[...].T
    w_ref[:, 2 * local + half :] = jnp.zeros((width, w_ref.shape[1] - 2 * local - half), BF)
    w_send_ref[...] = w_ref[cut, :]
    own = pl.ds(pl.multiple_of(side * length, length), length)
    other = pl.ds(pl.multiple_of((1 - side) * length, length), length)
    for row in range(rows):
        halo_ref[row * SPAN : (row + 1) * SPAN, :] = x_ref[row, length - SPAN :, :]
        lines = slice(row * half, (row + 1) * half)
        middle = s_ref[row, :, length - SPAN : length]
        s_send_ref[lines, :SPAN] = middle
        s_own_ref[lines, :SPAN] = middle
        s_send_ref[lines, SPAN:] = s_ref[row, :, other]
        s_own_ref[lines, SPAN:] = s_ref[row, :, own]


def open_step(at, qw, kw, vw, x, skip):
    rows, length, width = x.shape
    local, half = qw.shape[1], vw.shape[0]
    columns = -(-(2 * local + half) // 256) * 256
    shapes = [
        (width, columns),
        (width // 4, columns),
        (rows * SPAN, width),
        (rows * half, SPAN + length),
        (rows * half, SPAN + length),
    ]
    return pl.pallas_call(
        open_kernel,
        grid_spec=pltpu.PrefetchScalarGridSpec(
            num_scalar_prefetch=1,
            grid=(1,),
            in_specs=[whole_spec(v) for v in (qw, kw, vw, x, skip)],
            out_specs=[pl.BlockSpec(shape, lambda *_: (0, 0)) for shape in shapes],
        ),
        out_shape=[jax.ShapeDtypeStruct(shape, BF) for shape in shapes],
        cost_estimate=COST,
        name="open",
    )(at, qw, kw, vw, x, skip)


class Rows:
    def __init__(self, width, local, hidden):
        half = local // 2
        self.up = slice(0, hidden)
        self.query = slice(hidden, hidden + local)
        self.value = slice(hidden + local, hidden + local + half)
        start = -(-self.value.stop // 128) * 128
        self.pad = start - self.value.stop
        self.gain_1, self.shift_1, self.gain_2, self.shift_2, self.out, self.down = (
            slice(start + n * width, start + (n + 1) * width) for n in range(6)
        )
        self.size = start + 6 * width


def store_projection(o_ref, values, q_bias, v_bias):
    local, half = q_bias.shape[1], v_bias.shape[1]
    o_ref[:, :local] = ((values[:, :local] + q_bias) * (DH**-0.5)).astype(BF)
    o_ref[:, local : 2 * local] = values[:, local : 2 * local].astype(BF)
    stop = 2 * local + half
    o_ref[:, 2 * local : stop] = (values[:, 2 * local : stop] + v_bias).astype(BF)
    o_ref[:, stop:] = values[:, stop:].astype(BF)


def project_own_kernel(where, n_ref, h_ref, rows_ref, w_ref, ne_ref, o_ref):
    @pl.when(pl.program_id(1) == 0)
    def _():
        ne_ref[...] = norm_rows(
            h_ref[...].astype(F32), rows_ref[:, where.gain_1], rows_ref[:, where.shift_1]
        ).astype(BF)

    @pl.when(pl.program_id(1) > 0)
    def _():
        ne_ref[...] = n_ref[...]

    store_projection(
        o_ref, dot_nn(ne_ref[...], w_ref[...]), rows_ref[:, where.query], rows_ref[:, where.value]
    )


def project_own(where, normed, halo, row_vectors, weight, rows):
    width, columns = weight.shape
    blocks = normed.shape[0] // SPAN // rows
    extended = lambda cols: pl.BlockSpec((SPAN, cols), lambda r, j: (r * (blocks + 1) + j, 0))
    size = rows * (blocks + 1) * SPAN
    return pl.pallas_call(
        functools.partial(project_own_kernel, where),
        grid=(rows, blocks + 1),
        in_specs=[
            pl.BlockSpec((SPAN, width), lambda r, j: (r * blocks + jnp.maximum(j - 1, 0), 0)),
            pl.BlockSpec((SPAN, width), lambda r, j: (r, 0)),
            whole_spec(row_vectors),
            whole_spec(weight),
        ],
        out_specs=[extended(width), extended(columns)],
        out_shape=[
            jax.ShapeDtypeStruct((size, width), BF),
            jax.ShapeDtypeStruct((size, columns), BF),
        ],
        cost_estimate=COST,
        name="project_own",
    )(normed, halo, row_vectors, weight)


def join_cores(at_ref, mine_ref, other_ref, scratch):
    depth = mine_ref.shape[0]
    core = at_ref[0]
    scratch[pl.ds(pl.multiple_of(core * depth, depth), depth), :] = mine_ref[...]
    scratch[pl.ds(pl.multiple_of((1 - core) * depth, depth), depth), :] = other_ref[...]


def project_other_kernel(where, at_ref, ne_ref, mine_ref, other_ref, rows_ref, o_ref, w_s):
    @pl.when(pl.program_id(0) == 0)
    def _():
        join_cores(at_ref, mine_ref, other_ref, w_s)

    store_projection(
        o_ref, dot_nn(ne_ref[...], w_s[...]), rows_ref[:, where.query], rows_ref[:, where.value]
    )


def project_other(where, at, normed_ext, mine, other, row_vectors):
    size, width = normed_ext.shape
    columns = mine.shape[1]
    return pl.pallas_call(
        functools.partial(project_other_kernel, where),
        grid_spec=pltpu.PrefetchScalarGridSpec(
            num_scalar_prefetch=1,
            grid=(size // SPAN,),
            in_specs=[
                pl.BlockSpec((SPAN, width), lambda i, a: (i, 0)),
                *[whole_spec(v) for v in (mine, other, row_vectors)],
            ],
            out_specs=pl.BlockSpec((SPAN, columns), lambda i, a: (i, 0)),
            scratch_shapes=[pltpu.VMEM((width, columns), BF)],
        ),
        out_shape=jax.ShapeDtypeStruct((size, columns), BF),
        cost_estimate=COST,
        name="project_other",
    )(at, normed_ext, mine, other, row_vectors)


def middle_kernel(
    where, at_ref, ml_ref, mr_ref, wl_ref, w1_ref, w2_ref, x_ref, rows_ref, hidden_ref, n_ref, wr_ref
):
    @pl.when(pl.program_id(0) == 0)
    def _():
        join_cores(at_ref, w1_ref, w2_ref, wr_ref)

    values = dot_nn(ml_ref[...], wl_ref[...]) + dot_nn(mr_ref[...], wr_ref[...])
    hidden = x_ref[...].astype(F32) + (values + rows_ref[:, where.out])
    hidden_ref[...] = hidden
    n_ref[...] = norm_rows(hidden, rows_ref[:, where.gain_2], rows_ref[:, where.shift_2]).astype(BF)


def middle(where, at, mixed_l, mixed_r, own, mine, other, x, row_vectors):
    tokens, width = x.shape
    local = mixed_l.shape[1]
    tile = lambda columns: pl.BlockSpec((RC, columns), lambda i, a: (i, 0))
    return pl.pallas_call(
        functools.partial(middle_kernel, where),
        grid_spec=pltpu.PrefetchScalarGridSpec(
            num_scalar_prefetch=1,
            grid=(tokens // RC,),
            in_specs=[
                tile(local), tile(local), *[whole_spec(v) for v in (own, mine, other)],
                tile(width), whole_spec(row_vectors),
            ],
            out_specs=[tile(width), tile(width), whole_spec(own)],
        ),
        out_shape=[
            jax.ShapeDtypeStruct((tokens, width), F32),
            jax.ShapeDtypeStruct((tokens, width), BF),
            jax.ShapeDtypeStruct(own.shape, BF),
        ],
        cost_estimate=COST,
        name="middle",
    )(at, mixed_l, mixed_r, own, mine, other, x, row_vectors)


def norm_pull(values, grad, gain_row):
    center = values - jnp.mean(values, axis=-1, keepdims=True)
    variance = jnp.mean(center * center, axis=-1, keepdims=True)
    rstd = lax.rsqrt(variance + 1e-05)
    unit = center * rstd
    scaled = grad * gain_row
    back = rstd * (
        scaled
        - jnp.mean(scaled, axis=-1, keepdims=True)
        - unit * jnp.mean(scaled * unit, axis=-1, keepdims=True)
    )
    return back, grad * unit


def down_rows(values):
    return jnp.sum(values, axis=0, keepdims=True)


def middle_back_kernel(
    where, at_ref, bl_ref, br_ref, hidden_ref, g_ref, ml_ref, mr_ref, wl_ref, wr_ref, rows_ref,
    hg_ref, gl_ref, gr_ref, keep_l_ref, keep_r_ref, send_ref, sums_ref, acc_l, acc_r,
):
    step = pl.program_id(0)

    @pl.when(step == 0)
    def _():
        acc_l[...] = jnp.zeros_like(acc_l)
        acc_r[...] = jnp.zeros_like(acc_r)
        sums_ref[...] = jnp.zeros_like(sums_ref)

    grad = bl_ref[...] + br_ref[...]
    back, gain_term = norm_pull(hidden_ref[...], grad, rows_ref[:, where.gain_2])
    cot = g_ref[...].astype(F32)
    hidden_grad = cot + back
    low = hidden_grad.astype(BF)
    hg_ref[...] = hidden_grad
    gl_ref[...] = dot_nt(low, wl_ref[...]).astype(BF)
    gr_ref[...] = dot_nt(low, wr_ref[...]).astype(BF)
    acc_l[...] += dot_tn(ml_ref[...], low)
    acc_r[...] += dot_tn(mr_ref[...], low)
    for at, term in enumerate((low.astype(F32), cot, gain_term, grad)):
        sums_ref[at : at + 1, :] += down_rows(term)

    @pl.when(step == pl.num_programs(0) - 1)
    def _():
        depth = keep_l_ref.shape[0]
        core = at_ref[0]
        mine = pl.ds(pl.multiple_of(core * depth, depth), depth)
        other = pl.ds(pl.multiple_of((1 - core) * depth, depth), depth)
        keep_l_ref[...] = acc_l[mine, :].astype(BF)
        keep_r_ref[...] = acc_r[mine, :].astype(BF)
        send_ref[:depth, :] = acc_l[other, :].astype(BF)
        send_ref[depth:, :] = acc_r[other, :].astype(BF)


def middle_back(where, at, back_l, back_r, hidden, grads, mixed_l, mixed_r, own, other, row_vectors):
    tokens, width = hidden.shape
    local = mixed_l.shape[1]
    tile = lambda columns: pl.BlockSpec((RC, columns), lambda i, a: (i, 0))
    fixed = lambda rows: pl.BlockSpec((rows, width), lambda i, a: (0, 0))
    return pl.pallas_call(
        functools.partial(middle_back_kernel, where),
        grid_spec=pltpu.PrefetchScalarGridSpec(
            num_scalar_prefetch=1,
            grid=(tokens // RC,),
            in_specs=[
                tile(width), tile(width), tile(width), tile(width), tile(local), tile(local),
                whole_spec(own), whole_spec(other), whole_spec(row_vectors),
            ],
            out_specs=[
                tile(width), tile(local), tile(local),
                fixed(local // 2), fixed(local // 2), fixed(local), fixed(8),
            ],
            scratch_shapes=[pltpu.VMEM((local, width), F32), pltpu.VMEM((local, width), F32)],
        ),
        out_shape=[
            jax.ShapeDtypeStruct((tokens, width), F32),
            jax.ShapeDtypeStruct((tokens, local), BF),
            jax.ShapeDtypeStruct((tokens, local), BF),
            jax.ShapeDtypeStruct((local // 2, width), BF),
            jax.ShapeDtypeStruct((local // 2, width), BF),
            jax.ShapeDtypeStruct((local, width), BF),
            jax.ShapeDtypeStruct((8, width), F32),
        ],
        cost_estimate=COST,
        name="middle_back",
    )(at, back_l, back_r, hidden, grads, mixed_l, mixed_r, own, other, row_vectors)


def project_grad_kernel(at_ref, n_ref, d_ref, keep_ref, send_ref, sum_ref):
    values = dot_tn(n_ref[...], d_ref[...]).astype(BF)

    @pl.when(pl.program_id(0) == 0)
    def _():
        send_ref[...] = values
        sum_ref[...] = down_rows(d_ref[...].astype(F32))

    @pl.when(pl.program_id(0) == 1)
    def _():
        keep_ref[...] = values


def project_grad(at, normed_ext, grads):
    size, width = normed_ext.shape
    columns = grads.shape[1]
    fixed = pl.BlockSpec((width // 2, columns), lambda i, a: (0, 0))
    return pl.pallas_call(
        project_grad_kernel,
        grid_spec=pltpu.PrefetchScalarGridSpec(
            num_scalar_prefetch=1,
            grid=(2,),
            in_specs=[
                pl.BlockSpec((size, width // 2), lambda i, a: (0, i * a[0] + (1 - i) * (1 - a[0]))),
                whole_spec(grads),
            ],
            out_specs=[fixed, fixed, pl.BlockSpec((1, columns), lambda i, a: (0, 0))],
        ),
        out_shape=[
            jax.ShapeDtypeStruct((width // 2, columns), BF),
            jax.ShapeDtypeStruct((width // 2, columns), BF),
            jax.ShapeDtypeStruct((1, columns), F32),
        ],
        cost_estimate=COST,
        name="project_grad",
    )(at, normed_ext, grads)


def first_back_kernel(
    where, at_ref, dl_ref, dr_ref, wl_ref, mine_ref, other_ref, x_ref, h_ref, hg_ref, rows_ref,
    ig_ref, ih_ref, sums_ref, w_s,
):
    block = pl.program_id(1)

    @pl.when((pl.program_id(0) == 0) & (block == 0))
    def _():
        join_cores(at_ref, mine_ref, other_ref, w_s)
        sums_ref[...] = jnp.zeros_like(sums_ref)

    grad = dot_nt(dl_ref[...], wl_ref[...]) + dot_nt(dr_ref[...], w_s[...])
    values = jnp.where(block == 0, h_ref[...], x_ref[...]).astype(F32)
    back, gain_term = norm_pull(values, grad, rows_ref[:, where.gain_1])
    sums_ref[0:1, :] += down_rows(gain_term)
    sums_ref[1:2, :] += down_rows(grad)

    @pl.when(block == 0)
    def _():
        ih_ref[...] = back.astype(BF)

    @pl.when(block > 0)
    def _():
        ig_ref[...] = hg_ref[...] + back


def first_back(where, at, grads_l, grads_r, own, mine, other, x, halo, hidden_grad, row_vectors, rows):
    tokens, width = x.shape
    columns = grads_l.shape[1]
    blocks = tokens // SPAN // rows
    extended = pl.BlockSpec((SPAN, columns), lambda r, j, a: (r * (blocks + 1) + j, 0))
    inner = pl.BlockSpec((SPAN, width), lambda r, j, a: (r * blocks + jnp.maximum(j - 1, 0), 0))
    outer = pl.BlockSpec((SPAN, width), lambda r, j, a: (r, 0))
    return pl.pallas_call(
        functools.partial(first_back_kernel, where),
        grid_spec=pltpu.PrefetchScalarGridSpec(
            num_scalar_prefetch=1,
            grid=(rows, blocks + 1),
            in_specs=[
                extended, extended, *[whole_spec(v) for v in (own, mine, other)],
                inner, outer, inner, whole_spec(row_vectors),
            ],
            out_specs=[inner, outer, pl.BlockSpec((8, width), lambda r, j, a: (0, 0))],
            scratch_shapes=[pltpu.VMEM((width, columns), BF)],
        ),
        out_shape=[
            jax.ShapeDtypeStruct((tokens, width), F32),
            jax.ShapeDtypeStruct((rows * SPAN, width), BF),
            jax.ShapeDtypeStruct((8, width), F32),
        ],
        cost_estimate=COST,
        name="first_back",
    )(at, grads_l, grads_r, own, mine, other, x, halo, hidden_grad, row_vectors)


def add_halo_kernel(ig_ref, got_ref, o_ref):
    o_ref[...] = ig_ref[...] + got_ref[...].astype(F32)


def add_halo(input_grad, got, rows):
    width = got.shape[1]
    blocks = input_grad.shape[0] // SPAN // rows
    last = pl.BlockSpec((SPAN, width), lambda r: (r * blocks + blocks - 1, 0))
    return pl.pallas_call(
        add_halo_kernel,
        grid=(rows,),
        in_specs=[last, pl.BlockSpec((SPAN, width), lambda r: (r, 0))],
        out_specs=last,
        out_shape=jax.ShapeDtypeStruct(input_grad.shape, F32),
        input_output_aliases={0: 0},
        cost_estimate=COST,
        name="add_halo",
    )(input_grad, got)


def skip_grad_kernel(at_ref, mine_ref, got_ref, o_ref):
    side = at_ref[1]
    rows, half, total = o_ref.shape
    length = total // 2
    own = pl.ds(pl.multiple_of(side * length, length), length)
    other = pl.ds(pl.multiple_of((1 - side) * length, length), length)
    for row in range(rows):
        lines = slice(row * half, (row + 1) * half)
        o_ref[row, :, own] = mine_ref[lines, SPAN:].astype(F32)
        o_ref[row, :, other] = got_ref[lines, SPAN:].astype(F32)
        o_ref[row, :, length - SPAN : length] += mine_ref[lines, :SPAN].astype(F32) + got_ref[
            lines, :SPAN
        ].astype(F32)


def skip_grad_of(at, mine, got, rows):
    lines, size = mine.shape
    shape = (rows, lines // rows, 2 * (size - SPAN))
    return pl.pallas_call(
        skip_grad_kernel,
        grid_spec=pltpu.PrefetchScalarGridSpec(
            num_scalar_prefetch=1,
            grid=(1,),
            in_specs=[whole_spec(mine), whole_spec(got)],
            out_specs=pl.BlockSpec(shape, lambda i, a: (0, 0, 0)),
        ),
        out_shape=jax.ShapeDtypeStruct(shape, F32),
        cost_estimate=COST,
        name="skip_grad",
    )(at, mine, got)


def small_kernel(where, at_ref, m_ref, f_ref, ql_ref, qr_ref, l1_ref, l2_ref, r1_ref, r2_ref, own_ref, other_ref):
    core = at_ref[0]
    local = where.query.stop - where.query.start
    half = where.value.stop - where.value.start
    piece = l1_ref.shape[1]
    for o_ref, q_ref, one_ref, two_ref in (
        (own_ref, ql_ref, l1_ref, l2_ref), (other_ref, qr_ref, r1_ref, r2_ref)
    ):
        o_ref[...] = jnp.zeros_like(o_ref)
        o_ref[:, pl.ds(pl.multiple_of(core * piece, 128), piece)] = one_ref[...]
        o_ref[:, pl.ds(pl.multiple_of((1 - core) * piece, 128), piece)] = two_ref[...]
        o_ref[:, where.query] = q_ref[:, :local]
        o_ref[:, where.value] = q_ref[:, 2 * local : 2 * local + half]
        o_ref[:, where.out] = m_ref[0:1, :]
        o_ref[:, where.down] = m_ref[1:2, :]
        o_ref[:, where.gain_2] = m_ref[2:3, :]
        o_ref[:, where.shift_2] = m_ref[3:4, :]
        o_ref[:, where.gain_1] = f_ref[0:1, :]
        o_ref[:, where.shift_1] = f_ref[1:2, :]


def small_step(where, at, *values):
    return pl.pallas_call(
        functools.partial(small_kernel, where),
        grid_spec=pltpu.PrefetchScalarGridSpec(
            num_scalar_prefetch=1,
            grid=(1,),
            in_specs=[whole_spec(v) for v in values],
            out_specs=[pl.BlockSpec((1, where.size), lambda i, a: (0, 0))] * 2,
        ),
        out_shape=[jax.ShapeDtypeStruct((1, where.size), F32)] * 2,
        cost_estimate=COST,
        name="small",
    )(at, *values)


def feed_out_kernel(parts, factor, at_ref, mine_ref, other_ref, up_ref, down_ref, out_ref):
    core = at_ref[0]
    a, b, c = parts
    step = a + b + c
    piece = up_ref.shape[1] // 2
    for ref, at in ((mine_ref, core), (other_ref, 1 - core)):
        lanes = pl.ds(pl.multiple_of(at * piece, 128), piece)
        for digit in range(factor):
            start = digit * step
            up_ref[digit * a : (digit + 1) * a, lanes] = ref[start : start + a, :].astype(F32)
            rows = pl.ds(pl.multiple_of(at * factor * b, 8) + digit * b, b)
            down_ref[rows, :] = ref[start + a : start + a + b, :].astype(F32)
            rows = pl.ds(pl.multiple_of(at * factor * c, 8) + digit * c, c)
            out_ref[rows, :] = ref[start + a + b : start + step, :].astype(F32)


def feed_out(at, mine, other, parts, factor):
    a, b, c = parts
    width = mine.shape[1]
    shapes = [(factor * a, 2 * width), (2 * factor * b, width), (2 * factor * c, width)]
    return pl.pallas_call(
        functools.partial(feed_out_kernel, parts, factor),
        grid_spec=pltpu.PrefetchScalarGridSpec(
            num_scalar_prefetch=1,
            grid=(1,),
            in_specs=[whole_spec(mine), whole_spec(other)],
            out_specs=[pl.BlockSpec(s, lambda i, a: (0, 0)) for s in shapes],
        ),
        out_shape=[jax.ShapeDtypeStruct(s, F32) for s in shapes],
        cost_estimate=COST,
        name="feed_out",
    )(at, mine, other)


def project_out_kernel(at_ref, mine_ref, other_ref, q_ref, k_ref, v_ref):
    core = at_ref[0]
    depth = mine_ref.shape[0]
    local = q_ref.shape[1]
    for ref, at in ((mine_ref, core), (other_ref, 1 - core)):
        rows = pl.ds(pl.multiple_of(at * depth, depth), depth)
        q_ref[rows, :] = ref[:, :local].astype(F32)
        k_ref[rows, :] = ref[:, local : 2 * local].astype(F32)
        v_ref[:, rows] = ref[:, 2 * local : 2 * local + v_ref.shape[0]].astype(F32).T


def project_out(at, mine, other, local):
    depth = mine.shape[0]
    shapes = [(2 * depth, local), (2 * depth, local), (local // 2, 2 * depth)]
    return pl.pallas_call(
        project_out_kernel,
        grid_spec=pltpu.PrefetchScalarGridSpec(
            num_scalar_prefetch=1,
            grid=(1,),
            in_specs=[whole_spec(mine), whole_spec(other)],
            out_specs=[pl.BlockSpec(s, lambda i, a: (0, 0)) for s in shapes],
        ),
        out_shape=[jax.ShapeDtypeStruct(s, F32) for s in shapes],
        cost_estimate=COST,
        name="project_out",
    )(at, mine, other)


def after(value, *others):
    return lax.optimization_barrier((value, *others))[0]


def together(*values):
    return lax.optimization_barrier(values)


class Chips:
    def __init__(self, count):
        self.count = count
        chips = count // 2
        self.factors = []
        if (chips.bit_length() - 1) % 2:
            self.factors.append(2)
            chips //= 2
        while chips > 1:
            self.factors.append(4)
            chips //= 4
        self.index = lax.axis_index("dp")
        self.core = self.index % 2
        self.near = (self.index // 2) % 2

    def flip(self, value, bit):
        return lax.ppermute(value, "dp", [(i, i ^ bit) for i in range(self.count)])

    def swap_core(self, value):
        return self.flip(value, 1)

    def swap_near(self, value):
        return self.flip(value, 2)

    def shift(self, value, stride, factor, by):
        perm = []
        for i in range(self.count):
            digit = (i // stride) % factor
            perm.append((i, i + (((digit + by) % factor) - digit) * stride))
        return lax.ppermute(value, "dp", perm)

    def stages(self):
        stride = 2
        for factor in self.factors:
            yield stride, factor, (self.index // stride) % factor
            stride *= factor

    def scatter_start(self, value, stage):
        stride, factor, digit = stage
        rows = value.shape[0] // factor
        parts = [lax.dynamic_slice_in_dim(value, digit * rows, rows, 0)]
        for by in range(1, factor):
            part = lax.dynamic_slice_in_dim(value, ((digit + by) % factor) * rows, rows, 0)
            parts.append(self.shift(part, stride, factor, by))
        return tuple(parts)

    def scatter(self, value, stage):
        return add(*self.scatter_start(value, stage))

    def gather_start(self, value, stage):
        stride, factor, digit = stage
        return (value, *(self.shift(value, stride, factor, by) for by in range(1, factor)))

    def gather(self, value, stage):
        return self.gather_finish(self.gather_start(value, stage), stage)

    def gather_finish(self, parts, stage):
        stride, factor, digit = stage
        return jnp.concatenate(
            [
                lax.select_n((digit - at) % factor, *parts)
                if factor > 2
                else jnp.where(digit == at, parts[0], parts[1])
                for at in range(factor)
            ],
            axis=0,
        )

    def sum_small(self, value):
        value = value + self.swap_core(value)
        for stride, factor, digit in self.stages():
            total = value
            for by in range(1, factor):
                total = total + self.shift(value, stride, factor, by)
            value = total
        return value


def swap_tensor(value):
    return lax.ppermute(value, "tensor", [(0, 1), (1, 0)])


def block_of(value, at, count, axis):
    size = value.shape[axis] // count
    return lax.dynamic_slice_in_dim(value, at * size, size, axis)


def in_order(bit, mine, other, axis):
    return jnp.concatenate(
        [jnp.where(bit == 0, mine, other), jnp.where(bit == 0, other, mine)], axis=axis
    )


def add(*values):
    total = values[0].astype(F32)
    for value in values[1:]:
        total = total + value.astype(F32)
    return total.astype(BF)


def on_device(
    dp_count,
    block_input,
    skip_values,
    segment_ids,
    row_fill,
    query_weight,
    query_bias,
    key_weight,
    value_weight,
    value_bias,
    out_weight,
    out_bias,
    up_weight,
    up_bias,
    down_weight,
    down_bias,
    first_gain,
    first_shift,
    second_gain,
    second_shift,
    cotangent,
):
    chips = Chips(dp_count)
    core, near = chips.core, chips.near
    side = lax.axis_index("tensor")
    at = jnp.stack([core, side, 2 * core + near]).astype(jnp.int32)
    rows, length, width = block_input.shape
    tokens = rows * length
    local = query_weight.shape[1]
    local_half = local // 2
    hidden_local = up_weight.shape[1]
    piece = hidden_local // 2
    quarter = 2 * core + near
    stages = list(chips.stages())
    where = Rows(width, local, hidden_local)

    qkv_own, qkv_send, halo_send, skip_send, skip_own = open_step(
        at, query_weight, key_weight, value_weight.T, block_input, jnp.swapaxes(skip_values, 1, 2)
    )
    halo = lax.ppermute(halo_send, "tensor", [(0, 1)])
    qkv_tensor = swap_tensor(qkv_send)
    row_vectors = jnp.concatenate(
        [
            up_bias, query_bias, value_bias, jnp.zeros((where.pad,), F32),
            first_gain, first_shift, second_gain, second_shift, out_bias, down_bias,
        ]
    ).reshape(1, -1)
    rows_other = swap_tensor(after(row_vectors, qkv_send))
    normed = norm_rows(
        after(block_input, halo_send).astype(F32), first_gain, first_shift
    ).astype(BF).reshape(tokens, width)

    position = jnp.arange(segment_ids.shape[1], dtype=jnp.int32)
    usable = jnp.where(position[None] < row_fill[:, None], segment_ids, -1)
    query_seg = lax.dynamic_slice_in_dim(segment_ids, side * length, length, 1)
    key_seg = jnp.concatenate(
        [
            jnp.where(side == 0, -1, usable[:, length - SPAN : length]),
            lax.dynamic_slice_in_dim(usable, side * length, length, 1),
        ],
        axis=1,
    )
    query_seg = query_seg.reshape(rows, 1, length)
    key_seg = key_seg.reshape(rows, SPAN + length, 1)

    key_seg, query_seg, normed, row_vectors, qkv_tensor = together(
        key_seg, query_seg, normed, row_vectors, qkv_tensor
    )
    qkv_near = chips.swap_near(qkv_tensor)
    skip_got = swap_tensor(after(skip_send, qkv_tensor))

    normed_ext, qkv_l = project_own(where, normed, halo, row_vectors, qkv_own, rows)
    qkv_l, qkv_near, skip_got = together(qkv_l, qkv_near, skip_got)
    qkv_mine = in_order(near, qkv_tensor, qkv_near, 0)
    qkv_theirs = chips.swap_core(qkv_mine)
    down_tensor = swap_tensor(after(block_of(down_weight, quarter, 4, 0), qkv_near))
    out_mine = swap_tensor(after(block_of(out_weight, core, 2, 0), qkv_near))
    mixed_l, sums_l = attend_forward(after(qkv_l, qkv_mine), skip_own, key_seg, query_seg)
    mixed_l, qkv_theirs, out_mine, down_tensor, rows_other = together(
        mixed_l, qkv_theirs, out_mine, down_tensor, rows_other
    )
    up_mine = swap_tensor(after(block_of(up_weight, core, 2, 1), down_tensor))
    down_near = chips.swap_near(down_tensor)
    out_theirs = chips.swap_core(out_mine)
    qkv_r = project_other(where, at, after(normed_ext, mixed_l), qkv_mine, qkv_theirs, rows_other)
    mixed_r, sums_r = attend_forward(qkv_r, skip_got, key_seg, query_seg)
    mixed_r, down_near, out_theirs = together(mixed_r, down_near, out_theirs)
    down_r1 = in_order(near, down_tensor, down_near, 0)
    down_r2 = chips.swap_core(down_r1)
    hidden, normed_two, out_other = middle(
        where, at, mixed_l, mixed_r, out_weight, out_mine, out_theirs,
        after(block_input, down_r1).reshape(tokens, width), row_vectors,
    )
    normed_two, up_mine = together(normed_two, up_mine)
    up_r1 = up_mine
    up_r2 = chips.swap_core(up_r1)

    out_grad = cotangent.reshape(tokens, width)
    (up_g_l2, up_g_l1, down_g_l2, down_g_l1, bias_g_l2, bias_g_l1, f_l, b_l) = feed(
        at, normed_two, out_grad, up_weight, up_weight, row_vectors, down_weight, down_weight, True,
    )
    up_r2, down_r2, b_l, up_g_l2, down_g_l2 = together(up_r2, down_r2, b_l, up_g_l2, down_g_l2)
    up_c_l, down_c_l = chips.swap_core(up_g_l2), chips.swap_core(down_g_l2)
    (up_g_r2, up_g_r1, down_g_r2, down_g_r1, bias_g_r2, bias_g_r1, f_r, b_r) = feed(
        at, after(normed_two, b_l), out_grad, up_r2, up_r1, rows_other, down_r2, down_r1, False
    )
    up_g_r2, up_g_r1, down_g_r2, down_g_r1, b_r, up_c_l, down_c_l = together(
        up_g_r2, up_g_r1, down_g_r2, down_g_r1, b_r, up_c_l, down_c_l
    )

    up_c_r, down_c_r = chips.swap_core(up_g_r2), chips.swap_core(down_g_r2)
    up_l, down_l = add(up_g_l1, up_c_l), add(down_g_l1, down_c_l)
    down_lx = chips.scatter_start(down_l, stages[0])
    (hidden_grad, mixed_g_l, mixed_g_r, out_keep_l, out_keep_r, out_send, middle_sums) = middle_back(
        where, at, b_l, b_r, hidden, out_grad, mixed_l, mixed_r, out_weight, out_other, row_vectors
    )
    mixed_g_r, out_send, up_c_r, down_c_r, down_lx = together(
        mixed_g_r, out_send, up_c_r, down_c_r, down_lx
    )

    up_sum_r, down_sum_r = add(up_g_r1, up_c_r), add(down_g_r1, down_c_r)
    up_t = swap_tensor(up_sum_r)
    down_rx = chips.scatter_start(down_sum_r, stages[0])
    out_c = chips.swap_core(out_send)
    qkv_g_r, skip_g_r = attend_backward(
        qkv_r, skip_got, key_seg, query_seg, sums_r, after(mixed_g_r, up_sum_r, down_sum_r)
    )
    qkv_g_r, skip_g_r, down_rx, out_c = together(qkv_g_r, skip_g_r, down_rx, out_c)

    out_rows = local // 2
    down_y = add(*down_rx)
    down_t = swap_tensor(down_y)
    out_y = add(out_keep_r, out_c[out_rows:])
    out_t = swap_tensor(out_y)
    qkv_keep_r, qkv_send_r, qkv_sums_r = project_grad(
        at, after(normed_ext, down_y, out_y), qkv_g_r
    )
    qkv_keep_r, qkv_send_r, up_t = together(qkv_keep_r, qkv_send_r, up_t)
    qkv_c_r = chips.swap_core(qkv_send_r)
    up_1 = add(up_l, up_t)
    up_x = chips.scatter_start(up_1, stages[0])
    qkv_y = add(qkv_keep_r, qkv_c_r)
    qkv_t = swap_tensor(qkv_y)
    qkv_g_l, skip_g_l = attend_backward(
        qkv_l, skip_own, key_seg, query_seg, sums_l, after(mixed_g_l, up_1, qkv_y)
    )
    qkv_g_l, skip_g_l, up_x, down_t, out_t = together(qkv_g_l, skip_g_l, up_x, down_t, out_t)
    skip_back = swap_tensor(skip_g_r)
    out_x = chips.scatter_start(add(out_keep_l, out_c[:out_rows], out_t), stages[0])
    qkv_keep_l, qkv_send_l, qkv_sums_l = project_grad(at, normed_ext, qkv_g_l)
    qkv_c_l = chips.swap_core(qkv_send_l)
    up_2, down_2 = add(*up_x), add(*down_lx, down_t)
    qkv_keep_l, qkv_sums_l, out_x, up_2, down_2 = together(
        qkv_keep_l, qkv_sums_l, out_x, up_2, down_2
    )

    out_2 = add(*out_x)
    feed_2 = jnp.concatenate([up_2, down_2, out_2], axis=0)
    feed_x = chips.scatter_start(feed_2, stages[1])
    input_grad, halo_grad, first_sums = first_back(
        where, at, after(qkv_g_l, feed_2), qkv_g_r, qkv_own, qkv_mine, qkv_theirs,
        block_input.reshape(tokens, width), halo, hidden_grad, row_vectors, rows,
    )
    input_grad, halo_grad, first_sums, qkv_c_l, qkv_t = together(
        input_grad, halo_grad, first_sums, qkv_c_l, qkv_t
    )
    halo_got = lax.ppermute(halo_grad, "tensor", [(1, 0)])
    qkv_x = chips.scatter_start(add(qkv_keep_l, qkv_c_l, qkv_t), stages[0])

    own_small, other_small = small_step(
        where, at, middle_sums, first_sums, qkv_sums_l, qkv_sums_r,
        bias_g_l1, bias_g_l2, bias_g_r1, bias_g_r2,
    )
    small_t = swap_tensor(other_small)
    block_output = hidden + (f_l + after(f_r, input_grad) + down_bias)
    block_output, qkv_x, feed_x, small_t = together(block_output, qkv_x, feed_x, small_t)

    feed_3 = add(*feed_x)
    for stage in stages[2:]:
        feed_3 = chips.scatter(feed_3, stage)
    for stage in reversed(stages[2:]):
        feed_3 = chips.gather(feed_3, stage)
    qkv_2 = add(*qkv_x)
    qkv_x = chips.scatter_start(qkv_2, stages[1])
    feed_x = chips.gather_start(feed_3, stages[1])
    small = own_small + small_t
    small = small + chips.swap_core(small)
    skip_grad = skip_grad_of(at, after(skip_g_l, block_output), skip_back, rows)
    skip_grad, qkv_x, feed_x, small = together(skip_grad, qkv_x, feed_x, small)
    qkv_3 = add(*qkv_x)
    for stage in stages[2:]:
        qkv_3 = chips.scatter(qkv_3, stage)
    for stage in reversed(stages[2:]):
        qkv_3 = chips.gather(qkv_3, stage)
    qkv_x = chips.gather_start(qkv_3, stages[1])
    feed_4 = chips.gather_finish(feed_x, stages[1])
    feed_x = chips.gather_start(feed_4, stages[0])
    small_x = chips.gather_start(small, stages[0])
    input_grad = add_halo(after(input_grad, skip_grad), halo_got, rows)
    input_grad, qkv_x, small_x = together(input_grad, qkv_x, small_x)
    qkv_4 = chips.gather_finish(qkv_x, stages[1])
    qkv_x = chips.gather_start(qkv_4, stages[0])
    small = sum(small_x)
    for stage in stages[1:]:
        small = sum(chips.gather_start(small, stage))
    feed_x, qkv_x, small = together(feed_x, qkv_x, small)
    feed_4 = chips.gather_finish(feed_x, stages[0])
    feed_other = chips.swap_core(feed_4)
    qkv_4 = chips.gather_finish(qkv_x, stages[0])
    qkv_other = chips.swap_core(qkv_4)
    parts = up_2.shape[0], down_2.shape[0], out_2.shape[0]
    up_weight_grad, down_weight_grad, out_weight_grad = feed_out(
        at, feed_4, feed_other, parts, stages[0][1]
    )
    query_weight_grad, key_weight_grad, value_weight_grad = project_out(
        at, qkv_4, qkv_other, local
    )
    small = small[0]

    return (
        block_output.reshape(rows, length, width),
        input_grad.reshape(rows, length, width),
        jnp.swapaxes(skip_grad, 1, 2),
        query_weight_grad,
        small[where.query],
        key_weight_grad,
        value_weight_grad.T,
        small[where.value],
        out_weight_grad,
        small[where.out],
        up_weight_grad,
        small[where.up],
        down_weight_grad,
        small[where.down],
        small[where.gain_1],
        small[where.shift_1],
        small[where.gain_2],
        small[where.shift_2],
    )


def solution(mesh):
    in_specs = (
        P("dp", "tensor", None),
        P("dp", None, "tensor"),
        P("dp", None),
        P("dp"),
        P(None, "tensor"),
        P("tensor"),
        P(None, "tensor"),
        P(None, "tensor"),
        P("tensor"),
        P("tensor", None),
        P(),
        P(None, "tensor"),
        P("tensor"),
        P("tensor", None),
        P(),
        P(),
        P(),
        P(),
        P(),
        P("dp", "tensor", None),
    )
    out_specs = (
        P("dp", "tensor", None),
        P("dp", "tensor", None),
        P("dp", None, "tensor"),
        P(None, "tensor"),
        P("tensor"),
        P(None, "tensor"),
        P(None, "tensor"),
        P("tensor"),
        P("tensor", None),
        P(),
        P(None, "tensor"),
        P("tensor"),
        P("tensor", None),
        P(),
        P(),
        P(),
        P(),
        P(),
    )
    return jax.shard_map(
        functools.partial(on_device, mesh.shape["dp"]),
        mesh=mesh,
        in_specs=in_specs,
        out_specs=out_specs,
        check_vma=False,
    )
```

```python
import functools
import itertools

import jax
import jax.numpy as jnp
from jax import lax
from jax.experimental import pallas as pl
from jax.experimental.pallas import tpu as pltpu
from jax.sharding import PartitionSpec as P

DH = 64
BF = jnp.bfloat16
F32 = jnp.float32
SPAN = 256
QB = 128
WIN = SPAN + QB
TH = 768
RC = 256
NEG = -1000000000.0
COST = pl.CostEstimate(flops=1 << 20, bytes_accessed=1 << 20, transcendentals=0)


def dot_nn(a, b):
    return lax.dot_general(a, b, (((1,), (0,)), ((), ())), preferred_element_type=F32)


def dot_nt(a, b):
    return lax.dot_general(a, b, (((1,), (1,)), ((), ())), preferred_element_type=F32)


def dot_tn(a, b):
    return lax.dot_general(a, b, (((0,), (0,)), ((), ())), preferred_element_type=F32)


def split_pair(block, low_lane):
    zero = jnp.zeros_like(block)
    return jnp.concatenate(
        [jnp.where(low_lane, block, zero), jnp.where(low_lane, zero, block)], axis=0
    )


def window_bias(kseg_ref, qseg_ref, start):
    key_at = lax.broadcasted_iota(jnp.int32, (WIN, QB), 0)
    query_at = lax.broadcasted_iota(jnp.int32, (WIN, QB), 1) + SPAN
    kseg = kseg_ref[0, start : start + WIN, :]
    qseg = qseg_ref[0, :, start : start + QB]
    allowed = ((kseg == qseg) & (key_at <= query_at)) | (key_at == query_at)
    bias = jnp.where(allowed, 0.0, NEG).astype(F32)
    return jnp.concatenate([bias, bias], axis=1)


def pair_values(x_ref, s_ref, t_s, pairs):
    base = 4 * pairs * DH
    for at in range(0, pairs, 2):
        fresh = x_ref[:, base + at * DH : base + at * DH + 128].T
        for pair in range(at, min(at + 2, pairs)):
            t_s[pair, :DH, :] = fresh[(pair - at) * DH : (pair - at + 1) * DH, :]
            t_s[pair, DH:, :] = s_ref[pair * DH : (pair + 1) * DH, :]


def attend_forward_kernel(pairs, x_ref, s_ref, kseg_ref, qseg_ref, o_ref, lse_ref, t_s):
    o_blocks = o_ref.shape[0] // QB
    pair_values(x_ref, s_ref, t_s, pairs)

    low = lax.broadcasted_iota(jnp.int32, (QB, 128), 1) < DH
    for block, pair in itertools.product(range(o_blocks), range(pairs)):
        start = block * QB
        if pair == 0:
            bias = window_bias(kseg_ref, qseg_ref, start)
        win = slice(start, start + WIN)
        rows = slice(start + SPAN, start + SPAN + QB)
        here = slice(start, start + QB)
        cols = slice(pair * 128, pair * 128 + 128)
        key_cols = slice((pairs + pair) * 128, (pairs + pair) * 128 + 128)
        queries = split_pair(x_ref[rows, cols], low)
        scores = dot_nt(x_ref[win, key_cols], queries) + bias
        largest = jnp.max(scores, axis=0, keepdims=True)
        expon = jnp.exp(scores - largest)
        total = jnp.sum(expon, axis=0, keepdims=True)
        probs = (expon * (1.0 / total)).astype(BF)
        out = dot_nn(t_s[pair, :, win], probs)
        out = jnp.concatenate([out[:DH, :QB], out[DH:, QB:]], axis=0)
        o_ref[here, cols] = out.T.astype(BF)
        lse_ref[0, block, pair : pair + 1, :] = largest + jnp.log(total)


def attend_backward_kernel(
    pairs, x_ref, s_ref, kseg_ref, qseg_ref, lse_ref, g_ref, dx_ref, ds_ref, v_s, t_s, dk_s, dv_s
):
    o_blocks = g_ref.shape[0] // QB
    pair_values(x_ref, s_ref, t_s, pairs)
    for pair in range(pairs):
        v_s[pair] = t_s[pair].T
        key_cols = slice((pairs + pair) * 128, (pairs + pair) * 128 + 128)
        t_s[pair] = x_ref[:, key_cols].T
    dk_s[...] = jnp.zeros_like(dk_s)
    dv_s[...] = jnp.zeros_like(dv_s)
    dx_ref[:SPAN, : pairs * 128] = jnp.zeros((SPAN, pairs * 128), BF)

    low = lax.broadcasted_iota(jnp.int32, (QB, 128), 1) < DH
    for block, pair in itertools.product(range(o_blocks), range(pairs)):
        start = block * QB
        if pair == 0:
            bias = window_bias(kseg_ref, qseg_ref, start)
        win = slice(start, start + WIN)
        rows = slice(start + SPAN, start + SPAN + QB)
        here = slice(start, start + QB)
        cols = slice(pair * 128, pair * 128 + 128)
        key_cols = slice((pairs + pair) * 128, (pairs + pair) * 128 + 128)
        queries = split_pair(x_ref[rows, cols], low)
        grads = split_pair(g_ref[here, cols], low)
        scores = dot_nt(x_ref[win, key_cols], queries) + bias
        probs = jnp.exp(scores - lse_ref[0, block, pair : pair + 1, :])
        prob_grad = dot_nt(v_s[pair, win], grads)
        row_total = jnp.sum(probs * prob_grad, axis=0, keepdims=True)
        score_grad = (probs * (prob_grad - row_total)).astype(BF)
        dv_s[pair, win] += dot_nn(probs.astype(BF), grads)
        dk_s[pair, win] += dot_nn(score_grad, queries)
        out = dot_nn(t_s[pair, :, win], score_grad)
        out = jnp.concatenate([out[:DH, :QB], out[DH:, QB:]], axis=0)
        dx_ref[rows, cols] = (out.T * (DH**-0.5)).astype(BF)

    base = 4 * pairs * DH
    low_all = lax.broadcasted_iota(jnp.int32, (x_ref.shape[0], 128), 1) < DH
    for pair in range(pairs):
        key_cols = slice((pairs + pair) * 128, (pairs + pair) * 128 + 128)
        dx_ref[:, key_cols] = dk_s[pair].astype(BF)
        ds_ref[pair * DH : (pair + 1) * DH, :] = dv_s[pair].astype(BF).T[DH:, :]
    for at in range(0, pairs, 2):
        second = pltpu.roll(dv_s[at + 1], DH, 1) if at + 1 < pairs else jnp.zeros_like(dv_s[at])
        dx_ref[:, base + at * DH : base + at * DH + 128] = jnp.where(
            low_all, dv_s[at], second
        ).astype(BF)


def attention_specs(rows, blocks, columns, pairs):
    extended = SPAN + blocks * QB
    x_spec = pl.BlockSpec((extended, columns), lambda r: (r, 0))
    s_spec = pl.BlockSpec((pairs * DH, extended), lambda r: (r, 0))
    kseg_spec = pl.BlockSpec((1, extended, 1), lambda r: (r, 0, 0))
    qseg_spec = pl.BlockSpec((1, 1, blocks * QB), lambda r: (r, 0, 0))
    o_spec = pl.BlockSpec((blocks * QB, pairs * 128), lambda r: (r, 0))
    lse_spec = pl.BlockSpec((1, blocks, pairs, 2 * QB), lambda r: (r, 0, 0, 0))
    return extended, x_spec, s_spec, kseg_spec, qseg_spec, o_spec, lse_spec


def attend_forward(extended_qkv, skip, kseg, qseg):
    rows, blocks, pairs = qseg.shape[0], qseg.shape[2] // QB, skip.shape[0] // DH // qseg.shape[0]
    columns = extended_qkv.shape[1]
    extended, x_spec, s_spec, kseg_spec, qseg_spec, o_spec, lse_spec = attention_specs(
        rows, blocks, columns, pairs
    )
    return pl.pallas_call(
        functools.partial(attend_forward_kernel, pairs),
        grid=(rows,),
        in_specs=[x_spec, s_spec, kseg_spec, qseg_spec],
        out_specs=[o_spec, lse_spec],
        out_shape=[
            jax.ShapeDtypeStruct((rows * blocks * QB, pairs * 128), BF),
            jax.ShapeDtypeStruct((rows, blocks, pairs, 2 * QB), F32),
        ],
        scratch_shapes=[
            pltpu.VMEM((pairs, 128, extended), BF),
        ],
        cost_estimate=COST,
        name="attend_forward",
    )(extended_qkv, skip, kseg, qseg)


def attend_backward(extended_qkv, skip, kseg, qseg, sums, grads):
    rows, blocks, pairs = qseg.shape[0], qseg.shape[2] // QB, skip.shape[0] // DH // qseg.shape[0]
    columns = extended_qkv.shape[1]
    extended, x_spec, s_spec, kseg_spec, qseg_spec, o_spec, lse_spec = attention_specs(
        rows, blocks, columns, pairs
    )
    return pl.pallas_call(
        functools.partial(attend_backward_kernel, pairs),
        grid=(rows,),
        in_specs=[x_spec, s_spec, kseg_spec, qseg_spec, lse_spec, o_spec],
        out_specs=[x_spec, s_spec],
        out_shape=[
            jax.ShapeDtypeStruct((rows * extended, columns), BF),
            jax.ShapeDtypeStruct((rows * pairs * DH, extended), BF),
        ],
        scratch_shapes=[
            pltpu.VMEM((pairs, extended, 128), BF),
            pltpu.VMEM((pairs, 128, extended), BF),
            pltpu.VMEM((pairs, extended, 128), F32),
            pltpu.VMEM((pairs, extended, 128), F32),
        ],
        cost_estimate=COST,
        name="attend_backward",
    )(extended_qkv, skip, kseg, qseg, sums, grads)


def feed_kernel(
    core_ref,
    n_ref,
    g_ref,
    ua_ref,
    ub_ref,
    ba_ref,
    bb_ref,
    da_ref,
    db_ref,
    wua_ref,
    wub_ref,
    wda_ref,
    wdb_ref,
    ga_ref,
    gb_ref,
    down_ref,
    second_ref,
    turned_s,
    act_s,
    upg_s,
):
    step = pl.program_id(0)
    half = pl.num_programs(0) // 2
    first = step < half

    @pl.when(step == 0)
    def _():
        turned_s[...] = n_ref[...].T
        down_ref[...] = jnp.zeros_like(down_ref)
        second_ref[...] = jnp.zeros_like(second_ref)

    up_tile = jnp.where(first, ua_ref[...], ub_ref[...])
    down_tile = jnp.where(first, da_ref[...], db_ref[...])
    bias = jnp.where(first, ba_ref[...], bb_ref[...])
    root = 0.7978845608028654
    for start in range(0, n_ref.shape[0], RC):
        rows = slice(start, start + RC)
        upward = dot_nn(n_ref[rows, :], up_tile) + bias
        act_grad = dot_nt(g_ref[rows, :], down_tile)
        square = upward * upward
        bent = jnp.tanh(root * upward * (1.0 + 0.044715 * square))
        gate = 0.5 * (1.0 + bent)
        slope = gate + 0.5 * root * upward * (1.0 - bent * bent) * (1.0 + 0.134145 * square)
        act = (upward * gate).astype(BF)
        upg = (act_grad * slope).astype(BF)
        act_s[rows, :] = act
        upg_s[rows, :] = upg
        down_ref[rows, :] += dot_nn(act, down_tile)
        second_ref[rows, :] += dot_nt(upg, up_tile)
    up_weight_grad = dot_nn(turned_s[...], upg_s[...]).astype(BF)
    down_weight_grad = dot_tn(act_s[...], g_ref[...]).astype(BF)
    bias_grad = jnp.sum(upg_s[...].astype(F32), axis=0, keepdims=True)

    @pl.when(first)
    def _():
        wua_ref[...] = up_weight_grad
        wda_ref[...] = down_weight_grad
        ga_ref[...] = bias_grad

    @pl.when(jnp.logical_not(first))
    def _():
        wub_ref[...] = up_weight_grad
        wdb_ref[...] = down_weight_grad
        gb_ref[...] = bias_grad


def feed(at, normed, grads, up_a, up_b, bias, down_a, down_b, whole):
    tokens, width = normed.shape
    piece = up_a.shape[1] // 2 if whole else up_a.shape[1]
    tiles = piece // TH

    def a_at(i, c):
        at = jnp.minimum(i, tiles - 1)
        return at + (1 - c[0]) * tiles if whole else at

    def b_at(i, c):
        at = jnp.maximum(i - tiles, 0)
        return at + c[0] * tiles if whole else at

    def out_a(i, c):
        return jnp.minimum(i, tiles - 1)

    def out_b(i, c):
        return jnp.maximum(i - tiles, 0)

    resident = pl.BlockSpec((tokens, width), lambda i, c: (0, 0))
    once = pl.BlockSpec((tokens, width), lambda i, c: (0, 0))
    in_specs = [
        resident,
        resident,
        pl.BlockSpec((width, TH), lambda i, c: (0, a_at(i, c))),
        pl.BlockSpec((width, TH), lambda i, c: (0, b_at(i, c))),
        pl.BlockSpec((1, TH), lambda i, c: (0, out_a(i, c) + (1 - c[0]) * tiles)),
        pl.BlockSpec((1, TH), lambda i, c: (0, out_b(i, c) + c[0] * tiles)),
        pl.BlockSpec((TH, width), lambda i, c: (a_at(i, c), 0)),
        pl.BlockSpec((TH, width), lambda i, c: (b_at(i, c), 0)),
    ]
    out_specs = [
        pl.BlockSpec((width, TH), lambda i, c: (0, out_a(i, c))),
        pl.BlockSpec((width, TH), lambda i, c: (0, out_b(i, c))),
        pl.BlockSpec((TH, width), lambda i, c: (out_a(i, c), 0)),
        pl.BlockSpec((TH, width), lambda i, c: (out_b(i, c), 0)),
        pl.BlockSpec((1, TH), lambda i, c: (0, out_a(i, c))),
        pl.BlockSpec((1, TH), lambda i, c: (0, out_b(i, c))),
        once,
        once,
    ]
    out_shape = [
        jax.ShapeDtypeStruct((width, piece), BF),
        jax.ShapeDtypeStruct((width, piece), BF),
        jax.ShapeDtypeStruct((piece, width), BF),
        jax.ShapeDtypeStruct((piece, width), BF),
        jax.ShapeDtypeStruct((1, piece), F32),
        jax.ShapeDtypeStruct((1, piece), F32),
        jax.ShapeDtypeStruct((tokens, width), F32),
        jax.ShapeDtypeStruct((tokens, width), F32),
    ]
    return pl.pallas_call(
        feed_kernel,
        grid_spec=pltpu.PrefetchScalarGridSpec(
            num_scalar_prefetch=1,
            grid=(2 * tiles,),
            in_specs=in_specs,
            out_specs=out_specs,
            scratch_shapes=[
                pltpu.VMEM((width, tokens), BF),
                pltpu.VMEM((tokens, TH), BF),
                pltpu.VMEM((tokens, TH), BF),
            ],
        ),
        out_shape=out_shape,
        compiler_params=pltpu.CompilerParams(vmem_limit_bytes=56 << 20),
        cost_estimate=COST,
        name="feed",
    )(at, normed, grads, up_a, up_b, bias, bias, down_a, down_b)


def norm_rows(values, gain_row, shift_row):
    center = values - jnp.mean(values, axis=-1, keepdims=True)
    variance = jnp.mean(center * center, axis=-1, keepdims=True)
    return center * lax.rsqrt(variance + 1e-05) * gain_row + shift_row


def whole_spec(value):
    zeros = (0,) * value.ndim
    return pl.BlockSpec(value.shape, lambda *_: zeros)


def open_kernel(
    at_ref, qw_ref, kw_ref, vw_ref, x_ref, s_ref, w_ref, w_send_ref, halo_ref, s_send_ref, s_own_ref
):
    side = at_ref[1]
    rows, length, width = x_ref.shape
    local, half = qw_ref.shape[1], vw_ref.shape[0]
    depth = w_send_ref.shape[0]
    cut = pl.ds(pl.multiple_of(at_ref[0] * depth, depth), depth)
    w_ref[:, :local] = qw_ref[...]
    w_ref[:, local : 2 * local] = kw_ref[...]
    w_ref[:, 2 * local : 2 * local + half] = vw_ref[...].T
    w_ref[:, 2 * local + half :] = jnp.zeros((width, w_ref.shape[1] - 2 * local - half), BF)
    w_send_ref[...] = w_ref[cut, :]
    own = pl.ds(pl.multiple_of(side * length, length), length)
    other = pl.ds(pl.multiple_of((1 - side) * length, length), length)
    for row in range(rows):
        halo_ref[row * SPAN : (row + 1) * SPAN, :] = x_ref[row, length - SPAN :, :]
        lines = slice(row * half, (row + 1) * half)
        middle = s_ref[row, :, length - SPAN : length]
        s_send_ref[lines, :SPAN] = middle
        s_own_ref[lines, :SPAN] = middle
        s_send_ref[lines, SPAN:] = s_ref[row, :, other]
        s_own_ref[lines, SPAN:] = s_ref[row, :, own]


def open_step(at, qw, kw, vw, x, skip):
    rows, length, width = x.shape
    local, half = qw.shape[1], vw.shape[0]
    columns = -(-(2 * local + half) // 256) * 256
    shapes = [
        (width, columns),
        (width // 2, columns),
        (rows * SPAN, width),
        (rows * half, SPAN + length),
        (rows * half, SPAN + length),
    ]
    return pl.pallas_call(
        open_kernel,
        grid_spec=pltpu.PrefetchScalarGridSpec(
            num_scalar_prefetch=1,
            grid=(1,),
            in_specs=[whole_spec(v) for v in (qw, kw, vw, x, skip)],
            out_specs=[pl.BlockSpec(shape, lambda *_: (0, 0)) for shape in shapes],
        ),
        out_shape=[jax.ShapeDtypeStruct(shape, BF) for shape in shapes],
        cost_estimate=COST,
        name="open",
    )(at, qw, kw, vw, x, skip)


class Rows:
    def __init__(self, width, local, hidden):
        half = local // 2
        self.up = slice(0, hidden)
        self.query = slice(hidden, hidden + local)
        self.value = slice(hidden + local, hidden + local + half)
        start = -(-self.value.stop // 128) * 128
        self.pad = start - self.value.stop
        self.gain_1, self.shift_1, self.gain_2, self.shift_2, self.out, self.down = (
            slice(start + n * width, start + (n + 1) * width) for n in range(6)
        )
        self.size = start + 6 * width


def store_projection(o_ref, values, q_bias, v_bias):
    local, half = q_bias.shape[1], v_bias.shape[1]
    o_ref[:, :local] = ((values[:, :local] + q_bias) * (DH**-0.5)).astype(BF)
    o_ref[:, local : 2 * local] = values[:, local : 2 * local].astype(BF)
    stop = 2 * local + half
    o_ref[:, 2 * local : stop] = (values[:, 2 * local : stop] + v_bias).astype(BF)
    o_ref[:, stop:] = values[:, stop:].astype(BF)


def project_own_kernel(where, n_ref, h_ref, rows_ref, w_ref, ne_ref, o_ref):
    ne_ref[:SPAN, :] = norm_rows(
        h_ref[...].astype(F32), rows_ref[:, where.gain_1], rows_ref[:, where.shift_1]
    ).astype(BF)
    ne_ref[SPAN:, :] = n_ref[...]
    store_projection(
        o_ref, dot_nn(ne_ref[...], w_ref[...]), rows_ref[:, where.query], rows_ref[:, where.value]
    )


def project_own(where, normed, halo, row_vectors, weight, rows):
    width, columns = weight.shape
    length = normed.shape[0] // rows
    size = SPAN + length
    row = lambda count, cols: pl.BlockSpec((count, cols), lambda r: (r, 0))
    return pl.pallas_call(
        functools.partial(project_own_kernel, where),
        grid=(rows,),
        in_specs=[row(length, width), row(SPAN, width), whole_spec(row_vectors), whole_spec(weight)],
        out_specs=[row(size, width), row(size, columns)],
        out_shape=[
            jax.ShapeDtypeStruct((rows * size, width), BF),
            jax.ShapeDtypeStruct((rows * size, columns), BF),
        ],
        cost_estimate=COST,
        name="project_own",
    )(normed, halo, row_vectors, weight)


def join_cores(at_ref, mine_ref, other_ref, scratch):
    depth = mine_ref.shape[0]
    core = at_ref[0]
    scratch[pl.ds(pl.multiple_of(core * depth, depth), depth), :] = mine_ref[...]
    scratch[pl.ds(pl.multiple_of((1 - core) * depth, depth), depth), :] = other_ref[...]


def project_other_kernel(where, at_ref, ne_ref, mine_ref, other_ref, rows_ref, o_ref, w_s):
    @pl.when(pl.program_id(0) == 0)
    def _():
        join_cores(at_ref, mine_ref, other_ref, w_s)

    store_projection(
        o_ref, dot_nn(ne_ref[...], w_s[...]), rows_ref[:, where.query], rows_ref[:, where.value]
    )


def project_other(where, at, normed_ext, mine, other, row_vectors, rows):
    size, width = normed_ext.shape
    step = size // rows
    columns = mine.shape[1]
    return pl.pallas_call(
        functools.partial(project_other_kernel, where),
        grid_spec=pltpu.PrefetchScalarGridSpec(
            num_scalar_prefetch=1,
            grid=(rows,),
            in_specs=[
                pl.BlockSpec((step, width), lambda i, a: (i, 0)),
                *[whole_spec(v) for v in (mine, other, row_vectors)],
            ],
            out_specs=pl.BlockSpec((step, columns), lambda i, a: (i, 0)),
            scratch_shapes=[pltpu.VMEM((width, columns), BF)],
        ),
        out_shape=jax.ShapeDtypeStruct((size, columns), BF),
        cost_estimate=COST,
        name="project_other",
    )(at, normed_ext, mine, other, row_vectors)


def middle_kernel(
    where, at_ref, ml_ref, mr_ref, wl_ref, w1_ref, w2_ref, x_ref, rows_ref, hidden_ref, n_ref, wr_ref
):
    @pl.when(pl.program_id(0) == 0)
    def _():
        join_cores(at_ref, w1_ref, w2_ref, wr_ref)

    values = dot_nn(ml_ref[...], wl_ref[...]) + dot_nn(mr_ref[...], wr_ref[...])
    hidden = x_ref[...].astype(F32) + (values + rows_ref[:, where.out])
    hidden_ref[...] = hidden
    n_ref[...] = norm_rows(hidden, rows_ref[:, where.gain_2], rows_ref[:, where.shift_2]).astype(BF)


def middle(where, at, mixed_l, mixed_r, own, mine, other, x, row_vectors):
    tokens, width = x.shape
    local = mixed_l.shape[1]
    tile = lambda columns: pl.BlockSpec((RC, columns), lambda i, a: (i, 0))
    return pl.pallas_call(
        functools.partial(middle_kernel, where),
        grid_spec=pltpu.PrefetchScalarGridSpec(
            num_scalar_prefetch=1,
            grid=(tokens // RC,),
            in_specs=[
                tile(local), tile(local), *[whole_spec(v) for v in (own, mine, other)],
                tile(width), whole_spec(row_vectors),
            ],
            out_specs=[tile(width), tile(width), whole_spec(own)],
        ),
        out_shape=[
            jax.ShapeDtypeStruct((tokens, width), F32),
            jax.ShapeDtypeStruct((tokens, width), BF),
            jax.ShapeDtypeStruct(own.shape, BF),
        ],
        cost_estimate=COST,
        name="middle",
    )(at, mixed_l, mixed_r, own, mine, other, x, row_vectors)


def norm_pull(values, grad, gain_row):
    center = values - jnp.mean(values, axis=-1, keepdims=True)
    variance = jnp.mean(center * center, axis=-1, keepdims=True)
    rstd = lax.rsqrt(variance + 1e-05)
    unit = center * rstd
    scaled = grad * gain_row
    back = rstd * (
        scaled
        - jnp.mean(scaled, axis=-1, keepdims=True)
        - unit * jnp.mean(scaled * unit, axis=-1, keepdims=True)
    )
    return back, grad * unit


def down_rows(values):
    return jnp.sum(values, axis=0, keepdims=True)


def middle_back_kernel(
    where, bl_ref, br_ref, hidden_ref, g_ref, ml_ref, mr_ref, wl_ref, wr_ref, rows_ref,
    hg_ref, gl_ref, gr_ref, ol_ref, or_ref, sums_ref, acc_l, acc_r,
):
    step = pl.program_id(0)

    @pl.when(step == 0)
    def _():
        acc_l[...] = jnp.zeros_like(acc_l)
        acc_r[...] = jnp.zeros_like(acc_r)
        sums_ref[...] = jnp.zeros_like(sums_ref)

    grad = bl_ref[...] + br_ref[...]
    back, gain_term = norm_pull(hidden_ref[...], grad, rows_ref[:, where.gain_2])
    cot = g_ref[...].astype(F32)
    hidden_grad = cot + back
    low = hidden_grad.astype(BF)
    hg_ref[...] = hidden_grad
    gl_ref[...] = dot_nt(low, wl_ref[...]).astype(BF)
    gr_ref[...] = dot_nt(low, wr_ref[...]).astype(BF)
    turned = low.T
    acc_l[...] += dot_nn(turned, ml_ref[...])
    acc_r[...] += dot_nn(turned, mr_ref[...])
    for at, term in enumerate((low.astype(F32), cot, gain_term, grad)):
        sums_ref[at : at + 1, :] += down_rows(term)

    @pl.when(step == pl.num_programs(0) - 1)
    def _():
        ol_ref[...] = acc_l[...].astype(BF)
        or_ref[...] = acc_r[...].astype(BF)


def middle_back(where, back_l, back_r, hidden, grads, mixed_l, mixed_r, own, other, row_vectors):
    tokens, width = hidden.shape
    local = mixed_l.shape[1]
    tile = lambda columns: pl.BlockSpec((RC, columns), lambda i: (i, 0))
    fixed = lambda rows, columns: pl.BlockSpec((rows, columns), lambda i: (0, 0))
    return pl.pallas_call(
        functools.partial(middle_back_kernel, where),
        grid=(tokens // RC,),
        in_specs=[
            tile(width), tile(width), tile(width), tile(width), tile(local), tile(local),
            whole_spec(own), whole_spec(other), whole_spec(row_vectors),
        ],
        out_specs=[
            tile(width), tile(local), tile(local),
            fixed(width, local), fixed(width, local), fixed(8, width),
        ],
        scratch_shapes=[pltpu.VMEM((width, local), F32), pltpu.VMEM((width, local), F32)],
        out_shape=[
            jax.ShapeDtypeStruct((tokens, width), F32),
            jax.ShapeDtypeStruct((tokens, local), BF),
            jax.ShapeDtypeStruct((tokens, local), BF),
            jax.ShapeDtypeStruct((width, local), BF),
            jax.ShapeDtypeStruct((width, local), BF),
            jax.ShapeDtypeStruct((8, width), F32),
        ],
        cost_estimate=COST,
        name="middle_back",
    )(back_l, back_r, hidden, grads, mixed_l, mixed_r, own, other, row_vectors)


def project_grad_kernel(at_ref, n_ref, d_ref, w_ref, keep_ref, send_ref, sum_ref):
    values = dot_tn(n_ref[...], d_ref[...]).astype(BF)
    columns = d_ref.shape[1]

    @pl.when(pl.program_id(0) == 0)
    def _():
        send_ref[:, :columns] = values
        send_ref[:, columns:] = w_ref[...]
        sum_ref[...] = down_rows(d_ref[...].astype(F32))

    @pl.when(pl.program_id(0) == 1)
    def _():
        keep_ref[:, :columns] = values
        keep_ref[:, columns:] = w_ref[...]


def project_grad(at, normed_ext, grads, out_grad):
    size, width = normed_ext.shape
    columns, more = grads.shape[1], out_grad.shape[1]
    fixed = pl.BlockSpec((width // 2, columns + more), lambda i, a: (0, 0))
    half = lambda i, a: i * a[0] + (1 - i) * (1 - a[0])
    return pl.pallas_call(
        project_grad_kernel,
        grid_spec=pltpu.PrefetchScalarGridSpec(
            num_scalar_prefetch=1,
            grid=(2,),
            in_specs=[
                pl.BlockSpec((size, width // 2), lambda i, a: (0, half(i, a))),
                whole_spec(grads),
                pl.BlockSpec((width // 2, more), lambda i, a: (half(i, a), 0)),
            ],
            out_specs=[fixed, fixed, pl.BlockSpec((1, columns), lambda i, a: (0, 0))],
        ),
        out_shape=[
            jax.ShapeDtypeStruct((width // 2, columns + more), BF),
            jax.ShapeDtypeStruct((width // 2, columns + more), BF),
            jax.ShapeDtypeStruct((1, columns), F32),
        ],
        cost_estimate=COST,
        name="project_grad",
    )(at, normed_ext, grads, out_grad)


def first_back_kernel(
    where, at_ref, dl_ref, dr_ref, wl_ref, mine_ref, other_ref, x_ref, h_ref, hg_ref, rows_ref,
    ig_ref, ih_ref, sums_ref, w_s,
):
    block = pl.program_id(1)

    @pl.when((pl.program_id(0) == 0) & (block == 0))
    def _():
        join_cores(at_ref, mine_ref, other_ref, w_s)
        sums_ref[...] = jnp.zeros_like(sums_ref)

    grad = dot_nt(dl_ref[...], wl_ref[...]) + dot_nt(dr_ref[...], w_s[...])
    values = jnp.where(block == 0, h_ref[...], x_ref[...]).astype(F32)
    back, gain_term = norm_pull(values, grad, rows_ref[:, where.gain_1])
    sums_ref[0:1, :] += down_rows(gain_term)
    sums_ref[1:2, :] += down_rows(grad)

    @pl.when(block == 0)
    def _():
        ih_ref[...] = back.astype(BF)

    @pl.when(block > 0)
    def _():
        ig_ref[...] = hg_ref[...] + back


def first_back(where, at, grads_l, grads_r, own, mine, other, x, halo, hidden_grad, row_vectors, rows):
    tokens, width = x.shape
    columns = grads_l.shape[1]
    blocks = tokens // SPAN // rows
    extended = pl.BlockSpec((SPAN, columns), lambda r, j, a: (r * (blocks + 1) + j, 0))
    inner = pl.BlockSpec((SPAN, width), lambda r, j, a: (r * blocks + jnp.maximum(j - 1, 0), 0))
    outer = pl.BlockSpec((SPAN, width), lambda r, j, a: (r, 0))
    return pl.pallas_call(
        functools.partial(first_back_kernel, where),
        grid_spec=pltpu.PrefetchScalarGridSpec(
            num_scalar_prefetch=1,
            grid=(rows, blocks + 1),
            in_specs=[
                extended, extended, *[whole_spec(v) for v in (own, mine, other)],
                inner, outer, inner, whole_spec(row_vectors),
            ],
            out_specs=[inner, outer, pl.BlockSpec((8, width), lambda r, j, a: (0, 0))],
            scratch_shapes=[pltpu.VMEM((width, columns), BF)],
        ),
        out_shape=[
            jax.ShapeDtypeStruct((tokens, width), F32),
            jax.ShapeDtypeStruct((rows * SPAN, width), BF),
            jax.ShapeDtypeStruct((8, width), F32),
        ],
        cost_estimate=COST,
        name="first_back",
    )(at, grads_l, grads_r, own, mine, other, x, halo, hidden_grad, row_vectors)


def add_halo_kernel(ig_ref, got_ref, o_ref):
    o_ref[...] = ig_ref[...] + got_ref[...].astype(F32)


def add_halo(input_grad, got, rows):
    width = got.shape[1]
    blocks = input_grad.shape[0] // SPAN // rows
    last = pl.BlockSpec((SPAN, width), lambda r: (r * blocks + blocks - 1, 0))
    return pl.pallas_call(
        add_halo_kernel,
        grid=(rows,),
        in_specs=[last, pl.BlockSpec((SPAN, width), lambda r: (r, 0))],
        out_specs=last,
        out_shape=jax.ShapeDtypeStruct(input_grad.shape, F32),
        input_output_aliases={0: 0},
        cost_estimate=COST,
        name="add_halo",
    )(input_grad, got)


def skip_grad_kernel(at_ref, mine_ref, got_ref, o_ref):
    side = at_ref[1]
    rows, half, total = o_ref.shape
    length = total // 2
    own = pl.ds(pl.multiple_of(side * length, length), length)
    other = pl.ds(pl.multiple_of((1 - side) * length, length), length)
    for row in range(rows):
        lines = slice(row * half, (row + 1) * half)
        o_ref[row, :, own] = mine_ref[lines, SPAN:].astype(F32)
        o_ref[row, :, other] = got_ref[lines, SPAN:].astype(F32)
        o_ref[row, :, length - SPAN : length] += mine_ref[lines, :SPAN].astype(F32) + got_ref[
            lines, :SPAN
        ].astype(F32)


def skip_grad_of(at, mine, got, rows):
    lines, size = mine.shape
    shape = (rows, lines // rows, 2 * (size - SPAN))
    return pl.pallas_call(
        skip_grad_kernel,
        grid_spec=pltpu.PrefetchScalarGridSpec(
            num_scalar_prefetch=1,
            grid=(1,),
            in_specs=[whole_spec(mine), whole_spec(got)],
            out_specs=pl.BlockSpec(shape, lambda i, a: (0, 0, 0)),
        ),
        out_shape=jax.ShapeDtypeStruct(shape, F32),
        cost_estimate=COST,
        name="skip_grad",
    )(at, mine, got)


def small_kernel(where, at_ref, m_ref, f_ref, ql_ref, qr_ref, l1_ref, l2_ref, r1_ref, r2_ref, own_ref, other_ref):
    core = at_ref[0]
    local = where.query.stop - where.query.start
    half = where.value.stop - where.value.start
    piece = l1_ref.shape[1]
    for o_ref, q_ref, one_ref, two_ref in (
        (own_ref, ql_ref, l1_ref, l2_ref), (other_ref, qr_ref, r1_ref, r2_ref)
    ):
        o_ref[...] = jnp.zeros_like(o_ref)
        o_ref[:, pl.ds(pl.multiple_of(core * piece, 128), piece)] = one_ref[...]
        o_ref[:, pl.ds(pl.multiple_of((1 - core) * piece, 128), piece)] = two_ref[...]
        o_ref[:, where.query] = q_ref[:, :local]
        o_ref[:, where.value] = q_ref[:, 2 * local : 2 * local + half]
        o_ref[:, where.out] = m_ref[0:1, :]
        o_ref[:, where.down] = m_ref[1:2, :]
        o_ref[:, where.gain_2] = m_ref[2:3, :]
        o_ref[:, where.shift_2] = m_ref[3:4, :]
        o_ref[:, where.gain_1] = f_ref[0:1, :]
        o_ref[:, where.shift_1] = f_ref[1:2, :]


def small_step(where, at, *values):
    return pl.pallas_call(
        functools.partial(small_kernel, where),
        grid_spec=pltpu.PrefetchScalarGridSpec(
            num_scalar_prefetch=1,
            grid=(1,),
            in_specs=[whole_spec(v) for v in values],
            out_specs=[pl.BlockSpec((1, where.size), lambda i, a: (0, 0))] * 2,
        ),
        out_shape=[jax.ShapeDtypeStruct((1, where.size), F32)] * 2,
        cost_estimate=COST,
        name="small",
    )(at, *values)


def down_out_kernel(at_ref, mine_ref, other_ref, o_ref):
    is_mine = pl.program_id(0) // 2 == at_ref[0]
    o_ref[...] = jnp.where(is_mine, mine_ref[...], other_ref[...]).astype(F32)


def down_out(at, mine, other):
    rows, width = mine.shape
    block = pl.BlockSpec((rows // 2, width), lambda i, a: (i % 2, 0))
    return pl.pallas_call(
        down_out_kernel,
        grid_spec=pltpu.PrefetchScalarGridSpec(
            num_scalar_prefetch=1,
            grid=(4,),
            in_specs=[block, block],
            out_specs=pl.BlockSpec((rows // 2, width), lambda i, a: (i, 0)),
        ),
        out_shape=jax.ShapeDtypeStruct((2 * rows, width), F32),
        cost_estimate=COST,
        name="down_out",
    )(at, mine, other)


def up_out_kernel(at_ref, mine_ref, other_ref, o_ref):
    core = at_ref[0]
    piece = mine_ref.shape[1]
    for ref, at in ((mine_ref, core), (other_ref, 1 - core)):
        o_ref[:, pl.ds(pl.multiple_of(at * piece, 128), piece)] = ref[...].astype(F32)


def up_out(at, mine, other):
    rows, width = mine.shape
    block = pl.BlockSpec((rows // 4, width), lambda i, a: (i, 0))
    return pl.pallas_call(
        up_out_kernel,
        grid_spec=pltpu.PrefetchScalarGridSpec(
            num_scalar_prefetch=1,
            grid=(4,),
            in_specs=[block, block],
            out_specs=pl.BlockSpec((rows // 4, 2 * width), lambda i, a: (i, 0)),
        ),
        out_shape=jax.ShapeDtypeStruct((rows, 2 * width), F32),
        cost_estimate=COST,
        name="up_out",
    )(at, mine, other)


def project_out_kernel(blocks, at_ref, mine_ref, other_ref, q_ref, k_ref, v_ref, out_ref, small_ref):
    core = at_ref[0]
    local = q_ref.shape[1]
    depth = q_ref.shape[0] // 2
    count = depth // blocks
    step = mine_ref.shape[0] // blocks
    columns = mine_ref.shape[1] - local
    for ref, at in ((mine_ref, core), (other_ref, 1 - core)):
        start = pl.multiple_of(at * depth, depth)
        places = [(n % (blocks // 2)) * 2 + n // (blocks // 2) for n in range(blocks)]
        parts = [ref[n * step : n * step + count, :].astype(F32) for n in places]
        values = jnp.concatenate(parts, axis=0)
        rows = pl.ds(start, depth)
        q_ref[rows, :] = values[:, :local]
        k_ref[rows, :] = values[:, local : 2 * local]
        v_ref[:, rows] = values[:, 2 * local : 2 * local + v_ref.shape[0]].T
        out_ref[:, rows] = values[:, columns:].T
    small_ref[...] = sum(
        mine_ref[n * step + count : (n + 1) * step, :].astype(F32) for n in range(blocks)
    )


def project_out(at, mine, other, local, depth, blocks):
    columns = mine.shape[1]
    rest = (mine.shape[0] - depth) // blocks
    shapes = [
        (2 * depth, local), (2 * depth, local), (local // 2, 2 * depth), (local, 2 * depth),
        (rest, columns),
    ]
    return pl.pallas_call(
        functools.partial(project_out_kernel, blocks),
        grid_spec=pltpu.PrefetchScalarGridSpec(
            num_scalar_prefetch=1,
            grid=(1,),
            in_specs=[whole_spec(mine), whole_spec(other)],
            out_specs=[pl.BlockSpec(s, lambda i, a: (0, 0)) for s in shapes],
        ),
        out_shape=[jax.ShapeDtypeStruct(s, F32) for s in shapes],
        cost_estimate=COST,
        name="project_out",
    )(at, mine, other)


def after(value, *others):
    return lax.optimization_barrier((value, *others))[0]


def together(*values):
    return lax.optimization_barrier(values)


class Chips:
    def __init__(self, count):
        self.count = count
        self.factors = [2] * ((count // 2).bit_length() - 1)
        self.index = lax.axis_index("dp")
        self.core = self.index % 2

    def flip(self, value, bit):
        return lax.ppermute(value, "dp", [(i, i ^ bit) for i in range(self.count)])

    def swap_core(self, value):
        return self.flip(value, 1)

    def shift(self, value, stride, factor, by):
        perm = []
        for i in range(self.count):
            digit = (i // stride) % factor
            perm.append((i, i + (((digit + by) % factor) - digit) * stride))
        return lax.ppermute(value, "dp", perm)

    def stages(self):
        stride = 2
        for factor in self.factors:
            yield stride, factor, (self.index // stride) % factor
            stride *= factor

    def scatter_start(self, value, stage):
        stride, factor, digit = stage
        rows = value.shape[0] // factor
        parts = [lax.dynamic_slice_in_dim(value, digit * rows, rows, 0)]
        for by in range(1, factor):
            part = lax.dynamic_slice_in_dim(value, ((digit + by) % factor) * rows, rows, 0)
            parts.append(self.shift(part, stride, factor, by))
        return tuple(parts)

    def scatter(self, value, stage):
        return add(*self.scatter_start(value, stage))

    def gather_start(self, value, stage):
        stride, factor, digit = stage
        return (value, *(self.shift(value, stride, factor, by) for by in range(1, factor)))

    def gather(self, value, stage):
        return self.gather_finish(self.gather_start(value, stage), stage)

    def gather_finish(self, parts, stage):
        stride, factor, digit = stage
        return jnp.concatenate(
            [
                lax.select_n((digit - at) % factor, *parts)
                if factor > 2
                else jnp.where(digit == at, parts[0], parts[1])
                for at in range(factor)
            ],
            axis=0,
        )

    def sum_small(self, value):
        value = value + self.swap_core(value)
        for stride, factor, digit in self.stages():
            total = value
            for by in range(1, factor):
                total = total + self.shift(value, stride, factor, by)
            value = total
        return value


def swap_tensor(value):
    return lax.ppermute(value, "tensor", [(0, 1), (1, 0)])


def block_of(value, at, count, axis):
    size = value.shape[axis] // count
    return lax.dynamic_slice_in_dim(value, at * size, size, axis)


def in_order(bit, mine, other, axis):
    return jnp.concatenate(
        [jnp.where(bit == 0, mine, other), jnp.where(bit == 0, other, mine)], axis=axis
    )


def add(*values):
    total = values[0].astype(F32)
    for value in values[1:]:
        total = total + value.astype(F32)
    return total.astype(BF)


def on_device(
    dp_count,
    block_input,
    skip_values,
    segment_ids,
    row_fill,
    query_weight,
    query_bias,
    key_weight,
    value_weight,
    value_bias,
    out_weight,
    out_bias,
    up_weight,
    up_bias,
    down_weight,
    down_bias,
    first_gain,
    first_shift,
    second_gain,
    second_shift,
    cotangent,
):
    chips = Chips(dp_count)
    core = chips.core
    side = lax.axis_index("tensor")
    at = jnp.stack([core, side]).astype(jnp.int32)
    rows, length, width = block_input.shape
    tokens = rows * length
    local = query_weight.shape[1]
    local_half = local // 2
    hidden_local = up_weight.shape[1]
    piece = hidden_local // 2
    stages = list(chips.stages())
    where = Rows(width, local, hidden_local)

    qkv_own, qkv_send, halo_send, skip_send, skip_own = open_step(
        at, query_weight, key_weight, value_weight.T, block_input, jnp.swapaxes(skip_values, 1, 2)
    )
    halo = lax.ppermute(halo_send, "tensor", [(0, 1)])
    row_vectors = jnp.concatenate(
        [
            up_bias, query_bias, value_bias, jnp.zeros((where.pad,), F32),
            first_gain, first_shift, second_gain, second_shift, out_bias, down_bias,
        ]
    ).reshape(1, -1)
    normed = norm_rows(
        after(block_input, halo_send).astype(F32), first_gain, first_shift
    ).astype(BF).reshape(tokens, width)

    position = jnp.arange(segment_ids.shape[1], dtype=jnp.int32)
    usable = jnp.where(position[None] < row_fill[:, None], segment_ids, -1)
    query_seg = lax.dynamic_slice_in_dim(segment_ids, side * length, length, 1)
    key_seg = jnp.concatenate(
        [
            jnp.where(side == 0, -1, usable[:, length - SPAN : length]),
            lax.dynamic_slice_in_dim(usable, side * length, length, 1),
        ],
        axis=1,
    )
    query_seg = query_seg.reshape(rows, 1, length)
    key_seg = key_seg.reshape(rows, SPAN + length, 1)

    out_piece = block_of(out_weight, core, 2, 0)
    down_piece = block_of(down_weight, core, 2, 0)
    up_piece = block_of(up_weight, core, 2, 1)
    key_seg, query_seg, normed, row_vectors, qkv_send, out_piece, down_piece, up_piece = together(
        key_seg, query_seg, normed, row_vectors, qkv_send, out_piece, down_piece, up_piece
    )
    qkv_mine = swap_tensor(qkv_send)
    rows_other = swap_tensor(after(row_vectors, qkv_send))

    normed_ext, qkv_l = project_own(where, normed, halo, row_vectors, qkv_own, rows)
    qkv_l, skip_send, qkv_mine, rows_other = together(qkv_l, skip_send, qkv_mine, rows_other)
    qkv_theirs = chips.swap_core(qkv_mine)
    skip_got = swap_tensor(skip_send)
    mixed_l, sums_l = attend_forward(qkv_l, skip_own, key_seg, query_seg)
    mixed_l, qkv_theirs, skip_got, out_piece, down_piece = together(
        mixed_l, qkv_theirs, skip_got, out_piece, down_piece
    )
    out_mine = swap_tensor(out_piece)
    qkv_r = project_other(
        where, at, after(normed_ext, mixed_l), qkv_mine, qkv_theirs, rows_other, rows
    )
    qkv_r, out_mine, down_piece, up_piece = together(qkv_r, out_mine, down_piece, up_piece)
    down_r1 = swap_tensor(down_piece)
    out_theirs = chips.swap_core(out_mine)
    up_r1 = swap_tensor(up_piece)
    mixed_r, sums_r = attend_forward(qkv_r, skip_got, key_seg, query_seg)
    mixed_r, out_theirs = together(mixed_r, out_theirs)
    hidden, normed_two, out_other = middle(
        where, at, mixed_l, mixed_r, out_weight, out_mine, out_theirs,
        block_input.reshape(tokens, width), row_vectors,
    )

    out_grad = cotangent.reshape(tokens, width)
    (up_g_l2, up_g_l1, down_g_l2, down_g_l1, bias_g_l2, bias_g_l1, f_l, b_l) = feed(
        at, normed_two, out_grad, up_weight, up_weight, row_vectors, down_weight, down_weight, True,
    )
    b_l, up_g_l2, down_g_l2, down_r1, up_r1 = together(b_l, up_g_l2, down_g_l2, down_r1, up_r1)
    down_r2 = chips.swap_core(down_r1)
    up_r2 = chips.swap_core(up_r1)
    block_half = hidden + (after(f_l, b_l) + down_bias)
    block_half, up_r2, down_r2, up_g_l2, down_g_l2 = together(
        block_half, up_r2, down_r2, up_g_l2, down_g_l2
    )
    up_c_l, down_c_l = chips.swap_core(up_g_l2), chips.swap_core(down_g_l2)
    (up_g_r2, up_g_r1, down_g_r2, down_g_r1, bias_g_r2, bias_g_r1, f_r, b_r) = feed(
        at, after(normed_two, block_half), out_grad, up_r2, up_r1, rows_other, down_r2, down_r1, False
    )
    up_g_r2, up_g_r1, down_g_r2, down_g_r1, b_r, up_c_l, down_c_l = together(
        up_g_r2, up_g_r1, down_g_r2, down_g_r1, b_r, up_c_l, down_c_l
    )

    up_c_r, down_c_r = chips.swap_core(up_g_r2), chips.swap_core(down_g_r2)
    up_l, down_l = add(up_g_l1, up_c_l), add(down_g_l1, down_c_l)
    down_lx = chips.scatter_start(down_l, stages[0])
    hidden_grad, mixed_g_l, mixed_g_r, out_g_l, out_g_r, middle_sums = middle_back(
        where, b_l, b_r, hidden, out_grad, mixed_l, mixed_r, out_weight, out_other, row_vectors
    )
    mixed_g_r, up_c_r, down_c_r, down_lx = together(mixed_g_r, up_c_r, down_c_r, down_lx)

    up_sum_r, down_sum_r = add(up_g_r1, up_c_r), add(down_g_r1, down_c_r)
    down_rx = chips.scatter_start(down_sum_r, stages[0])
    up_t = swap_tensor(up_sum_r)
    qkv_g_r, skip_g_r = attend_backward(
        qkv_r, skip_got, key_seg, query_seg, sums_r, after(mixed_g_r, up_sum_r, down_sum_r)
    )
    qkv_g_r, skip_g_r, down_rx = together(qkv_g_r, skip_g_r, down_rx)

    down_y = add(*down_rx)
    down_t = swap_tensor(down_y)
    qkv_keep_r, qkv_send_r, qkv_sums_r = project_grad(
        at, after(normed_ext, down_y), qkv_g_r, out_g_r
    )
    qkv_keep_r, qkv_send_r, up_t = together(qkv_keep_r, qkv_send_r, up_t)
    qkv_c_r = chips.swap_core(qkv_send_r)
    up_1 = add(up_l, up_t)
    up_x = chips.scatter_start(up_1, stages[0])
    qkv_y = add(qkv_keep_r, qkv_c_r)
    qkv_t_1 = swap_tensor(qkv_y[: width // 6])
    qkv_g_l, skip_g_l = attend_backward(
        qkv_l, skip_own, key_seg, query_seg, sums_l, after(mixed_g_l, up_1, qkv_y)
    )
    qkv_g_l, skip_g_l, up_x, down_t, qkv_t_1 = together(qkv_g_l, skip_g_l, up_x, down_t, qkv_t_1)
    qkv_t_2 = swap_tensor(qkv_y[width // 6 :])

    def rest(value):
        for stage in stages[3:]:
            value = chips.scatter(value, stage)
        for stage in reversed(stages[3:]):
            value = chips.gather(value, stage)
        return value

    factor = stages[0][1]
    up_rows = up_1.shape[0] // factor
    feed_2 = jnp.concatenate([add(*up_x), add(*down_lx, down_t)], axis=0)
    feed_x = chips.scatter_start(feed_2, stages[1])
    qkv_keep_l, qkv_send_l, qkv_sums_l = project_grad(
        at, after(normed_ext, feed_2), qkv_g_l, out_g_l
    )
    qkv_keep_l, qkv_send_l, qkv_sums_l, feed_x, qkv_t_2 = together(
        qkv_keep_l, qkv_send_l, qkv_sums_l, feed_x, qkv_t_2
    )
    qkv_c_l = chips.swap_core(qkv_send_l)
    feed_3 = add(*feed_x)
    feed_x = chips.scatter_start(feed_3, stages[2])
    qkv_t = jnp.concatenate([qkv_t_1, qkv_t_2], axis=0)

    qkv_1 = add(qkv_keep_l, qkv_c_l, qkv_t)
    qkv_x = chips.scatter_start(qkv_1, stages[0])
    skip_back = swap_tensor(after(skip_g_r, qkv_1))
    input_grad, halo_grad, first_sums = first_back(
        where, at, after(qkv_g_l, qkv_1, feed_3), qkv_g_r, qkv_own, qkv_mine, qkv_theirs,
        block_input.reshape(tokens, width), halo, hidden_grad, row_vectors, rows,
    )
    input_grad, halo_grad, first_sums, qkv_x, feed_x = together(
        input_grad, halo_grad, first_sums, qkv_x, feed_x
    )

    qkv_2 = add(*qkv_x)
    qkv_x = chips.scatter_start(qkv_2, stages[1])
    feed_4 = rest(add(*feed_x))
    feed_x = chips.gather_start(after(feed_4, qkv_2), stages[2])
    own_small, other_small = small_step(
        where, at, middle_sums, after(first_sums, qkv_2, feed_4), qkv_sums_l, qkv_sums_r,
        bias_g_l1, bias_g_l2, bias_g_r1, bias_g_r2,
    )
    small_t = swap_tensor(other_small)
    halo_got = lax.ppermute(after(halo_grad, other_small), "tensor", [(1, 0)])
    skip_grad = skip_grad_of(at, after(skip_g_l, own_small), skip_back, rows)
    skip_grad, qkv_x, small_t = together(skip_grad, qkv_x, small_t)
    qkv_3 = add(*qkv_x)
    qkv_x = chips.scatter_start(qkv_3, stages[2])
    small = own_small + small_t
    small_c = chips.swap_core(small)
    block_output = block_half + after(f_r, small, qkv_3)
    block_output, small_c, feed_x = together(block_output, small_c, feed_x)
    feed_5 = chips.gather_finish(feed_x, stages[2])
    feed_x = chips.gather_start(feed_5, stages[1])
    small = small + small_c
    for stage in stages[3:]:
        small = sum(chips.gather_start(small, stage))
    columns = qkv_2.shape[1]
    small_rows = -(-where.size // (8 * columns)) * 8
    small = jnp.pad(small[0], (0, small_rows * columns - where.size)).reshape(small_rows, columns)
    small, qkv_x = together(after(small, feed_5), qkv_x)

    qkv_4 = jnp.concatenate([rest(add(*qkv_x)), small.astype(BF)], axis=0)
    qkv_x = chips.gather_start(qkv_4, stages[0])
    qkv_x, feed_x = together(qkv_x, feed_x)
    feed_6 = chips.gather_finish(feed_x, stages[1])
    up_6, down_6 = feed_6[:up_rows], feed_6[up_rows:]
    up_x = chips.gather_start(up_6, stages[0])
    qkv_5 = chips.gather_finish(qkv_x, stages[0])
    qkv_x = chips.gather_start(after(qkv_5, up_6), stages[2])
    qkv_x, up_x, down_6 = together(qkv_x, up_x, down_6)
    down_x = chips.gather_start(down_6, stages[0])
    up_7 = chips.gather_finish(up_x, stages[0])
    up_c = chips.swap_core(up_7)
    qkv_6 = chips.gather_finish(qkv_x, stages[2])
    qkv_x = chips.gather_start(after(qkv_6, up_7), stages[1])
    input_grad = add_halo(after(input_grad, qkv_6, up_7), halo_got, rows)
    up_weight_grad = up_out(at, after(up_7, input_grad), up_c)
    up_weight_grad, qkv_x, down_x = together(up_weight_grad, qkv_x, down_x)
    qkv_7 = chips.gather_finish(qkv_x, stages[1])
    qkv_other = chips.swap_core(qkv_7)
    down_7 = chips.gather_finish(down_x, stages[0])
    down_c = chips.swap_core(down_7)
    query_weight_grad, key_weight_grad, value_weight_grad, out_weight_grad, small = project_out(
        at, after(qkv_7, down_7), qkv_other, local, width // 2, factor**3
    )
    query_weight_grad, down_c = together(query_weight_grad, down_c)
    down_weight_grad = down_out(at, down_7, down_c)
    small = small.reshape(-1)

    return (
        block_output.reshape(rows, length, width),
        input_grad.reshape(rows, length, width),
        jnp.swapaxes(skip_grad, 1, 2),
        query_weight_grad,
        small[where.query],
        key_weight_grad,
        value_weight_grad.T,
        small[where.value],
        out_weight_grad,
        small[where.out],
        up_weight_grad,
        small[where.up],
        down_weight_grad,
        small[where.down],
        small[where.gain_1],
        small[where.shift_1],
        small[where.gain_2],
        small[where.shift_2],
    )


def solution(mesh):
    in_specs = (
        P("dp", "tensor", None),
        P("dp", None, "tensor"),
        P("dp", None),
        P("dp"),
        P(None, "tensor"),
        P("tensor"),
        P(None, "tensor"),
        P(None, "tensor"),
        P("tensor"),
        P("tensor", None),
        P(),
        P(None, "tensor"),
        P("tensor"),
        P("tensor", None),
        P(),
        P(),
        P(),
        P(),
        P(),
        P("dp", "tensor", None),
    )
    out_specs = (
        P("dp", "tensor", None),
        P("dp", "tensor", None),
        P("dp", None, "tensor"),
        P(None, "tensor"),
        P("tensor"),
        P(None, "tensor"),
        P(None, "tensor"),
        P("tensor"),
        P("tensor", None),
        P(),
        P(None, "tensor"),
        P("tensor"),
        P("tensor", None),
        P(),
        P(),
        P(),
        P(),
        P(),
    )
    return jax.shard_map(
        functools.partial(on_device, mesh.shape["dp"]),
        mesh=mesh,
        in_specs=in_specs,
        out_specs=out_specs,
        check_vma=False,
    )
```

```python
import functools
import itertools

import jax
import jax.numpy as jnp
from jax import lax
from jax.experimental import pallas as pl
from jax.experimental.pallas import tpu as pltpu
from jax.sharding import PartitionSpec as P

DH = 64
BF = jnp.bfloat16
F32 = jnp.float32
SPAN = 256
QB = 128
WIN = SPAN + QB
TH = 768
RC = 256
NEG = -1000000000.0
COST = pl.CostEstimate(flops=1 << 20, bytes_accessed=1 << 20, transcendentals=0)


def dot_nn(a, b):
    return lax.dot_general(a, b, (((1,), (0,)), ((), ())), preferred_element_type=F32)


def dot_nt(a, b):
    return lax.dot_general(a, b, (((1,), (1,)), ((), ())), preferred_element_type=F32)


def dot_tn(a, b):
    return lax.dot_general(a, b, (((0,), (0,)), ((), ())), preferred_element_type=F32)


def split_pair(block, low_lane):
    zero = jnp.zeros_like(block)
    return jnp.concatenate(
        [jnp.where(low_lane, block, zero), jnp.where(low_lane, zero, block)], axis=0
    )


def window_bias(kseg_ref, qseg_ref, start):
    key_at = lax.broadcasted_iota(jnp.int32, (WIN, QB), 0)
    query_at = lax.broadcasted_iota(jnp.int32, (WIN, QB), 1) + SPAN
    kseg = kseg_ref[0, start : start + WIN, :]
    qseg = qseg_ref[0, :, start : start + QB]
    allowed = ((kseg == qseg) & (key_at <= query_at)) | (key_at == query_at)
    bias = jnp.where(allowed, 0.0, NEG).astype(F32)
    return jnp.concatenate([bias, bias], axis=1)


def pair_values(x_ref, s_ref, t_s, pairs):
    base = 4 * pairs * DH
    for at in range(0, pairs, 2):
        fresh = x_ref[:, base + at * DH : base + at * DH + 128].T
        for pair in range(at, min(at + 2, pairs)):
            t_s[pair, :DH, :] = fresh[(pair - at) * DH : (pair - at + 1) * DH, :]
            t_s[pair, DH:, :] = s_ref[pair * DH : (pair + 1) * DH, :]


def attend_forward_kernel(pairs, x_ref, s_ref, kseg_ref, qseg_ref, o_ref, lse_ref, turned_ref, t_s):
    o_blocks = o_ref.shape[0] // QB
    pair_values(x_ref, s_ref, t_s, pairs)

    low = lax.broadcasted_iota(jnp.int32, (QB, 128), 1) < DH
    for block, pair in itertools.product(range(o_blocks), range(pairs)):
        start = block * QB
        if pair == 0:
            bias = window_bias(kseg_ref, qseg_ref, start)
        win = slice(start, start + WIN)
        rows = slice(start + SPAN, start + SPAN + QB)
        here = slice(start, start + QB)
        cols = slice(pair * 128, pair * 128 + 128)
        key_cols = slice((pairs + pair) * 128, (pairs + pair) * 128 + 128)
        queries = split_pair(x_ref[rows, cols], low)
        scores = dot_nt(x_ref[win, key_cols], queries) + bias
        largest = jnp.max(scores, axis=0, keepdims=True)
        expon = jnp.exp(scores - largest)
        total = jnp.sum(expon, axis=0, keepdims=True)
        probs = (expon * (1.0 / total)).astype(BF)
        out = dot_nn(t_s[pair, :, win], probs)
        out = jnp.concatenate([out[:DH, :QB], out[DH:, QB:]], axis=0)
        turned_ref[cols, here] = out
        o_ref[here, cols] = out.T.astype(BF)
        lse_ref[0, block, pair : pair + 1, :] = largest + jnp.log(total)


def attend_backward_kernel(
    pairs, x_ref, s_ref, kseg_ref, qseg_ref, lse_ref, turned_ref, g_ref, dx_ref, ds_ref,
    v_s, t_s, dk_s, dv_s,
):
    o_blocks = g_ref.shape[0] // QB
    pair_values(x_ref, s_ref, t_s, pairs)
    for pair in range(pairs):
        v_s[pair] = t_s[pair].T
        key_cols = slice((pairs + pair) * 128, (pairs + pair) * 128 + 128)
        t_s[pair] = x_ref[:, key_cols].T
    dk_s[...] = jnp.zeros_like(dk_s)
    dv_s[...] = jnp.zeros_like(dv_s)
    dx_ref[:SPAN, : pairs * 128] = jnp.zeros((SPAN, pairs * 128), BF)

    low = lax.broadcasted_iota(jnp.int32, (QB, 128), 1) < DH
    for block, pair in itertools.product(range(o_blocks), range(pairs)):
        start = block * QB
        if pair == 0:
            bias = window_bias(kseg_ref, qseg_ref, start)
        win = slice(start, start + WIN)
        rows = slice(start + SPAN, start + SPAN + QB)
        here = slice(start, start + QB)
        cols = slice(pair * 128, pair * 128 + 128)
        key_cols = slice((pairs + pair) * 128, (pairs + pair) * 128 + 128)
        queries = split_pair(x_ref[rows, cols], low)
        grads = split_pair(g_ref[here, cols], low)
        scores = dot_nt(x_ref[win, key_cols], queries) + bias
        probs = jnp.exp(scores - lse_ref[0, block, pair : pair + 1, :])
        prob_grad = dot_nt(v_s[pair, win], grads)
        terms = g_ref[here, cols].T.astype(F32) * turned_ref[cols, here]
        row_total = jnp.concatenate([down_rows(terms[:DH]), down_rows(terms[DH:])], axis=1)
        score_grad = (probs * (prob_grad - row_total)).astype(BF)
        dv_s[pair, win] += dot_nn(probs.astype(BF), grads)
        dk_s[pair, win] += dot_nn(score_grad, queries)
        out = dot_nn(t_s[pair, :, win], score_grad)
        out = jnp.concatenate([out[:DH, :QB], out[DH:, QB:]], axis=0)
        dx_ref[rows, cols] = (out.T * (DH**-0.5)).astype(BF)

    base = 4 * pairs * DH
    low_all = lax.broadcasted_iota(jnp.int32, (x_ref.shape[0], 128), 1) < DH
    for pair in range(pairs):
        key_cols = slice((pairs + pair) * 128, (pairs + pair) * 128 + 128)
        dx_ref[:, key_cols] = dk_s[pair].astype(BF)
        ds_ref[pair * DH : (pair + 1) * DH, :] = dv_s[pair].astype(BF).T[DH:, :]
    for at in range(0, pairs, 2):
        second = pltpu.roll(dv_s[at + 1], DH, 1) if at + 1 < pairs else jnp.zeros_like(dv_s[at])
        dx_ref[:, base + at * DH : base + at * DH + 128] = jnp.where(
            low_all, dv_s[at], second
        ).astype(BF)


def attention_specs(rows, blocks, columns, pairs):
    extended = SPAN + blocks * QB
    x_spec = pl.BlockSpec((extended, columns), lambda r: (r, 0))
    s_spec = pl.BlockSpec((pairs * DH, extended), lambda r: (r, 0))
    kseg_spec = pl.BlockSpec((1, extended, 1), lambda r: (r, 0, 0))
    qseg_spec = pl.BlockSpec((1, 1, blocks * QB), lambda r: (r, 0, 0))
    o_spec = pl.BlockSpec((blocks * QB, pairs * 128), lambda r: (r, 0))
    lse_spec = pl.BlockSpec((1, blocks, pairs, 2 * QB), lambda r: (r, 0, 0, 0))
    turned_spec = pl.BlockSpec((pairs * 128, blocks * QB), lambda r: (r, 0))
    return extended, x_spec, s_spec, kseg_spec, qseg_spec, o_spec, lse_spec, turned_spec


def attend_forward(extended_qkv, skip, kseg, qseg):
    rows, blocks, pairs = qseg.shape[0], qseg.shape[2] // QB, skip.shape[0] // DH // qseg.shape[0]
    columns = extended_qkv.shape[1]
    extended, x_spec, s_spec, kseg_spec, qseg_spec, o_spec, lse_spec, turned_spec = attention_specs(
        rows, blocks, columns, pairs
    )
    return pl.pallas_call(
        functools.partial(attend_forward_kernel, pairs),
        grid=(rows,),
        in_specs=[x_spec, s_spec, kseg_spec, qseg_spec],
        out_specs=[o_spec, lse_spec, turned_spec],
        out_shape=[
            jax.ShapeDtypeStruct((rows * blocks * QB, pairs * 128), BF),
            jax.ShapeDtypeStruct((rows, blocks, pairs, 2 * QB), F32),
            jax.ShapeDtypeStruct((rows * pairs * 128, blocks * QB), F32),
        ],
        scratch_shapes=[
            pltpu.VMEM((pairs, 128, extended), BF),
        ],
        cost_estimate=COST,
        name="attend_forward",
    )(extended_qkv, skip, kseg, qseg)


def attend_backward(extended_qkv, skip, kseg, qseg, sums, turned, grads):
    rows, blocks, pairs = qseg.shape[0], qseg.shape[2] // QB, skip.shape[0] // DH // qseg.shape[0]
    columns = extended_qkv.shape[1]
    extended, x_spec, s_spec, kseg_spec, qseg_spec, o_spec, lse_spec, turned_spec = attention_specs(
        rows, blocks, columns, pairs
    )
    return pl.pallas_call(
        functools.partial(attend_backward_kernel, pairs),
        grid=(rows,),
        in_specs=[x_spec, s_spec, kseg_spec, qseg_spec, lse_spec, turned_spec, o_spec],
        out_specs=[x_spec, s_spec],
        out_shape=[
            jax.ShapeDtypeStruct((rows * extended, columns), BF),
            jax.ShapeDtypeStruct((rows * pairs * DH, extended), BF),
        ],
        scratch_shapes=[
            pltpu.VMEM((pairs, extended, 128), BF),
            pltpu.VMEM((pairs, 128, extended), BF),
            pltpu.VMEM((pairs, extended, 128), F32),
            pltpu.VMEM((pairs, extended, 128), F32),
        ],
        cost_estimate=COST,
        name="attend_backward",
    )(extended_qkv, skip, kseg, qseg, sums, turned, grads)


def feed_kernel(
    core_ref,
    n_ref,
    g_ref,
    ua_ref,
    ub_ref,
    ba_ref,
    bb_ref,
    da_ref,
    db_ref,
    wua_ref,
    wub_ref,
    wda_ref,
    wdb_ref,
    ga_ref,
    gb_ref,
    down_ref,
    second_ref,
    turned_s,
    act_s,
    upg_s,
):
    step = pl.program_id(0)
    half = pl.num_programs(0) // 2
    first = step < half

    @pl.when(step == 0)
    def _():
        turned_s[...] = n_ref[...].T
        down_ref[...] = jnp.zeros_like(down_ref)
        second_ref[...] = jnp.zeros_like(second_ref)

    up_tile = jnp.where(first, ua_ref[...], ub_ref[...])
    down_tile = jnp.where(first, da_ref[...], db_ref[...])
    bias = jnp.where(first, ba_ref[...], bb_ref[...])
    root = 0.7978845608028654
    for start in range(0, n_ref.shape[0], RC):
        rows = slice(start, start + RC)
        upward = dot_nn(n_ref[rows, :], up_tile) + bias
        act_grad = dot_nt(g_ref[rows, :], down_tile)
        square = upward * upward
        bent = jnp.tanh(root * upward * (1.0 + 0.044715 * square))
        gate = 0.5 * (1.0 + bent)
        slope = gate + 0.5 * root * upward * (1.0 - bent * bent) * (1.0 + 0.134145 * square)
        act = (upward * gate).astype(BF)
        upg = (act_grad * slope).astype(BF)
        act_s[rows, :] = act
        upg_s[rows, :] = upg
        down_ref[rows, :] += dot_nn(act, down_tile)
        second_ref[rows, :] += dot_nt(upg, up_tile)
    up_weight_grad = dot_nn(turned_s[...], upg_s[...]).astype(BF)
    down_weight_grad = dot_tn(act_s[...], g_ref[...]).astype(BF)
    bias_grad = jnp.sum(upg_s[...].astype(F32), axis=0, keepdims=True)

    @pl.when(first)
    def _():
        wua_ref[...] = up_weight_grad
        wda_ref[...] = down_weight_grad
        ga_ref[...] = bias_grad

    @pl.when(jnp.logical_not(first))
    def _():
        wub_ref[...] = up_weight_grad
        wdb_ref[...] = down_weight_grad
        gb_ref[...] = bias_grad


def feed(at, normed, grads, up_a, up_b, bias, down_a, down_b, whole):
    tokens, width = normed.shape
    piece = up_a.shape[1] // 2 if whole else up_a.shape[1]
    tiles = piece // TH

    def a_at(i, c):
        at = jnp.minimum(i, tiles - 1)
        return at + (1 - c[0]) * tiles if whole else at

    def b_at(i, c):
        at = jnp.maximum(i - tiles, 0)
        return at + c[0] * tiles if whole else at

    def out_a(i, c):
        return jnp.minimum(i, tiles - 1)

    def out_b(i, c):
        return jnp.maximum(i - tiles, 0)

    resident = pl.BlockSpec((tokens, width), lambda i, c: (0, 0))
    once = pl.BlockSpec((tokens, width), lambda i, c: (0, 0))
    in_specs = [
        resident,
        resident,
        pl.BlockSpec((width, TH), lambda i, c: (0, a_at(i, c))),
        pl.BlockSpec((width, TH), lambda i, c: (0, b_at(i, c))),
        pl.BlockSpec((1, TH), lambda i, c: (0, out_a(i, c) + (1 - c[0]) * tiles)),
        pl.BlockSpec((1, TH), lambda i, c: (0, out_b(i, c) + c[0] * tiles)),
        pl.BlockSpec((TH, width), lambda i, c: (a_at(i, c), 0)),
        pl.BlockSpec((TH, width), lambda i, c: (b_at(i, c), 0)),
    ]
    out_specs = [
        pl.BlockSpec((width, TH), lambda i, c: (0, out_a(i, c))),
        pl.BlockSpec((width, TH), lambda i, c: (0, out_b(i, c))),
        pl.BlockSpec((TH, width), lambda i, c: (out_a(i, c), 0)),
        pl.BlockSpec((TH, width), lambda i, c: (out_b(i, c), 0)),
        pl.BlockSpec((1, TH), lambda i, c: (0, out_a(i, c))),
        pl.BlockSpec((1, TH), lambda i, c: (0, out_b(i, c))),
        once,
        once,
    ]
    out_shape = [
        jax.ShapeDtypeStruct((width, piece), BF),
        jax.ShapeDtypeStruct((width, piece), BF),
        jax.ShapeDtypeStruct((piece, width), BF),
        jax.ShapeDtypeStruct((piece, width), BF),
        jax.ShapeDtypeStruct((1, piece), F32),
        jax.ShapeDtypeStruct((1, piece), F32),
        jax.ShapeDtypeStruct((tokens, width), F32),
        jax.ShapeDtypeStruct((tokens, width), F32),
    ]
    return pl.pallas_call(
        feed_kernel,
        grid_spec=pltpu.PrefetchScalarGridSpec(
            num_scalar_prefetch=1,
            grid=(2 * tiles,),
            in_specs=in_specs,
            out_specs=out_specs,
            scratch_shapes=[
                pltpu.VMEM((width, tokens), BF),
                pltpu.VMEM((tokens, TH), BF),
                pltpu.VMEM((tokens, TH), BF),
            ],
        ),
        out_shape=out_shape,
        compiler_params=pltpu.CompilerParams(vmem_limit_bytes=56 << 20),
        cost_estimate=COST,
        name="feed",
    )(at, normed, grads, up_a, up_b, bias, bias, down_a, down_b)


def norm_rows(values, gain_row, shift_row):
    center = values - jnp.mean(values, axis=-1, keepdims=True)
    variance = jnp.mean(center * center, axis=-1, keepdims=True)
    return center * lax.rsqrt(variance + 1e-05) * gain_row + shift_row


def whole_spec(value):
    zeros = (0,) * value.ndim
    return pl.BlockSpec(value.shape, lambda *_: zeros)


def open_kernel(
    at_ref, qw_ref, kw_ref, vw_ref, x_ref, s_ref, w_ref, w_send_ref, halo_ref, s_send_ref, s_own_ref
):
    side = at_ref[1]
    rows, length, width = x_ref.shape
    local, half = qw_ref.shape[1], vw_ref.shape[0]
    depth = w_send_ref.shape[0]
    cut = pl.ds(pl.multiple_of(at_ref[0] * depth, depth), depth)
    w_ref[:, :local] = qw_ref[...]
    w_ref[:, local : 2 * local] = kw_ref[...]
    w_ref[:, 2 * local : 2 * local + half] = vw_ref[...].T
    w_ref[:, 2 * local + half :] = jnp.zeros((width, w_ref.shape[1] - 2 * local - half), BF)
    w_send_ref[...] = w_ref[cut, :]
    own = pl.ds(pl.multiple_of(side * length, length), length)
    other = pl.ds(pl.multiple_of((1 - side) * length, length), length)
    for row in range(rows):
        halo_ref[row * SPAN : (row + 1) * SPAN, :] = x_ref[row, length - SPAN :, :]
        lines = slice(row * half, (row + 1) * half)
        middle = s_ref[row, :, length - SPAN : length]
        s_send_ref[lines, :SPAN] = middle
        s_own_ref[lines, :SPAN] = middle
        s_send_ref[lines, SPAN:] = s_ref[row, :, other]
        s_own_ref[lines, SPAN:] = s_ref[row, :, own]


def open_step(at, qw, kw, vw, x, skip):
    rows, length, width = x.shape
    local, half = qw.shape[1], vw.shape[0]
    columns = -(-(2 * local + half) // 256) * 256
    shapes = [
        (width, columns),
        (width // 2, columns),
        (rows * SPAN, width),
        (rows * half, SPAN + length),
        (rows * half, SPAN + length),
    ]
    return pl.pallas_call(
        open_kernel,
        grid_spec=pltpu.PrefetchScalarGridSpec(
            num_scalar_prefetch=1,
            grid=(1,),
            in_specs=[whole_spec(v) for v in (qw, kw, vw, x, skip)],
            out_specs=[pl.BlockSpec(shape, lambda *_: (0, 0)) for shape in shapes],
        ),
        out_shape=[jax.ShapeDtypeStruct(shape, BF) for shape in shapes],
        cost_estimate=COST,
        name="open",
    )(at, qw, kw, vw, x, skip)


class Rows:
    def __init__(self, width, local, hidden):
        half = local // 2
        self.up = slice(0, hidden)
        self.query = slice(hidden, hidden + local)
        self.value = slice(hidden + local, hidden + local + half)
        start = -(-self.value.stop // 128) * 128
        self.pad = start - self.value.stop
        self.gain_1, self.shift_1, self.gain_2, self.shift_2, self.out, self.down = (
            slice(start + n * width, start + (n + 1) * width) for n in range(6)
        )
        self.size = start + 6 * width


def store_projection(o_ref, values, q_bias, v_bias):
    local, half = q_bias.shape[1], v_bias.shape[1]
    o_ref[:, :local] = ((values[:, :local] + q_bias) * (DH**-0.5)).astype(BF)
    o_ref[:, local : 2 * local] = values[:, local : 2 * local].astype(BF)
    stop = 2 * local + half
    o_ref[:, 2 * local : stop] = (values[:, 2 * local : stop] + v_bias).astype(BF)
    o_ref[:, stop:] = values[:, stop:].astype(BF)


def project_own_kernel(where, n_ref, h_ref, rows_ref, w_ref, ne_ref, o_ref):
    ne_ref[:SPAN, :] = norm_rows(
        h_ref[...].astype(F32), rows_ref[:, where.gain_1], rows_ref[:, where.shift_1]
    ).astype(BF)
    ne_ref[SPAN:, :] = n_ref[...]
    store_projection(
        o_ref, dot_nn(ne_ref[...], w_ref[...]), rows_ref[:, where.query], rows_ref[:, where.value]
    )


def project_own(where, normed, halo, row_vectors, weight, rows):
    width, columns = weight.shape
    length = normed.shape[0] // rows
    size = SPAN + length
    row = lambda count, cols: pl.BlockSpec((count, cols), lambda r: (r, 0))
    return pl.pallas_call(
        functools.partial(project_own_kernel, where),
        grid=(rows,),
        in_specs=[row(length, width), row(SPAN, width), whole_spec(row_vectors), whole_spec(weight)],
        out_specs=[row(size, width), row(size, columns)],
        out_shape=[
            jax.ShapeDtypeStruct((rows * size, width), BF),
            jax.ShapeDtypeStruct((rows * size, columns), BF),
        ],
        cost_estimate=COST,
        name="project_own",
    )(normed, halo, row_vectors, weight)


def join_cores(at_ref, mine_ref, other_ref, scratch):
    depth = mine_ref.shape[0]
    core = at_ref[0]
    scratch[pl.ds(pl.multiple_of(core * depth, depth), depth), :] = mine_ref[...]
    scratch[pl.ds(pl.multiple_of((1 - core) * depth, depth), depth), :] = other_ref[...]


def project_other_kernel(where, at_ref, ne_ref, mine_ref, other_ref, rows_ref, o_ref, w_s):
    @pl.when(pl.program_id(0) == 0)
    def _():
        join_cores(at_ref, mine_ref, other_ref, w_s)

    store_projection(
        o_ref, dot_nn(ne_ref[...], w_s[...]), rows_ref[:, where.query], rows_ref[:, where.value]
    )


def project_other(where, at, normed_ext, mine, other, row_vectors, rows):
    size, width = normed_ext.shape
    step = size // rows
    columns = mine.shape[1]
    return pl.pallas_call(
        functools.partial(project_other_kernel, where),
        grid_spec=pltpu.PrefetchScalarGridSpec(
            num_scalar_prefetch=1,
            grid=(rows,),
            in_specs=[
                pl.BlockSpec((step, width), lambda i, a: (i, 0)),
                *[whole_spec(v) for v in (mine, other, row_vectors)],
            ],
            out_specs=pl.BlockSpec((step, columns), lambda i, a: (i, 0)),
            scratch_shapes=[pltpu.VMEM((width, columns), BF)],
        ),
        out_shape=jax.ShapeDtypeStruct((size, columns), BF),
        cost_estimate=COST,
        name="project_other",
    )(at, normed_ext, mine, other, row_vectors)


def middle_kernel(
    where, at_ref, ml_ref, mr_ref, wl_ref, w1_ref, w2_ref, x_ref, rows_ref, hidden_ref, n_ref, wr_ref
):
    @pl.when(pl.program_id(0) == 0)
    def _():
        join_cores(at_ref, w1_ref, w2_ref, wr_ref)

    values = dot_nn(ml_ref[...], wl_ref[...]) + dot_nn(mr_ref[...], wr_ref[...])
    hidden = x_ref[...].astype(F32) + (values + rows_ref[:, where.out])
    hidden_ref[...] = hidden
    n_ref[...] = norm_rows(hidden, rows_ref[:, where.gain_2], rows_ref[:, where.shift_2]).astype(BF)


def middle(where, at, mixed_l, mixed_r, own, mine, other, x, row_vectors):
    tokens, width = x.shape
    local = mixed_l.shape[1]
    tile = lambda columns: pl.BlockSpec((RC, columns), lambda i, a: (i, 0))
    return pl.pallas_call(
        functools.partial(middle_kernel, where),
        grid_spec=pltpu.PrefetchScalarGridSpec(
            num_scalar_prefetch=1,
            grid=(tokens // RC,),
            in_specs=[
                tile(local), tile(local), *[whole_spec(v) for v in (own, mine, other)],
                tile(width), whole_spec(row_vectors),
            ],
            out_specs=[tile(width), tile(width), whole_spec(own)],
        ),
        out_shape=[
            jax.ShapeDtypeStruct((tokens, width), F32),
            jax.ShapeDtypeStruct((tokens, width), BF),
            jax.ShapeDtypeStruct(own.shape, BF),
        ],
        cost_estimate=COST,
        name="middle",
    )(at, mixed_l, mixed_r, own, mine, other, x, row_vectors)


def norm_pull(values, grad, gain_row):
    center = values - jnp.mean(values, axis=-1, keepdims=True)
    variance = jnp.mean(center * center, axis=-1, keepdims=True)
    rstd = lax.rsqrt(variance + 1e-05)
    unit = center * rstd
    scaled = grad * gain_row
    back = rstd * (
        scaled
        - jnp.mean(scaled, axis=-1, keepdims=True)
        - unit * jnp.mean(scaled * unit, axis=-1, keepdims=True)
    )
    return back, grad * unit


def down_rows(values):
    return jnp.sum(values, axis=0, keepdims=True)


def middle_back_kernel(
    where, bl_ref, br_ref, hidden_ref, g_ref, ml_ref, mr_ref, wl_ref, wr_ref, rows_ref,
    hg_ref, gl_ref, gr_ref, ol_ref, or_ref, sums_ref, acc_l, acc_r,
):
    step = pl.program_id(0)

    @pl.when(step == 0)
    def _():
        acc_l[...] = jnp.zeros_like(acc_l)
        acc_r[...] = jnp.zeros_like(acc_r)
        sums_ref[...] = jnp.zeros_like(sums_ref)

    grad = bl_ref[...] + br_ref[...]
    back, gain_term = norm_pull(hidden_ref[...], grad, rows_ref[:, where.gain_2])
    cot = g_ref[...].astype(F32)
    hidden_grad = cot + back
    low = hidden_grad.astype(BF)
    hg_ref[...] = hidden_grad
    gl_ref[...] = dot_nt(low, wl_ref[...]).astype(BF)
    gr_ref[...] = dot_nt(low, wr_ref[...]).astype(BF)
    turned = low.T
    acc_l[...] += dot_nn(turned, ml_ref[...])
    acc_r[...] += dot_nn(turned, mr_ref[...])
    for at, term in enumerate((low.astype(F32), cot, gain_term, grad)):
        sums_ref[at : at + 1, :] += down_rows(term)

    @pl.when(step == pl.num_programs(0) - 1)
    def _():
        ol_ref[...] = acc_l[...].astype(BF)
        or_ref[...] = acc_r[...].astype(BF)


def middle_back(where, back_l, back_r, hidden, grads, mixed_l, mixed_r, own, other, row_vectors):
    tokens, width = hidden.shape
    local = mixed_l.shape[1]
    tile = lambda columns: pl.BlockSpec((RC, columns), lambda i: (i, 0))
    fixed = lambda rows, columns: pl.BlockSpec((rows, columns), lambda i: (0, 0))
    return pl.pallas_call(
        functools.partial(middle_back_kernel, where),
        grid=(tokens // RC,),
        in_specs=[
            tile(width), tile(width), tile(width), tile(width), tile(local), tile(local),
            whole_spec(own), whole_spec(other), whole_spec(row_vectors),
        ],
        out_specs=[
            tile(width), tile(local), tile(local),
            fixed(width, local), fixed(width, local), fixed(8, width),
        ],
        scratch_shapes=[pltpu.VMEM((width, local), F32), pltpu.VMEM((width, local), F32)],
        out_shape=[
            jax.ShapeDtypeStruct((tokens, width), F32),
            jax.ShapeDtypeStruct((tokens, local), BF),
            jax.ShapeDtypeStruct((tokens, local), BF),
            jax.ShapeDtypeStruct((width, local), BF),
            jax.ShapeDtypeStruct((width, local), BF),
            jax.ShapeDtypeStruct((8, width), F32),
        ],
        cost_estimate=COST,
        name="middle_back",
    )(back_l, back_r, hidden, grads, mixed_l, mixed_r, own, other, row_vectors)


def project_grad_kernel(at_ref, n_ref, d_ref, w_ref, keep_ref, send_ref, sum_ref):
    values = dot_tn(n_ref[...], d_ref[...]).astype(BF)
    columns = d_ref.shape[1]

    @pl.when(pl.program_id(0) == 0)
    def _():
        send_ref[:, :columns] = values
        send_ref[:, columns:] = w_ref[...]
        sum_ref[...] = down_rows(d_ref[...].astype(F32))

    @pl.when(pl.program_id(0) == 1)
    def _():
        keep_ref[:, :columns] = values
        keep_ref[:, columns:] = w_ref[...]


def project_grad(at, normed_ext, grads, out_grad):
    size, width = normed_ext.shape
    columns, more = grads.shape[1], out_grad.shape[1]
    fixed = pl.BlockSpec((width // 2, columns + more), lambda i, a: (0, 0))
    half = lambda i, a: i * a[0] + (1 - i) * (1 - a[0])
    return pl.pallas_call(
        project_grad_kernel,
        grid_spec=pltpu.PrefetchScalarGridSpec(
            num_scalar_prefetch=1,
            grid=(2,),
            in_specs=[
                pl.BlockSpec((size, width // 2), lambda i, a: (0, half(i, a))),
                whole_spec(grads),
                pl.BlockSpec((width // 2, more), lambda i, a: (half(i, a), 0)),
            ],
            out_specs=[fixed, fixed, pl.BlockSpec((1, columns), lambda i, a: (0, 0))],
        ),
        out_shape=[
            jax.ShapeDtypeStruct((width // 2, columns + more), BF),
            jax.ShapeDtypeStruct((width // 2, columns + more), BF),
            jax.ShapeDtypeStruct((1, columns), F32),
        ],
        cost_estimate=COST,
        name="project_grad",
    )(at, normed_ext, grads, out_grad)


def first_back_kernel(
    where, at_ref, dl_ref, dr_ref, wl_ref, mine_ref, other_ref, x_ref, h_ref, hg_ref, rows_ref,
    ig_ref, ih_ref, sums_ref, w_s,
):
    block = pl.program_id(1)

    @pl.when((pl.program_id(0) == 0) & (block == 0))
    def _():
        join_cores(at_ref, mine_ref, other_ref, w_s)
        sums_ref[...] = jnp.zeros_like(sums_ref)

    grad = dot_nt(dl_ref[...], wl_ref[...]) + dot_nt(dr_ref[...], w_s[...])
    values = jnp.where(block == 0, h_ref[...], x_ref[...]).astype(F32)
    back, gain_term = norm_pull(values, grad, rows_ref[:, where.gain_1])
    sums_ref[0:1, :] += down_rows(gain_term)
    sums_ref[1:2, :] += down_rows(grad)

    @pl.when(block == 0)
    def _():
        ih_ref[...] = back.astype(BF)

    @pl.when(block > 0)
    def _():
        ig_ref[...] = hg_ref[...] + back


def first_back(where, at, grads_l, grads_r, own, mine, other, x, halo, hidden_grad, row_vectors, rows):
    tokens, width = x.shape
    columns = grads_l.shape[1]
    blocks = tokens // SPAN // rows
    extended = pl.BlockSpec((SPAN, columns), lambda r, j, a: (r * (blocks + 1) + j, 0))
    inner = pl.BlockSpec((SPAN, width), lambda r, j, a: (r * blocks + jnp.maximum(j - 1, 0), 0))
    outer = pl.BlockSpec((SPAN, width), lambda r, j, a: (r, 0))
    return pl.pallas_call(
        functools.partial(first_back_kernel, where),
        grid_spec=pltpu.PrefetchScalarGridSpec(
            num_scalar_prefetch=1,
            grid=(rows, blocks + 1),
            in_specs=[
                extended, extended, *[whole_spec(v) for v in (own, mine, other)],
                inner, outer, inner, whole_spec(row_vectors),
            ],
            out_specs=[inner, outer, pl.BlockSpec((8, width), lambda r, j, a: (0, 0))],
            scratch_shapes=[pltpu.VMEM((width, columns), BF)],
        ),
        out_shape=[
            jax.ShapeDtypeStruct((tokens, width), F32),
            jax.ShapeDtypeStruct((rows * SPAN, width), BF),
            jax.ShapeDtypeStruct((8, width), F32),
        ],
        cost_estimate=COST,
        name="first_back",
    )(at, grads_l, grads_r, own, mine, other, x, halo, hidden_grad, row_vectors)


def add_halo_kernel(ig_ref, got_ref, o_ref):
    o_ref[...] = ig_ref[...] + got_ref[...].astype(F32)


def add_halo(input_grad, got, rows):
    width = got.shape[1]
    blocks = input_grad.shape[0] // SPAN // rows
    last = pl.BlockSpec((SPAN, width), lambda r: (r * blocks + blocks - 1, 0))
    return pl.pallas_call(
        add_halo_kernel,
        grid=(rows,),
        in_specs=[last, pl.BlockSpec((SPAN, width), lambda r: (r, 0))],
        out_specs=last,
        out_shape=jax.ShapeDtypeStruct(input_grad.shape, F32),
        input_output_aliases={0: 0},
        cost_estimate=COST,
        name="add_halo",
    )(input_grad, got)


def skip_grad_kernel(at_ref, mine_ref, got_ref, o_ref):
    side = at_ref[1]
    rows, half, total = o_ref.shape
    length = total // 2
    own = pl.ds(pl.multiple_of(side * length, length), length)
    other = pl.ds(pl.multiple_of((1 - side) * length, length), length)
    for row in range(rows):
        lines = slice(row * half, (row + 1) * half)
        o_ref[row, :, own] = mine_ref[lines, SPAN:].astype(F32)
        o_ref[row, :, other] = got_ref[lines, SPAN:].astype(F32)
        o_ref[row, :, length - SPAN : length] += mine_ref[lines, :SPAN].astype(F32) + got_ref[
            lines, :SPAN
        ].astype(F32)


def skip_grad_of(at, mine, got, rows):
    lines, size = mine.shape
    shape = (rows, lines // rows, 2 * (size - SPAN))
    return pl.pallas_call(
        skip_grad_kernel,
        grid_spec=pltpu.PrefetchScalarGridSpec(
            num_scalar_prefetch=1,
            grid=(1,),
            in_specs=[whole_spec(mine), whole_spec(got)],
            out_specs=pl.BlockSpec(shape, lambda i, a: (0, 0, 0)),
        ),
        out_shape=jax.ShapeDtypeStruct(shape, F32),
        cost_estimate=COST,
        name="skip_grad",
    )(at, mine, got)


def small_kernel(where, at_ref, m_ref, f_ref, ql_ref, qr_ref, l1_ref, l2_ref, r1_ref, r2_ref, own_ref, other_ref):
    core = at_ref[0]
    local = where.query.stop - where.query.start
    half = where.value.stop - where.value.start
    piece = l1_ref.shape[1]
    for o_ref, q_ref, one_ref, two_ref in (
        (own_ref, ql_ref, l1_ref, l2_ref), (other_ref, qr_ref, r1_ref, r2_ref)
    ):
        o_ref[...] = jnp.zeros_like(o_ref)
        o_ref[:, pl.ds(pl.multiple_of(core * piece, 128), piece)] = one_ref[...]
        o_ref[:, pl.ds(pl.multiple_of((1 - core) * piece, 128), piece)] = two_ref[...]
        o_ref[:, where.query] = q_ref[:, :local]
        o_ref[:, where.value] = q_ref[:, 2 * local : 2 * local + half]
        o_ref[:, where.out] = m_ref[0:1, :]
        o_ref[:, where.down] = m_ref[1:2, :]
        o_ref[:, where.gain_2] = m_ref[2:3, :]
        o_ref[:, where.shift_2] = m_ref[3:4, :]
        o_ref[:, where.gain_1] = f_ref[0:1, :]
        o_ref[:, where.shift_1] = f_ref[1:2, :]


def small_step(where, at, *values):
    return pl.pallas_call(
        functools.partial(small_kernel, where),
        grid_spec=pltpu.PrefetchScalarGridSpec(
            num_scalar_prefetch=1,
            grid=(1,),
            in_specs=[whole_spec(v) for v in values],
            out_specs=[pl.BlockSpec((1, where.size), lambda i, a: (0, 0))] * 2,
        ),
        out_shape=[jax.ShapeDtypeStruct((1, where.size), F32)] * 2,
        cost_estimate=COST,
        name="small",
    )(at, *values)


def down_out_kernel(at_ref, mine_ref, other_ref, o_ref):
    is_mine = pl.program_id(0) // 2 == at_ref[0]
    o_ref[...] = jnp.where(is_mine, mine_ref[...], other_ref[...]).astype(F32)


def down_out(at, mine, other):
    rows, width = mine.shape
    block = pl.BlockSpec((rows // 2, width), lambda i, a: (i % 2, 0))
    return pl.pallas_call(
        down_out_kernel,
        grid_spec=pltpu.PrefetchScalarGridSpec(
            num_scalar_prefetch=1,
            grid=(4,),
            in_specs=[block, block],
            out_specs=pl.BlockSpec((rows // 2, width), lambda i, a: (i, 0)),
        ),
        out_shape=jax.ShapeDtypeStruct((2 * rows, width), F32),
        cost_estimate=COST,
        name="down_out",
    )(at, mine, other)


def up_out_kernel(at_ref, mine_ref, other_ref, o_ref):
    core = at_ref[0]
    piece = mine_ref.shape[1]
    for ref, at in ((mine_ref, core), (other_ref, 1 - core)):
        o_ref[:, pl.ds(pl.multiple_of(at * piece, 128), piece)] = ref[...].astype(F32)


def up_out(at, mine, other):
    rows, width = mine.shape
    block = pl.BlockSpec((rows // 4, width), lambda i, a: (i, 0))
    return pl.pallas_call(
        up_out_kernel,
        grid_spec=pltpu.PrefetchScalarGridSpec(
            num_scalar_prefetch=1,
            grid=(4,),
            in_specs=[block, block],
            out_specs=pl.BlockSpec((rows // 4, 2 * width), lambda i, a: (i, 0)),
        ),
        out_shape=jax.ShapeDtypeStruct((rows, 2 * width), F32),
        cost_estimate=COST,
        name="up_out",
    )(at, mine, other)


def project_out_kernel(blocks, at_ref, mine_ref, other_ref, q_ref, k_ref, v_ref, out_ref, small_ref):
    core = at_ref[0]
    local = q_ref.shape[1]
    depth = q_ref.shape[0] // 2
    count = depth // blocks
    step = mine_ref.shape[0] // blocks
    columns = mine_ref.shape[1] - local
    for ref, at in ((mine_ref, core), (other_ref, 1 - core)):
        start = pl.multiple_of(at * depth, depth)
        places = [(n % (blocks // 2)) * 2 + n // (blocks // 2) for n in range(blocks)]
        parts = [ref[n * step : n * step + count, :].astype(F32) for n in places]
        values = jnp.concatenate(parts, axis=0)
        rows = pl.ds(start, depth)
        q_ref[rows, :] = values[:, :local]
        k_ref[rows, :] = values[:, local : 2 * local]
        v_ref[:, rows] = values[:, 2 * local : 2 * local + v_ref.shape[0]].T
        out_ref[:, rows] = values[:, columns:].T
    small_ref[...] = sum(
        mine_ref[n * step + count : (n + 1) * step, :].astype(F32) for n in range(blocks)
    )


def project_out(at, mine, other, local, depth, blocks):
    columns = mine.shape[1]
    rest = (mine.shape[0] - depth) // blocks
    shapes = [
        (2 * depth, local), (2 * depth, local), (local // 2, 2 * depth), (local, 2 * depth),
        (rest, columns),
    ]
    return pl.pallas_call(
        functools.partial(project_out_kernel, blocks),
        grid_spec=pltpu.PrefetchScalarGridSpec(
            num_scalar_prefetch=1,
            grid=(1,),
            in_specs=[whole_spec(mine), whole_spec(other)],
            out_specs=[pl.BlockSpec(s, lambda i, a: (0, 0)) for s in shapes],
        ),
        out_shape=[jax.ShapeDtypeStruct(s, F32) for s in shapes],
        cost_estimate=COST,
        name="project_out",
    )(at, mine, other)


def after(value, *others):
    return lax.optimization_barrier((value, *others))[0]


def together(*values):
    return lax.optimization_barrier(values)


class Chips:
    def __init__(self, count):
        self.count = count
        self.factors = [2] * ((count // 2).bit_length() - 1)
        self.index = lax.axis_index("dp")
        self.core = self.index % 2

    def flip(self, value, bit):
        return lax.ppermute(value, "dp", [(i, i ^ bit) for i in range(self.count)])

    def swap_core(self, value):
        return self.flip(value, 1)

    def shift(self, value, stride, factor, by):
        perm = []
        for i in range(self.count):
            digit = (i // stride) % factor
            perm.append((i, i + (((digit + by) % factor) - digit) * stride))
        return lax.ppermute(value, "dp", perm)

    def stages(self):
        stride = 2
        for factor in self.factors:
            yield stride, factor, (self.index // stride) % factor
            stride *= factor

    def scatter_start(self, value, stage):
        stride, factor, digit = stage
        rows = value.shape[0] // factor
        parts = [lax.dynamic_slice_in_dim(value, digit * rows, rows, 0)]
        for by in range(1, factor):
            part = lax.dynamic_slice_in_dim(value, ((digit + by) % factor) * rows, rows, 0)
            parts.append(self.shift(part, stride, factor, by))
        return tuple(parts)

    def scatter(self, value, stage):
        return add(*self.scatter_start(value, stage))

    def gather_start(self, value, stage):
        stride, factor, digit = stage
        return (value, *(self.shift(value, stride, factor, by) for by in range(1, factor)))

    def gather(self, value, stage):
        return self.gather_finish(self.gather_start(value, stage), stage)

    def gather_finish(self, parts, stage):
        stride, factor, digit = stage
        return jnp.concatenate(
            [
                lax.select_n((digit - at) % factor, *parts)
                if factor > 2
                else jnp.where(digit == at, parts[0], parts[1])
                for at in range(factor)
            ],
            axis=0,
        )

    def sum_small(self, value):
        value = value + self.swap_core(value)
        for stride, factor, digit in self.stages():
            total = value
            for by in range(1, factor):
                total = total + self.shift(value, stride, factor, by)
            value = total
        return value


def swap_tensor(value):
    return lax.ppermute(value, "tensor", [(0, 1), (1, 0)])


def block_of(value, at, count, axis):
    size = value.shape[axis] // count
    return lax.dynamic_slice_in_dim(value, at * size, size, axis)


def in_order(bit, mine, other, axis):
    return jnp.concatenate(
        [jnp.where(bit == 0, mine, other), jnp.where(bit == 0, other, mine)], axis=axis
    )


def add(*values):
    total = values[0].astype(F32)
    for value in values[1:]:
        total = total + value.astype(F32)
    return total.astype(BF)


def on_device(
    dp_count,
    block_input,
    skip_values,
    segment_ids,
    row_fill,
    query_weight,
    query_bias,
    key_weight,
    value_weight,
    value_bias,
    out_weight,
    out_bias,
    up_weight,
    up_bias,
    down_weight,
    down_bias,
    first_gain,
    first_shift,
    second_gain,
    second_shift,
    cotangent,
):
    chips = Chips(dp_count)
    core = chips.core
    side = lax.axis_index("tensor")
    at = jnp.stack([core, side]).astype(jnp.int32)
    rows, length, width = block_input.shape
    tokens = rows * length
    local = query_weight.shape[1]
    local_half = local // 2
    hidden_local = up_weight.shape[1]
    piece = hidden_local // 2
    stages = list(chips.stages())
    where = Rows(width, local, hidden_local)

    out_mine = swap_tensor(block_of(out_weight, core, 2, 0))
    qkv_own, qkv_send, halo_send, skip_send, skip_own = open_step(
        at, query_weight, key_weight, value_weight.T, block_input, jnp.swapaxes(skip_values, 1, 2)
    )
    halo = lax.ppermute(halo_send, "tensor", [(0, 1)])
    row_vectors = jnp.concatenate(
        [
            up_bias, query_bias, value_bias, jnp.zeros((where.pad,), F32),
            first_gain, first_shift, second_gain, second_shift, out_bias, down_bias,
        ]
    ).reshape(1, -1)
    normed = norm_rows(
        after(block_input, halo_send).astype(F32), first_gain, first_shift
    ).astype(BF).reshape(tokens, width)

    position = jnp.arange(segment_ids.shape[1], dtype=jnp.int32)
    usable = jnp.where(position[None] < row_fill[:, None], segment_ids, -1)
    query_seg = lax.dynamic_slice_in_dim(segment_ids, side * length, length, 1)
    key_seg = jnp.concatenate(
        [
            jnp.where(side == 0, -1, usable[:, length - SPAN : length]),
            lax.dynamic_slice_in_dim(usable, side * length, length, 1),
        ],
        axis=1,
    )
    query_seg = query_seg.reshape(rows, 1, length)
    key_seg = key_seg.reshape(rows, SPAN + length, 1)

    down_piece = block_of(down_weight, core, 2, 0)
    up_piece = block_of(up_weight, core, 2, 1)
    key_seg, query_seg, normed, row_vectors, qkv_send, out_mine, down_piece, up_piece = together(
        key_seg, query_seg, normed, row_vectors, qkv_send, out_mine, down_piece, up_piece
    )
    out_theirs = chips.swap_core(out_mine)
    qkv_mine = swap_tensor(qkv_send)
    rows_other = swap_tensor(after(row_vectors, qkv_send))

    normed_ext, qkv_l = project_own(where, normed, halo, row_vectors, qkv_own, rows)
    lines = skip_send.shape[0] // 2
    qkv_l, skip_send_1, skip_send_2, out_theirs = together(
        qkv_l, skip_send[:lines], skip_send[lines:], out_theirs
    )
    skip_got_1 = swap_tensor(skip_send_1)
    mixed_l, sums_l, turned_l = attend_forward(qkv_l, skip_own, key_seg, query_seg)
    mixed_l, skip_got_1, qkv_mine, rows_other, skip_send_2 = together(
        mixed_l, skip_got_1, qkv_mine, rows_other, skip_send_2
    )
    skip_got_2 = swap_tensor(skip_send_2)
    qkv_theirs = chips.swap_core(qkv_mine)
    qkv_r = project_other(
        where, at, after(normed_ext, mixed_l), qkv_mine, qkv_theirs, rows_other, rows
    )
    qkv_r, skip_got_2, down_piece, up_piece = together(qkv_r, skip_got_2, down_piece, up_piece)
    down_r1 = swap_tensor(down_piece)
    up_r1 = swap_tensor(after(up_piece, down_piece))
    skip_got = jnp.concatenate([skip_got_1, skip_got_2], axis=0)
    mixed_r, sums_r, turned_r = attend_forward(qkv_r, skip_got, key_seg, query_seg)
    hidden, normed_two, out_other = middle(
        where, at, mixed_l, mixed_r, out_weight, out_mine, out_theirs,
        block_input.reshape(tokens, width), row_vectors,
    )

    out_grad = cotangent.reshape(tokens, width)
    (up_g_l2, up_g_l1, down_g_l2, down_g_l1, bias_g_l2, bias_g_l1, f_l, b_l) = feed(
        at, normed_two, out_grad, up_weight, up_weight, row_vectors, down_weight, down_weight, True,
    )
    b_l, up_g_l2, down_g_l2, down_r1, up_r1 = together(b_l, up_g_l2, down_g_l2, down_r1, up_r1)
    down_r2 = chips.swap_core(down_r1)
    up_r2 = chips.swap_core(up_r1)
    block_half = hidden + (after(f_l, b_l) + down_bias)
    block_half, up_r2, down_r2, up_g_l2, down_g_l2 = together(
        block_half, up_r2, down_r2, up_g_l2, down_g_l2
    )
    up_c_l, down_c_l = chips.swap_core(up_g_l2), chips.swap_core(down_g_l2)
    (up_g_r2, up_g_r1, down_g_r2, down_g_r1, bias_g_r2, bias_g_r1, f_r, b_r) = feed(
        at, after(normed_two, block_half), out_grad, up_r2, up_r1, rows_other, down_r2, down_r1, False
    )
    up_g_r2, up_g_r1, down_g_r2, down_g_r1, b_r, up_c_l, down_c_l = together(
        up_g_r2, up_g_r1, down_g_r2, down_g_r1, b_r, up_c_l, down_c_l
    )

    up_c_r, down_c_r = chips.swap_core(up_g_r2), chips.swap_core(down_g_r2)
    up_l, down_l = add(up_g_l1, up_c_l), add(down_g_l1, down_c_l)
    down_lx = chips.scatter_start(down_l, stages[0])
    up_c_r, down_c_r, up_l, down_l = together(up_c_r, down_c_r, up_l, down_l)
    up_sum_r, down_sum_r = add(up_g_r1, up_c_r), add(down_g_r1, down_c_r)
    up_t = swap_tensor(up_sum_r)
    down_rx = chips.scatter_start(down_sum_r, stages[0])
    hidden_grad, mixed_g_l, mixed_g_r, out_g_l, out_g_r, middle_sums = middle_back(
        where, b_l, after(b_r, up_sum_r, down_sum_r), hidden, out_grad, mixed_l, mixed_r,
        out_weight, out_other, row_vectors,
    )
    mixed_g_r, down_lx = together(mixed_g_r, down_lx)
    qkv_g_r, skip_g_r = attend_backward(
        qkv_r, skip_got, key_seg, query_seg, sums_r, turned_r, mixed_g_r
    )
    qkv_g_r, skip_g_r, down_rx = together(qkv_g_r, skip_g_r, down_rx)

    down_y = add(*down_rx)
    down_t = swap_tensor(down_y)
    qkv_keep_r, qkv_send_r, qkv_sums_r = project_grad(
        at, after(normed_ext, down_y), qkv_g_r, out_g_r
    )
    qkv_keep_r, qkv_send_r, up_t = together(qkv_keep_r, qkv_send_r, up_t)
    qkv_c_r = chips.swap_core(qkv_send_r)
    up_1 = add(up_l, up_t)
    up_x = chips.scatter_start(up_1, stages[0])
    lead = width // 6
    qkv_y_1 = add(qkv_keep_r[:lead], qkv_c_r[:lead])
    qkv_y_2 = add(qkv_keep_r[lead:], qkv_c_r[lead:])
    qkv_t_1 = swap_tensor(qkv_y_1)
    qkv_g_l, skip_g_l = attend_backward(
        qkv_l, skip_own, key_seg, query_seg, sums_l, turned_l, after(mixed_g_l, up_1, qkv_y_1, qkv_y_2)
    )
    qkv_g_l, skip_g_l, up_x, down_t, qkv_t_1 = together(qkv_g_l, skip_g_l, up_x, down_t, qkv_t_1)
    qkv_t_2 = swap_tensor(qkv_y_2)

    def rest(value):
        for stage in stages[3:]:
            value = chips.scatter(value, stage)
        for stage in reversed(stages[3:]):
            value = chips.gather(value, stage)
        return value

    factor = stages[0][1]
    up_rows = up_1.shape[0] // factor
    feed_2 = jnp.concatenate([add(*up_x), add(*down_lx, down_t)], axis=0)
    feed_x = chips.scatter_start(feed_2, stages[1])
    qkv_keep_l, qkv_send_l, qkv_sums_l = project_grad(
        at, after(normed_ext, feed_2), qkv_g_l, out_g_l
    )
    qkv_keep_l, qkv_send_l, qkv_sums_l, feed_x, qkv_t_2 = together(
        qkv_keep_l, qkv_send_l, qkv_sums_l, feed_x, qkv_t_2
    )
    qkv_c_l = chips.swap_core(qkv_send_l)
    feed_3 = add(*feed_x)
    feed_x = chips.scatter_start(feed_3, stages[2])

    qkv_1 = jnp.concatenate(
        [
            add(qkv_keep_l[:lead], qkv_c_l[:lead], qkv_t_1),
            add(qkv_keep_l[lead:], qkv_c_l[lead:], qkv_t_2),
        ],
        axis=0,
    )
    qkv_x = chips.scatter_start(qkv_1, stages[0])
    skip_back = swap_tensor(after(skip_g_r, qkv_1))
    input_grad, halo_grad, first_sums = first_back(
        where, at, after(qkv_g_l, qkv_1, feed_3), qkv_g_r, qkv_own, qkv_mine, qkv_theirs,
        block_input.reshape(tokens, width), halo, hidden_grad, row_vectors, rows,
    )
    input_grad, halo_grad, first_sums, qkv_x, feed_x = together(
        input_grad, halo_grad, first_sums, qkv_x, feed_x
    )

    qkv_2 = add(*qkv_x)
    qkv_x = chips.scatter_start(qkv_2, stages[1])
    feed_4 = rest(add(*feed_x))
    feed_x = chips.gather_start(after(feed_4, qkv_2), stages[2])
    own_small, other_small = small_step(
        where, at, middle_sums, after(first_sums, qkv_2, feed_4), qkv_sums_l, qkv_sums_r,
        bias_g_l1, bias_g_l2, bias_g_r1, bias_g_r2,
    )
    small_t = swap_tensor(other_small)
    halo_got = lax.ppermute(after(halo_grad, other_small), "tensor", [(1, 0)])
    skip_grad = skip_grad_of(at, after(skip_g_l, own_small), skip_back, rows)
    skip_grad, qkv_x, small_t = together(skip_grad, qkv_x, small_t)
    qkv_3 = add(*qkv_x)
    qkv_x = chips.scatter_start(qkv_3, stages[2])
    small = own_small + small_t
    small_c = chips.swap_core(small)
    block_output = block_half + after(f_r, small, qkv_3)
    block_output, small_c, feed_x = together(block_output, small_c, feed_x)
    feed_5 = chips.gather_finish(feed_x, stages[2])
    feed_x = chips.gather_start(feed_5, stages[1])
    small = small + small_c
    for stage in stages[3:]:
        small = sum(chips.gather_start(small, stage))
    columns = qkv_2.shape[1]
    small_rows = -(-where.size // (8 * columns)) * 8
    small = jnp.pad(small[0], (0, small_rows * columns - where.size)).reshape(small_rows, columns)
    small, qkv_x = together(after(small, feed_5), qkv_x)

    qkv_4 = jnp.concatenate([rest(add(*qkv_x)), small.astype(BF)], axis=0)
    qkv_x = chips.gather_start(qkv_4, stages[0])
    qkv_x, feed_x = together(qkv_x, feed_x)
    feed_6 = chips.gather_finish(feed_x, stages[1])
    up_6, down_6 = feed_6[:up_rows], feed_6[up_rows:]
    up_x = chips.gather_start(up_6, stages[0])
    qkv_5 = chips.gather_finish(qkv_x, stages[0])
    qkv_x = chips.gather_start(after(qkv_5, up_6), stages[2])
    qkv_x, up_x, down_6 = together(qkv_x, up_x, down_6)
    down_x = chips.gather_start(down_6, stages[0])
    up_7 = chips.gather_finish(up_x, stages[0])
    up_c = chips.swap_core(up_7)
    qkv_6 = chips.gather_finish(qkv_x, stages[2])
    qkv_x = chips.gather_start(after(qkv_6, up_7), stages[1])
    input_grad = add_halo(after(input_grad, qkv_6, up_7), halo_got, rows)
    up_weight_grad = up_out(at, after(up_7, input_grad), up_c)
    up_weight_grad, qkv_x, down_x = together(up_weight_grad, qkv_x, down_x)
    qkv_7 = chips.gather_finish(qkv_x, stages[1])
    qkv_other = chips.swap_core(qkv_7)
    down_7 = chips.gather_finish(down_x, stages[0])
    down_c = chips.swap_core(down_7)
    query_weight_grad, key_weight_grad, value_weight_grad, out_weight_grad, small = project_out(
        at, after(qkv_7, down_7), qkv_other, local, width // 2, factor**3
    )
    query_weight_grad, down_c = together(query_weight_grad, down_c)
    down_weight_grad = down_out(at, down_7, down_c)
    small = small.reshape(-1)

    return (
        block_output.reshape(rows, length, width),
        input_grad.reshape(rows, length, width),
        jnp.swapaxes(skip_grad, 1, 2),
        query_weight_grad,
        small[where.query],
        key_weight_grad,
        value_weight_grad.T,
        small[where.value],
        out_weight_grad,
        small[where.out],
        up_weight_grad,
        small[where.up],
        down_weight_grad,
        small[where.down],
        small[where.gain_1],
        small[where.shift_1],
        small[where.gain_2],
        small[where.shift_2],
    )


def solution(mesh):
    in_specs = (
        P("dp", "tensor", None),
        P("dp", None, "tensor"),
        P("dp", None),
        P("dp"),
        P(None, "tensor"),
        P("tensor"),
        P(None, "tensor"),
        P(None, "tensor"),
        P("tensor"),
        P("tensor", None),
        P(),
        P(None, "tensor"),
        P("tensor"),
        P("tensor", None),
        P(),
        P(),
        P(),
        P(),
        P(),
        P("dp", "tensor", None),
    )
    out_specs = (
        P("dp", "tensor", None),
        P("dp", "tensor", None),
        P("dp", None, "tensor"),
        P(None, "tensor"),
        P("tensor"),
        P(None, "tensor"),
        P(None, "tensor"),
        P("tensor"),
        P("tensor", None),
        P(),
        P(None, "tensor"),
        P("tensor"),
        P("tensor", None),
        P(),
        P(),
        P(),
        P(),
        P(),
    )
    return jax.shard_map(
        functools.partial(on_device, mesh.shape["dp"]),
        mesh=mesh,
        in_specs=in_specs,
        out_specs=out_specs,
        check_vma=False,
    )
```

```python
import functools
import itertools

import jax
import jax.numpy as jnp
from jax import lax
from jax.experimental import pallas as pl
from jax.experimental.pallas import tpu as pltpu
from jax.sharding import PartitionSpec as P

DH = 64
BF = jnp.bfloat16
F32 = jnp.float32
SPAN = 256
QB = 128
WIN = SPAN + QB
TH = 768
RC = 256
NEG = -1000000000.0
COST = pl.CostEstimate(flops=1 << 20, bytes_accessed=1 << 20, transcendentals=0)


def dot_nn(a, b):
    return lax.dot_general(a, b, (((1,), (0,)), ((), ())), preferred_element_type=F32)


def dot_nt(a, b):
    return lax.dot_general(a, b, (((1,), (1,)), ((), ())), preferred_element_type=F32)


def dot_tn(a, b):
    return lax.dot_general(a, b, (((0,), (0,)), ((), ())), preferred_element_type=F32)


def split_pair(block, low_lane):
    zero = jnp.zeros_like(block)
    return jnp.concatenate(
        [jnp.where(low_lane, block, zero), jnp.where(low_lane, zero, block)], axis=0
    )


def window_bias(kseg_ref, qseg_ref, start):
    key_at = lax.broadcasted_iota(jnp.int32, (WIN, QB), 0)
    query_at = lax.broadcasted_iota(jnp.int32, (WIN, QB), 1) + SPAN
    kseg = kseg_ref[0, start : start + WIN, :]
    qseg = qseg_ref[0, :, start : start + QB]
    allowed = ((kseg == qseg) & (key_at <= query_at)) | (key_at == query_at)
    bias = jnp.where(allowed, 0.0, NEG).astype(F32)
    return jnp.concatenate([bias, bias], axis=1)


def pair_values(x_ref, s_ref, t_s, pairs):
    base = 4 * pairs * DH
    for at in range(0, pairs, 2):
        fresh = x_ref[:, base + at * DH : base + at * DH + 128].T
        for pair in range(at, min(at + 2, pairs)):
            t_s[pair, :DH, :] = fresh[(pair - at) * DH : (pair - at + 1) * DH, :]
            t_s[pair, DH:, :] = s_ref[pair * DH : (pair + 1) * DH, :]


def attend_forward_kernel(pairs, x_ref, s_ref, kseg_ref, qseg_ref, o_ref, lse_ref, turned_ref, t_s):
    o_blocks = o_ref.shape[0] // QB
    pair_values(x_ref, s_ref, t_s, pairs)

    low = lax.broadcasted_iota(jnp.int32, (QB, 128), 1) < DH
    for block, pair in itertools.product(range(o_blocks), range(pairs)):
        start = block * QB
        if pair == 0:
            bias = window_bias(kseg_ref, qseg_ref, start)
        win = slice(start, start + WIN)
        rows = slice(start + SPAN, start + SPAN + QB)
        here = slice(start, start + QB)
        cols = slice(pair * 128, pair * 128 + 128)
        key_cols = slice((pairs + pair) * 128, (pairs + pair) * 128 + 128)
        queries = split_pair(x_ref[rows, cols], low)
        scores = dot_nt(x_ref[win, key_cols], queries) + bias
        largest = jnp.max(scores, axis=0, keepdims=True)
        expon = jnp.exp(scores - largest)
        total = jnp.sum(expon, axis=0, keepdims=True)
        probs = (expon * (1.0 / total)).astype(BF)
        out = dot_nn(t_s[pair, :, win], probs)
        out = jnp.concatenate([out[:DH, :QB], out[DH:, QB:]], axis=0)
        turned_ref[cols, here] = out
        o_ref[here, cols] = out.T.astype(BF)
        lse_ref[0, block, pair : pair + 1, :] = largest + jnp.log(total)


def attend_backward_kernel(
    pairs, x_ref, s_ref, kseg_ref, qseg_ref, lse_ref, turned_ref, g_ref, dx_ref, ds_ref,
    v_s, t_s, dk_s, dv_s,
):
    o_blocks = g_ref.shape[0] // QB
    pair_values(x_ref, s_ref, t_s, pairs)
    for pair in range(pairs):
        v_s[pair] = t_s[pair].T
        key_cols = slice((pairs + pair) * 128, (pairs + pair) * 128 + 128)
        t_s[pair] = x_ref[:, key_cols].T
    dk_s[...] = jnp.zeros_like(dk_s)
    dv_s[...] = jnp.zeros_like(dv_s)
    dx_ref[:SPAN, : pairs * 128] = jnp.zeros((SPAN, pairs * 128), BF)

    low = lax.broadcasted_iota(jnp.int32, (QB, 128), 1) < DH
    for block, pair in itertools.product(range(o_blocks), range(pairs)):
        start = block * QB
        if pair == 0:
            bias = window_bias(kseg_ref, qseg_ref, start)
        win = slice(start, start + WIN)
        rows = slice(start + SPAN, start + SPAN + QB)
        here = slice(start, start + QB)
        cols = slice(pair * 128, pair * 128 + 128)
        key_cols = slice((pairs + pair) * 128, (pairs + pair) * 128 + 128)
        queries = split_pair(x_ref[rows, cols], low)
        grads = split_pair(g_ref[here, cols], low)
        scores = dot_nt(x_ref[win, key_cols], queries) + bias
        probs = jnp.exp(scores - lse_ref[0, block, pair : pair + 1, :])
        prob_grad = dot_nt(v_s[pair, win], grads)
        terms = g_ref[here, cols].T.astype(F32) * turned_ref[cols, here]
        row_total = jnp.concatenate([down_rows(terms[:DH]), down_rows(terms[DH:])], axis=1)
        score_grad = (probs * (prob_grad - row_total)).astype(BF)
        dv_s[pair, win] += dot_nn(probs.astype(BF), grads)
        dk_s[pair, win] += dot_nn(score_grad, queries)
        out = dot_nn(t_s[pair, :, win], score_grad)
        out = jnp.concatenate([out[:DH, :QB], out[DH:, QB:]], axis=0)
        dx_ref[rows, cols] = (out.T * (DH**-0.5)).astype(BF)

    base = 4 * pairs * DH
    low_all = lax.broadcasted_iota(jnp.int32, (x_ref.shape[0], 128), 1) < DH
    for pair in range(pairs):
        key_cols = slice((pairs + pair) * 128, (pairs + pair) * 128 + 128)
        dx_ref[:, key_cols] = dk_s[pair].astype(BF)
        ds_ref[pair * DH : (pair + 1) * DH, :] = dv_s[pair].astype(BF).T[DH:, :]
    for at in range(0, pairs, 2):
        second = pltpu.roll(dv_s[at + 1], DH, 1) if at + 1 < pairs else jnp.zeros_like(dv_s[at])
        dx_ref[:, base + at * DH : base + at * DH + 128] = jnp.where(
            low_all, dv_s[at], second
        ).astype(BF)


def attention_specs(rows, blocks, columns, pairs):
    extended = SPAN + blocks * QB
    x_spec = pl.BlockSpec((extended, columns), lambda r: (r, 0))
    s_spec = pl.BlockSpec((pairs * DH, extended), lambda r: (r, 0))
    kseg_spec = pl.BlockSpec((1, extended, 1), lambda r: (r, 0, 0))
    qseg_spec = pl.BlockSpec((1, 1, blocks * QB), lambda r: (r, 0, 0))
    o_spec = pl.BlockSpec((blocks * QB, pairs * 128), lambda r: (r, 0))
    lse_spec = pl.BlockSpec((1, blocks, pairs, 2 * QB), lambda r: (r, 0, 0, 0))
    turned_spec = pl.BlockSpec((pairs * 128, blocks * QB), lambda r: (r, 0))
    return extended, x_spec, s_spec, kseg_spec, qseg_spec, o_spec, lse_spec, turned_spec


def attend_forward(extended_qkv, skip, kseg, qseg):
    rows, blocks, pairs = qseg.shape[0], qseg.shape[2] // QB, skip.shape[0] // DH // qseg.shape[0]
    columns = extended_qkv.shape[1]
    extended, x_spec, s_spec, kseg_spec, qseg_spec, o_spec, lse_spec, turned_spec = attention_specs(
        rows, blocks, columns, pairs
    )
    return pl.pallas_call(
        functools.partial(attend_forward_kernel, pairs),
        grid=(rows,),
        in_specs=[x_spec, s_spec, kseg_spec, qseg_spec],
        out_specs=[o_spec, lse_spec, turned_spec],
        out_shape=[
            jax.ShapeDtypeStruct((rows * blocks * QB, pairs * 128), BF),
            jax.ShapeDtypeStruct((rows, blocks, pairs, 2 * QB), F32),
            jax.ShapeDtypeStruct((rows * pairs * 128, blocks * QB), F32),
        ],
        scratch_shapes=[
            pltpu.VMEM((pairs, 128, extended), BF),
        ],
        cost_estimate=COST,
        name="attend_forward",
    )(extended_qkv, skip, kseg, qseg)


def attend_backward(extended_qkv, skip, kseg, qseg, sums, turned, grads):
    rows, blocks, pairs = qseg.shape[0], qseg.shape[2] // QB, skip.shape[0] // DH // qseg.shape[0]
    columns = extended_qkv.shape[1]
    extended, x_spec, s_spec, kseg_spec, qseg_spec, o_spec, lse_spec, turned_spec = attention_specs(
        rows, blocks, columns, pairs
    )
    return pl.pallas_call(
        functools.partial(attend_backward_kernel, pairs),
        grid=(rows,),
        in_specs=[x_spec, s_spec, kseg_spec, qseg_spec, lse_spec, turned_spec, o_spec],
        out_specs=[x_spec, s_spec],
        out_shape=[
            jax.ShapeDtypeStruct((rows * extended, columns), BF),
            jax.ShapeDtypeStruct((rows * pairs * DH, extended), BF),
        ],
        scratch_shapes=[
            pltpu.VMEM((pairs, extended, 128), BF),
            pltpu.VMEM((pairs, 128, extended), BF),
            pltpu.VMEM((pairs, extended, 128), F32),
            pltpu.VMEM((pairs, extended, 128), F32),
        ],
        cost_estimate=COST,
        name="attend_backward",
    )(extended_qkv, skip, kseg, qseg, sums, turned, grads)


def feed_kernel(
    core_ref,
    n_ref,
    g_ref,
    ua_ref,
    ub_ref,
    ba_ref,
    bb_ref,
    da_ref,
    db_ref,
    wua_ref,
    wub_ref,
    wda_ref,
    wdb_ref,
    ga_ref,
    gb_ref,
    down_ref,
    second_ref,
    turned_s,
    act_s,
    upg_s,
):
    step = pl.program_id(0)
    half = pl.num_programs(0) // 2
    first = step < half

    @pl.when(step == 0)
    def _():
        turned_s[...] = n_ref[...].T
        down_ref[...] = jnp.zeros_like(down_ref)
        second_ref[...] = jnp.zeros_like(second_ref)

    up_tile = jnp.where(first, ua_ref[...], ub_ref[...])
    down_tile = jnp.where(first, da_ref[...], db_ref[...])
    bias = jnp.where(first, ba_ref[...], bb_ref[...])
    root = 0.7978845608028654
    for start in range(0, n_ref.shape[0], RC):
        rows = slice(start, start + RC)
        upward = dot_nn(n_ref[rows, :], up_tile) + bias
        act_grad = dot_nt(g_ref[rows, :], down_tile)
        square = upward * upward
        bent = jnp.tanh(root * upward * (1.0 + 0.044715 * square))
        gate = 0.5 * (1.0 + bent)
        slope = gate + 0.5 * root * upward * (1.0 - bent * bent) * (1.0 + 0.134145 * square)
        act = (upward * gate).astype(BF)
        upg = (act_grad * slope).astype(BF)
        act_s[rows, :] = act
        upg_s[rows, :] = upg
        down_ref[rows, :] += dot_nn(act, down_tile)
        second_ref[rows, :] += dot_nt(upg, up_tile)
    up_weight_grad = dot_nn(turned_s[...], upg_s[...]).astype(BF)
    down_weight_grad = dot_tn(act_s[...], g_ref[...]).astype(BF)
    bias_grad = jnp.sum(upg_s[...].astype(F32), axis=0, keepdims=True)

    @pl.when(first)
    def _():
        wua_ref[...] = up_weight_grad
        wda_ref[...] = down_weight_grad
        ga_ref[...] = bias_grad

    @pl.when(jnp.logical_not(first))
    def _():
        wub_ref[...] = up_weight_grad
        wdb_ref[...] = down_weight_grad
        gb_ref[...] = bias_grad


def feed(at, normed, grads, up_a, up_b, bias, down_a, down_b, whole):
    tokens, width = normed.shape
    piece = up_a.shape[1] // 2 if whole else up_a.shape[1]
    tiles = piece // TH

    def a_at(i, c):
        at = jnp.minimum(i, tiles - 1)
        return at + (1 - c[0]) * tiles if whole else at

    def b_at(i, c):
        at = jnp.maximum(i - tiles, 0)
        return at + c[0] * tiles if whole else at

    def out_a(i, c):
        return jnp.minimum(i, tiles - 1)

    def out_b(i, c):
        return jnp.maximum(i - tiles, 0)

    resident = pl.BlockSpec((tokens, width), lambda i, c: (0, 0))
    once = pl.BlockSpec((tokens, width), lambda i, c: (0, 0))
    in_specs = [
        resident,
        resident,
        pl.BlockSpec((width, TH), lambda i, c: (0, a_at(i, c))),
        pl.BlockSpec((width, TH), lambda i, c: (0, b_at(i, c))),
        pl.BlockSpec((1, TH), lambda i, c: (0, out_a(i, c) + (1 - c[0]) * tiles)),
        pl.BlockSpec((1, TH), lambda i, c: (0, out_b(i, c) + c[0] * tiles)),
        pl.BlockSpec((TH, width), lambda i, c: (a_at(i, c), 0)),
        pl.BlockSpec((TH, width), lambda i, c: (b_at(i, c), 0)),
    ]
    out_specs = [
        pl.BlockSpec((width, TH), lambda i, c: (0, out_a(i, c))),
        pl.BlockSpec((width, TH), lambda i, c: (0, out_b(i, c))),
        pl.BlockSpec((TH, width), lambda i, c: (out_a(i, c), 0)),
        pl.BlockSpec((TH, width), lambda i, c: (out_b(i, c), 0)),
        pl.BlockSpec((1, TH), lambda i, c: (0, out_a(i, c))),
        pl.BlockSpec((1, TH), lambda i, c: (0, out_b(i, c))),
        once,
        once,
    ]
    out_shape = [
        jax.ShapeDtypeStruct((width, piece), BF),
        jax.ShapeDtypeStruct((width, piece), BF),
        jax.ShapeDtypeStruct((piece, width), BF),
        jax.ShapeDtypeStruct((piece, width), BF),
        jax.ShapeDtypeStruct((1, piece), F32),
        jax.ShapeDtypeStruct((1, piece), F32),
        jax.ShapeDtypeStruct((tokens, width), F32),
        jax.ShapeDtypeStruct((tokens, width), F32),
    ]
    return pl.pallas_call(
        feed_kernel,
        grid_spec=pltpu.PrefetchScalarGridSpec(
            num_scalar_prefetch=1,
            grid=(2 * tiles,),
            in_specs=in_specs,
            out_specs=out_specs,
            scratch_shapes=[
                pltpu.VMEM((width, tokens), BF),
                pltpu.VMEM((tokens, TH), BF),
                pltpu.VMEM((tokens, TH), BF),
            ],
        ),
        out_shape=out_shape,
        compiler_params=pltpu.CompilerParams(vmem_limit_bytes=56 << 20),
        cost_estimate=COST,
        name="feed",
    )(at, normed, grads, up_a, up_b, bias, bias, down_a, down_b)


def norm_rows(values, gain_row, shift_row):
    center = values - jnp.mean(values, axis=-1, keepdims=True)
    variance = jnp.mean(center * center, axis=-1, keepdims=True)
    return center * lax.rsqrt(variance + 1e-05) * gain_row + shift_row


def whole_spec(value):
    zeros = (0,) * value.ndim
    return pl.BlockSpec(value.shape, lambda *_: zeros)


def open_kernel(
    at_ref, qw_ref, kw_ref, vw_ref, s_ref, w_ref, w_send_ref, s_send_ref, s_own_ref
):
    side = at_ref[1]
    rows, half, total = s_ref.shape
    width, local, length = qw_ref.shape[0], qw_ref.shape[1], total // 2
    depth = w_send_ref.shape[0]
    cut = pl.ds(pl.multiple_of(at_ref[0] * depth, depth), depth)
    w_ref[:, :local] = qw_ref[...]
    w_ref[:, local : 2 * local] = kw_ref[...]
    w_ref[:, 2 * local : 2 * local + half] = vw_ref[...].T
    w_ref[:, 2 * local + half :] = jnp.zeros((width, w_ref.shape[1] - 2 * local - half), BF)
    w_send_ref[...] = w_ref[cut, :]
    own = pl.ds(pl.multiple_of(side * length, length), length)
    other = pl.ds(pl.multiple_of((1 - side) * length, length), length)
    for row in range(rows):
        lines = slice(row * half, (row + 1) * half)
        middle = s_ref[row, :, length - SPAN : length]
        s_send_ref[lines, :SPAN] = middle
        s_own_ref[lines, :SPAN] = middle
        s_send_ref[lines, SPAN:] = s_ref[row, :, other]
        s_own_ref[lines, SPAN:] = s_ref[row, :, own]


def open_step(at, qw, kw, vw, skip):
    rows, half, length = skip.shape[0], skip.shape[1], skip.shape[2] // 2
    width, local = qw.shape
    columns = -(-(2 * local + half) // 256) * 256
    shapes = [
        (width, columns),
        (width // 2, columns),
        (rows * half, SPAN + length),
        (rows * half, SPAN + length),
    ]
    return pl.pallas_call(
        open_kernel,
        grid_spec=pltpu.PrefetchScalarGridSpec(
            num_scalar_prefetch=1,
            grid=(1,),
            in_specs=[whole_spec(v) for v in (qw, kw, vw, skip)],
            out_specs=[pl.BlockSpec(shape, lambda *_: (0, 0)) for shape in shapes],
        ),
        out_shape=[jax.ShapeDtypeStruct(shape, BF) for shape in shapes],
        cost_estimate=COST,
        name="open",
    )(at, qw, kw, vw, skip)


class Rows:
    def __init__(self, width, local, hidden):
        half = local // 2
        self.up = slice(0, hidden)
        self.query = slice(hidden, hidden + local)
        self.value = slice(hidden + local, hidden + local + half)
        start = -(-self.value.stop // 128) * 128
        self.pad = start - self.value.stop
        self.gain_1, self.shift_1, self.gain_2, self.shift_2, self.out, self.down = (
            slice(start + n * width, start + (n + 1) * width) for n in range(6)
        )
        self.size = start + 6 * width


def store_projection(o_ref, values, q_bias, v_bias):
    local, half = q_bias.shape[1], v_bias.shape[1]
    o_ref[:, :local] = ((values[:, :local] + q_bias) * (DH**-0.5)).astype(BF)
    o_ref[:, local : 2 * local] = values[:, local : 2 * local].astype(BF)
    stop = 2 * local + half
    o_ref[:, 2 * local : stop] = (values[:, 2 * local : stop] + v_bias).astype(BF)
    o_ref[:, stop:] = values[:, stop:].astype(BF)


def project_own_kernel(where, n_ref, h_ref, rows_ref, w_ref, ne_ref, o_ref):
    ne_ref[:SPAN, :] = norm_rows(
        h_ref[...].astype(F32), rows_ref[:, where.gain_1], rows_ref[:, where.shift_1]
    ).astype(BF)
    ne_ref[SPAN:, :] = n_ref[...]
    store_projection(
        o_ref, dot_nn(ne_ref[...], w_ref[...]), rows_ref[:, where.query], rows_ref[:, where.value]
    )


def project_own(where, normed, halo, row_vectors, weight, rows):
    width, columns = weight.shape
    length = normed.shape[0] // rows
    size = SPAN + length
    row = lambda count, cols: pl.BlockSpec((count, cols), lambda r: (r, 0))
    return pl.pallas_call(
        functools.partial(project_own_kernel, where),
        grid=(rows,),
        in_specs=[row(length, width), row(SPAN, width), whole_spec(row_vectors), whole_spec(weight)],
        out_specs=[row(size, width), row(size, columns)],
        out_shape=[
            jax.ShapeDtypeStruct((rows * size, width), BF),
            jax.ShapeDtypeStruct((rows * size, columns), BF),
        ],
        cost_estimate=COST,
        name="project_own",
    )(normed, halo, row_vectors, weight)


def join_cores(at_ref, mine_ref, other_ref, scratch):
    depth = mine_ref.shape[0]
    core = at_ref[0]
    scratch[pl.ds(pl.multiple_of(core * depth, depth), depth), :] = mine_ref[...]
    scratch[pl.ds(pl.multiple_of((1 - core) * depth, depth), depth), :] = other_ref[...]


def project_other_kernel(where, at_ref, ne_ref, mine_ref, other_ref, rows_ref, o_ref, w_s):
    @pl.when(pl.program_id(0) == 0)
    def _():
        join_cores(at_ref, mine_ref, other_ref, w_s)

    store_projection(
        o_ref, dot_nn(ne_ref[...], w_s[...]), rows_ref[:, where.query], rows_ref[:, where.value]
    )


def project_other(where, at, normed_ext, mine, other, row_vectors, rows):
    size, width = normed_ext.shape
    step = size // rows
    columns = mine.shape[1]
    return pl.pallas_call(
        functools.partial(project_other_kernel, where),
        grid_spec=pltpu.PrefetchScalarGridSpec(
            num_scalar_prefetch=1,
            grid=(rows,),
            in_specs=[
                pl.BlockSpec((step, width), lambda i, a: (i, 0)),
                *[whole_spec(v) for v in (mine, other, row_vectors)],
            ],
            out_specs=pl.BlockSpec((step, columns), lambda i, a: (i, 0)),
            scratch_shapes=[pltpu.VMEM((width, columns), BF)],
        ),
        out_shape=jax.ShapeDtypeStruct((size, columns), BF),
        cost_estimate=COST,
        name="project_other",
    )(at, normed_ext, mine, other, row_vectors)


def middle_kernel(
    where, at_ref, ml_ref, mr_ref, wl_ref, w1_ref, w2_ref, x_ref, rows_ref, hidden_ref, n_ref, wr_ref
):
    @pl.when(pl.program_id(0) == 0)
    def _():
        join_cores(at_ref, w1_ref, w2_ref, wr_ref)

    values = dot_nn(ml_ref[...], wl_ref[...]) + dot_nn(mr_ref[...], wr_ref[...])
    hidden = x_ref[...].astype(F32) + (values + rows_ref[:, where.out])
    hidden_ref[...] = hidden
    n_ref[...] = norm_rows(hidden, rows_ref[:, where.gain_2], rows_ref[:, where.shift_2]).astype(BF)


def middle(where, at, mixed_l, mixed_r, own, mine, other, x, row_vectors):
    tokens, width = x.shape
    local = mixed_l.shape[1]
    tile = lambda columns: pl.BlockSpec((RC, columns), lambda i, a: (i, 0))
    return pl.pallas_call(
        functools.partial(middle_kernel, where),
        grid_spec=pltpu.PrefetchScalarGridSpec(
            num_scalar_prefetch=1,
            grid=(tokens // RC,),
            in_specs=[
                tile(local), tile(local), *[whole_spec(v) for v in (own, mine, other)],
                tile(width), whole_spec(row_vectors),
            ],
            out_specs=[tile(width), tile(width), whole_spec(own)],
        ),
        out_shape=[
            jax.ShapeDtypeStruct((tokens, width), F32),
            jax.ShapeDtypeStruct((tokens, width), BF),
            jax.ShapeDtypeStruct(own.shape, BF),
        ],
        cost_estimate=COST,
        name="middle",
    )(at, mixed_l, mixed_r, own, mine, other, x, row_vectors)


def norm_pull(values, grad, gain_row):
    center = values - jnp.mean(values, axis=-1, keepdims=True)
    variance = jnp.mean(center * center, axis=-1, keepdims=True)
    rstd = lax.rsqrt(variance + 1e-05)
    unit = center * rstd
    scaled = grad * gain_row
    back = rstd * (
        scaled
        - jnp.mean(scaled, axis=-1, keepdims=True)
        - unit * jnp.mean(scaled * unit, axis=-1, keepdims=True)
    )
    return back, grad * unit


def down_rows(values):
    return jnp.sum(values, axis=0, keepdims=True)


def middle_back_kernel(
    where, bl_ref, br_ref, hidden_ref, g_ref, ml_ref, mr_ref, wl_ref, wr_ref, rows_ref,
    hg_ref, gl_ref, gr_ref, ol_ref, or_ref, sums_ref, acc_l, acc_r,
):
    step = pl.program_id(0)

    @pl.when(step == 0)
    def _():
        acc_l[...] = jnp.zeros_like(acc_l)
        acc_r[...] = jnp.zeros_like(acc_r)
        sums_ref[...] = jnp.zeros_like(sums_ref)

    grad = bl_ref[...] + br_ref[...]
    back, gain_term = norm_pull(hidden_ref[...], grad, rows_ref[:, where.gain_2])
    cot = g_ref[...].astype(F32)
    hidden_grad = cot + back
    low = hidden_grad.astype(BF)
    hg_ref[...] = hidden_grad
    gl_ref[...] = dot_nt(low, wl_ref[...]).astype(BF)
    gr_ref[...] = dot_nt(low, wr_ref[...]).astype(BF)
    turned = low.T
    acc_l[...] += dot_nn(turned, ml_ref[...])
    acc_r[...] += dot_nn(turned, mr_ref[...])
    for at, term in enumerate((low.astype(F32), cot, gain_term, grad)):
        sums_ref[at : at + 1, :] += down_rows(term)

    @pl.when(step == pl.num_programs(0) - 1)
    def _():
        ol_ref[...] = acc_l[...].astype(BF)
        or_ref[...] = acc_r[...].astype(BF)


def middle_back(where, back_l, back_r, hidden, grads, mixed_l, mixed_r, own, other, row_vectors):
    tokens, width = hidden.shape
    local = mixed_l.shape[1]
    tile = lambda columns: pl.BlockSpec((RC, columns), lambda i: (i, 0))
    fixed = lambda rows, columns: pl.BlockSpec((rows, columns), lambda i: (0, 0))
    return pl.pallas_call(
        functools.partial(middle_back_kernel, where),
        grid=(tokens // RC,),
        in_specs=[
            tile(width), tile(width), tile(width), tile(width), tile(local), tile(local),
            whole_spec(own), whole_spec(other), whole_spec(row_vectors),
        ],
        out_specs=[
            tile(width), tile(local), tile(local),
            fixed(width, local), fixed(width, local), fixed(8, width),
        ],
        scratch_shapes=[pltpu.VMEM((width, local), F32), pltpu.VMEM((width, local), F32)],
        out_shape=[
            jax.ShapeDtypeStruct((tokens, width), F32),
            jax.ShapeDtypeStruct((tokens, local), BF),
            jax.ShapeDtypeStruct((tokens, local), BF),
            jax.ShapeDtypeStruct((width, local), BF),
            jax.ShapeDtypeStruct((width, local), BF),
            jax.ShapeDtypeStruct((8, width), F32),
        ],
        cost_estimate=COST,
        name="middle_back",
    )(back_l, back_r, hidden, grads, mixed_l, mixed_r, own, other, row_vectors)


def project_grad_kernel(at_ref, n_ref, d_ref, w_ref, keep_ref, send_ref, sum_ref):
    values = dot_tn(n_ref[...], d_ref[...]).astype(BF)
    columns = d_ref.shape[1]

    @pl.when(pl.program_id(0) == 0)
    def _():
        send_ref[:, :columns] = values
        send_ref[:, columns:] = w_ref[...]
        sum_ref[...] = down_rows(d_ref[...].astype(F32))

    @pl.when(pl.program_id(0) == 1)
    def _():
        keep_ref[:, :columns] = values
        keep_ref[:, columns:] = w_ref[...]


def project_grad(at, normed_ext, grads, out_grad):
    size, width = normed_ext.shape
    columns, more = grads.shape[1], out_grad.shape[1]
    fixed = pl.BlockSpec((width // 2, columns + more), lambda i, a: (0, 0))
    half = lambda i, a: i * a[0] + (1 - i) * (1 - a[0])
    return pl.pallas_call(
        project_grad_kernel,
        grid_spec=pltpu.PrefetchScalarGridSpec(
            num_scalar_prefetch=1,
            grid=(2,),
            in_specs=[
                pl.BlockSpec((size, width // 2), lambda i, a: (0, half(i, a))),
                whole_spec(grads),
                pl.BlockSpec((width // 2, more), lambda i, a: (half(i, a), 0)),
            ],
            out_specs=[fixed, fixed, pl.BlockSpec((1, columns), lambda i, a: (0, 0))],
        ),
        out_shape=[
            jax.ShapeDtypeStruct((width // 2, columns + more), BF),
            jax.ShapeDtypeStruct((width // 2, columns + more), BF),
            jax.ShapeDtypeStruct((1, columns), F32),
        ],
        cost_estimate=COST,
        name="project_grad",
    )(at, normed_ext, grads, out_grad)


def first_back_kernel(
    where, at_ref, dl_ref, dr_ref, wl_ref, mine_ref, other_ref, x_ref, h_ref, hg_ref, rows_ref,
    ig_ref, ih_ref, sums_ref, w_s,
):
    block = pl.program_id(1)

    @pl.when((pl.program_id(0) == 0) & (block == 0))
    def _():
        join_cores(at_ref, mine_ref, other_ref, w_s)
        sums_ref[...] = jnp.zeros_like(sums_ref)

    grad = dot_nt(dl_ref[...], wl_ref[...]) + dot_nt(dr_ref[...], w_s[...])
    values = jnp.where(block == 0, h_ref[...], x_ref[...]).astype(F32)
    back, gain_term = norm_pull(values, grad, rows_ref[:, where.gain_1])
    sums_ref[0:1, :] += down_rows(gain_term)
    sums_ref[1:2, :] += down_rows(grad)

    @pl.when(block == 0)
    def _():
        ih_ref[...] = back.astype(BF)

    @pl.when(block > 0)
    def _():
        ig_ref[...] = hg_ref[...] + back


def first_back(where, at, grads_l, grads_r, own, mine, other, x, halo, hidden_grad, row_vectors, rows):
    tokens, width = x.shape
    columns = grads_l.shape[1]
    blocks = tokens // SPAN // rows
    extended = pl.BlockSpec((SPAN, columns), lambda r, j, a: (r * (blocks + 1) + j, 0))
    inner = pl.BlockSpec((SPAN, width), lambda r, j, a: (r * blocks + jnp.maximum(j - 1, 0), 0))
    outer = pl.BlockSpec((SPAN, width), lambda r, j, a: (r, 0))
    return pl.pallas_call(
        functools.partial(first_back_kernel, where),
        grid_spec=pltpu.PrefetchScalarGridSpec(
            num_scalar_prefetch=1,
            grid=(rows, blocks + 1),
            in_specs=[
                extended, extended, *[whole_spec(v) for v in (own, mine, other)],
                inner, outer, inner, whole_spec(row_vectors),
            ],
            out_specs=[inner, outer, pl.BlockSpec((8, width), lambda r, j, a: (0, 0))],
            scratch_shapes=[pltpu.VMEM((width, columns), BF)],
        ),
        out_shape=[
            jax.ShapeDtypeStruct((tokens, width), F32),
            jax.ShapeDtypeStruct((rows * SPAN, width), BF),
            jax.ShapeDtypeStruct((8, width), F32),
        ],
        cost_estimate=COST,
        name="first_back",
    )(at, grads_l, grads_r, own, mine, other, x, halo, hidden_grad, row_vectors)


def add_halo_kernel(ig_ref, got_ref, o_ref):
    o_ref[...] = ig_ref[...] + got_ref[...].astype(F32)


def add_halo(input_grad, got, rows):
    width = got.shape[1]
    blocks = input_grad.shape[0] // SPAN // rows
    last = pl.BlockSpec((SPAN, width), lambda r: (r * blocks + blocks - 1, 0))
    return pl.pallas_call(
        add_halo_kernel,
        grid=(rows,),
        in_specs=[last, pl.BlockSpec((SPAN, width), lambda r: (r, 0))],
        out_specs=last,
        out_shape=jax.ShapeDtypeStruct(input_grad.shape, F32),
        input_output_aliases={0: 0},
        cost_estimate=COST,
        name="add_halo",
    )(input_grad, got)


def skip_grad_kernel(at_ref, mine_ref, got_ref, o_ref):
    side = at_ref[1]
    rows, half, total = o_ref.shape
    length = total // 2
    own = pl.ds(pl.multiple_of(side * length, length), length)
    other = pl.ds(pl.multiple_of((1 - side) * length, length), length)
    for row in range(rows):
        lines = slice(row * half, (row + 1) * half)
        o_ref[row, :, own] = mine_ref[lines, SPAN:].astype(F32)
        o_ref[row, :, other] = got_ref[lines, SPAN:].astype(F32)
        o_ref[row, :, length - SPAN : length] += mine_ref[lines, :SPAN].astype(F32) + got_ref[
            lines, :SPAN
        ].astype(F32)


def skip_grad_of(at, mine, got, rows):
    lines, size = mine.shape
    shape = (rows, lines // rows, 2 * (size - SPAN))
    return pl.pallas_call(
        skip_grad_kernel,
        grid_spec=pltpu.PrefetchScalarGridSpec(
            num_scalar_prefetch=1,
            grid=(1,),
            in_specs=[whole_spec(mine), whole_spec(got)],
            out_specs=pl.BlockSpec(shape, lambda i, a: (0, 0, 0)),
        ),
        out_shape=jax.ShapeDtypeStruct(shape, F32),
        cost_estimate=COST,
        name="skip_grad",
    )(at, mine, got)


def small_kernel(where, at_ref, m_ref, f_ref, ql_ref, qr_ref, l1_ref, l2_ref, r1_ref, r2_ref, own_ref, other_ref):
    core = at_ref[0]
    local = where.query.stop - where.query.start
    half = where.value.stop - where.value.start
    piece = l1_ref.shape[1]
    for o_ref, q_ref, one_ref, two_ref in (
        (own_ref, ql_ref, l1_ref, l2_ref), (other_ref, qr_ref, r1_ref, r2_ref)
    ):
        o_ref[...] = jnp.zeros_like(o_ref)
        o_ref[:, pl.ds(pl.multiple_of(core * piece, 128), piece)] = one_ref[...]
        o_ref[:, pl.ds(pl.multiple_of((1 - core) * piece, 128), piece)] = two_ref[...]
        o_ref[:, where.query] = q_ref[:, :local]
        o_ref[:, where.value] = q_ref[:, 2 * local : 2 * local + half]
        o_ref[:, where.out] = m_ref[0:1, :]
        o_ref[:, where.down] = m_ref[1:2, :]
        o_ref[:, where.gain_2] = m_ref[2:3, :]
        o_ref[:, where.shift_2] = m_ref[3:4, :]
        o_ref[:, where.gain_1] = f_ref[0:1, :]
        o_ref[:, where.shift_1] = f_ref[1:2, :]


def small_step(where, at, *values):
    return pl.pallas_call(
        functools.partial(small_kernel, where),
        grid_spec=pltpu.PrefetchScalarGridSpec(
            num_scalar_prefetch=1,
            grid=(1,),
            in_specs=[whole_spec(v) for v in values],
            out_specs=[pl.BlockSpec((1, where.size), lambda i, a: (0, 0))] * 2,
        ),
        out_shape=[jax.ShapeDtypeStruct((1, where.size), F32)] * 2,
        cost_estimate=COST,
        name="small",
    )(at, *values)


def down_out_kernel(at_ref, mine_ref, other_ref, o_ref):
    is_mine = pl.program_id(0) // 2 == at_ref[0]
    o_ref[...] = jnp.where(is_mine, mine_ref[...], other_ref[...]).astype(F32)


def down_out(at, mine, other):
    rows, width = mine.shape
    block = pl.BlockSpec((rows // 2, width), lambda i, a: (i % 2, 0))
    return pl.pallas_call(
        down_out_kernel,
        grid_spec=pltpu.PrefetchScalarGridSpec(
            num_scalar_prefetch=1,
            grid=(4,),
            in_specs=[block, block],
            out_specs=pl.BlockSpec((rows // 2, width), lambda i, a: (i, 0)),
        ),
        out_shape=jax.ShapeDtypeStruct((2 * rows, width), F32),
        cost_estimate=COST,
        name="down_out",
    )(at, mine, other)


def up_out_kernel(at_ref, mine_ref, other_ref, o_ref):
    core = at_ref[0]
    piece = mine_ref.shape[1]
    for ref, at in ((mine_ref, core), (other_ref, 1 - core)):
        o_ref[:, pl.ds(pl.multiple_of(at * piece, 128), piece)] = ref[...].astype(F32)


def up_out(at, mine, other):
    rows, width = mine.shape
    block = pl.BlockSpec((rows // 4, width), lambda i, a: (i, 0))
    return pl.pallas_call(
        up_out_kernel,
        grid_spec=pltpu.PrefetchScalarGridSpec(
            num_scalar_prefetch=1,
            grid=(4,),
            in_specs=[block, block],
            out_specs=pl.BlockSpec((rows // 4, 2 * width), lambda i, a: (i, 0)),
        ),
        out_shape=jax.ShapeDtypeStruct((rows, 2 * width), F32),
        cost_estimate=COST,
        name="up_out",
    )(at, mine, other)


def project_out_kernel(blocks, at_ref, mine_ref, other_ref, q_ref, k_ref, v_ref, out_ref, small_ref):
    core = at_ref[0]
    local = q_ref.shape[1]
    depth = q_ref.shape[0] // 2
    count = depth // blocks
    step = mine_ref.shape[0] // blocks
    columns = mine_ref.shape[1] - local
    for ref, at in ((mine_ref, core), (other_ref, 1 - core)):
        start = pl.multiple_of(at * depth, depth)
        places = [(n % (blocks // 2)) * 2 + n // (blocks // 2) for n in range(blocks)]
        parts = [ref[n * step : n * step + count, :].astype(F32) for n in places]
        values = jnp.concatenate(parts, axis=0)
        rows = pl.ds(start, depth)
        q_ref[rows, :] = values[:, :local]
        k_ref[rows, :] = values[:, local : 2 * local]
        v_ref[:, rows] = values[:, 2 * local : 2 * local + v_ref.shape[0]].T
        out_ref[:, rows] = values[:, columns:].T
    small_ref[...] = sum(
        mine_ref[n * step + count : (n + 1) * step, :].astype(F32) for n in range(blocks)
    )


def project_out(at, mine, other, local, depth, blocks):
    columns = mine.shape[1]
    rest = (mine.shape[0] - depth) // blocks
    shapes = [
        (2 * depth, local), (2 * depth, local), (local // 2, 2 * depth), (local, 2 * depth),
        (rest, columns),
    ]
    return pl.pallas_call(
        functools.partial(project_out_kernel, blocks),
        grid_spec=pltpu.PrefetchScalarGridSpec(
            num_scalar_prefetch=1,
            grid=(1,),
            in_specs=[whole_spec(mine), whole_spec(other)],
            out_specs=[pl.BlockSpec(s, lambda i, a: (0, 0)) for s in shapes],
        ),
        out_shape=[jax.ShapeDtypeStruct(s, F32) for s in shapes],
        cost_estimate=COST,
        name="project_out",
    )(at, mine, other)


def after(value, *others):
    return lax.optimization_barrier((value, *others))[0]


def together(*values):
    return lax.optimization_barrier(values)


class Chips:
    def __init__(self, count):
        self.count = count
        self.factors = [2] * ((count // 2).bit_length() - 1)
        self.index = lax.axis_index("dp")
        self.core = self.index % 2

    def flip(self, value, bit):
        return lax.ppermute(value, "dp", [(i, i ^ bit) for i in range(self.count)])

    def swap_core(self, value):
        return self.flip(value, 1)

    def shift(self, value, stride, factor, by):
        perm = []
        for i in range(self.count):
            digit = (i // stride) % factor
            perm.append((i, i + (((digit + by) % factor) - digit) * stride))
        return lax.ppermute(value, "dp", perm)

    def stages(self):
        stride = 2
        for factor in self.factors:
            yield stride, factor, (self.index // stride) % factor
            stride *= factor

    def scatter_start(self, value, stage):
        stride, factor, digit = stage
        rows = value.shape[0] // factor
        parts = [lax.dynamic_slice_in_dim(value, digit * rows, rows, 0)]
        for by in range(1, factor):
            part = lax.dynamic_slice_in_dim(value, ((digit + by) % factor) * rows, rows, 0)
            parts.append(self.shift(part, stride, factor, by))
        return tuple(parts)

    def scatter(self, value, stage):
        return add(*self.scatter_start(value, stage))

    def gather_start(self, value, stage):
        stride, factor, digit = stage
        return (value, *(self.shift(value, stride, factor, by) for by in range(1, factor)))

    def gather(self, value, stage):
        return self.gather_finish(self.gather_start(value, stage), stage)

    def gather_finish(self, parts, stage):
        stride, factor, digit = stage
        return jnp.concatenate(
            [
                lax.select_n((digit - at) % factor, *parts)
                if factor > 2
                else jnp.where(digit == at, parts[0], parts[1])
                for at in range(factor)
            ],
            axis=0,
        )

    def sum_small(self, value):
        value = value + self.swap_core(value)
        for stride, factor, digit in self.stages():
            total = value
            for by in range(1, factor):
                total = total + self.shift(value, stride, factor, by)
            value = total
        return value


def swap_tensor(value):
    return lax.ppermute(value, "tensor", [(0, 1), (1, 0)])


def block_of(value, at, count, axis):
    size = value.shape[axis] // count
    return lax.dynamic_slice_in_dim(value, at * size, size, axis)


def in_order(bit, mine, other, axis):
    return jnp.concatenate(
        [jnp.where(bit == 0, mine, other), jnp.where(bit == 0, other, mine)], axis=axis
    )


def add(*values):
    total = values[0].astype(F32)
    for value in values[1:]:
        total = total + value.astype(F32)
    return total.astype(BF)


def on_device(
    dp_count,
    block_input,
    skip_values,
    segment_ids,
    row_fill,
    query_weight,
    query_bias,
    key_weight,
    value_weight,
    value_bias,
    out_weight,
    out_bias,
    up_weight,
    up_bias,
    down_weight,
    down_bias,
    first_gain,
    first_shift,
    second_gain,
    second_shift,
    cotangent,
):
    chips = Chips(dp_count)
    core = chips.core
    side = lax.axis_index("tensor")
    at = jnp.stack([core, side]).astype(jnp.int32)
    rows, length, width = block_input.shape
    tokens = rows * length
    local = query_weight.shape[1]
    local_half = local // 2
    hidden_local = up_weight.shape[1]
    piece = hidden_local // 2
    stages = list(chips.stages())
    where = Rows(width, local, hidden_local)

    out_mine = swap_tensor(block_of(out_weight, core, 2, 0))
    halo_send = block_input[:, length - SPAN :].reshape(rows * SPAN, width)
    halo = lax.ppermute(halo_send, "tensor", [(0, 1)])
    qkv_own, qkv_send, skip_send, skip_own = open_step(
        at, after(query_weight, halo_send), key_weight, value_weight.T,
        jnp.swapaxes(skip_values, 1, 2),
    )
    row_vectors = jnp.concatenate(
        [
            up_bias, query_bias, value_bias, jnp.zeros((where.pad,), F32),
            first_gain, first_shift, second_gain, second_shift, out_bias, down_bias,
        ]
    ).reshape(1, -1)
    normed = norm_rows(
        after(block_input, halo_send).astype(F32), first_gain, first_shift
    ).astype(BF).reshape(tokens, width)

    position = jnp.arange(segment_ids.shape[1], dtype=jnp.int32)
    usable = jnp.where(position[None] < row_fill[:, None], segment_ids, -1)
    query_seg = lax.dynamic_slice_in_dim(segment_ids, side * length, length, 1)
    key_seg = jnp.concatenate(
        [
            jnp.where(side == 0, -1, usable[:, length - SPAN : length]),
            lax.dynamic_slice_in_dim(usable, side * length, length, 1),
        ],
        axis=1,
    )
    query_seg = query_seg.reshape(rows, 1, length)
    key_seg = key_seg.reshape(rows, SPAN + length, 1)

    down_piece = block_of(down_weight, core, 2, 0)
    up_piece = block_of(up_weight, core, 2, 1)
    key_seg, query_seg, normed, row_vectors, qkv_send, out_mine, down_piece, up_piece = together(
        key_seg, query_seg, normed, row_vectors, qkv_send, out_mine, down_piece, up_piece
    )
    out_theirs = chips.swap_core(out_mine)
    qkv_mine = swap_tensor(qkv_send)
    rows_other = swap_tensor(after(row_vectors, qkv_send))

    normed_ext, qkv_l = project_own(where, normed, halo, row_vectors, qkv_own, rows)
    lines = skip_send.shape[0] // 2
    qkv_l, skip_send_1, skip_send_2, out_theirs = together(
        qkv_l, skip_send[:lines], skip_send[lines:], out_theirs
    )
    skip_got_1 = swap_tensor(skip_send_1)
    mixed_l, sums_l, turned_l = attend_forward(qkv_l, skip_own, key_seg, query_seg)
    mixed_l, skip_got_1, qkv_mine, rows_other, skip_send_2 = together(
        mixed_l, skip_got_1, qkv_mine, rows_other, skip_send_2
    )
    skip_got_2 = swap_tensor(skip_send_2)
    qkv_theirs = chips.swap_core(qkv_mine)
    qkv_r = project_other(
        where, at, after(normed_ext, mixed_l), qkv_mine, qkv_theirs, rows_other, rows
    )
    qkv_r, skip_got_2, down_piece, up_piece = together(qkv_r, skip_got_2, down_piece, up_piece)
    down_r1 = swap_tensor(down_piece)
    up_r1 = swap_tensor(after(up_piece, down_piece))
    skip_got = jnp.concatenate([skip_got_1, skip_got_2], axis=0)
    mixed_r, sums_r, turned_r = attend_forward(qkv_r, skip_got, key_seg, query_seg)
    hidden, normed_two, out_other = middle(
        where, at, mixed_l, mixed_r, out_weight, out_mine, out_theirs,
        block_input.reshape(tokens, width), row_vectors,
    )

    out_grad = cotangent.reshape(tokens, width)
    (up_g_l2, up_g_l1, down_g_l2, down_g_l1, bias_g_l2, bias_g_l1, f_l, b_l) = feed(
        at, normed_two, out_grad, up_weight, up_weight, row_vectors, down_weight, down_weight, True,
    )
    b_l, up_g_l2, down_g_l2, down_r1, up_r1 = together(b_l, up_g_l2, down_g_l2, down_r1, up_r1)
    down_r2 = chips.swap_core(down_r1)
    up_r2 = chips.swap_core(up_r1)
    block_half = hidden + (after(f_l, b_l) + down_bias)
    block_half, up_r2, down_r2, up_g_l2, down_g_l2 = together(
        block_half, up_r2, down_r2, up_g_l2, down_g_l2
    )
    up_c_l, down_c_l = chips.swap_core(up_g_l2), chips.swap_core(down_g_l2)
    (up_g_r2, up_g_r1, down_g_r2, down_g_r1, bias_g_r2, bias_g_r1, f_r, b_r) = feed(
        at, after(normed_two, block_half), out_grad, up_r2, up_r1, rows_other, down_r2, down_r1, False
    )
    up_g_r2, up_g_r1, down_g_r2, down_g_r1, b_r, up_c_l, down_c_l = together(
        up_g_r2, up_g_r1, down_g_r2, down_g_r1, b_r, up_c_l, down_c_l
    )

    up_c_r, down_c_r = chips.swap_core(up_g_r2), chips.swap_core(down_g_r2)
    up_l, down_l = add(up_g_l1, up_c_l), add(down_g_l1, down_c_l)
    down_lx = chips.scatter_start(down_l, stages[0])
    up_c_r, down_c_r, up_l, down_l = together(up_c_r, down_c_r, up_l, down_l)
    up_sum_r, down_sum_r = add(up_g_r1, up_c_r), add(down_g_r1, down_c_r)
    up_t = swap_tensor(up_sum_r)
    down_rx = chips.scatter_start(down_sum_r, stages[0])
    hidden_grad, mixed_g_l, mixed_g_r, out_g_l, out_g_r, middle_sums = middle_back(
        where, b_l, after(b_r, up_sum_r, down_sum_r), hidden, out_grad, mixed_l, mixed_r,
        out_weight, out_other, row_vectors,
    )
    mixed_g_r, down_lx = together(mixed_g_r, down_lx)
    qkv_g_r, skip_g_r = attend_backward(
        qkv_r, skip_got, key_seg, query_seg, sums_r, turned_r, mixed_g_r
    )
    qkv_g_r, skip_g_r, down_rx = together(qkv_g_r, skip_g_r, down_rx)

    down_y = add(*down_rx)
    down_t = swap_tensor(down_y)
    qkv_keep_r, qkv_send_r, qkv_sums_r = project_grad(
        at, after(normed_ext, down_y), qkv_g_r, out_g_r
    )
    qkv_keep_r, qkv_send_r, up_t = together(qkv_keep_r, qkv_send_r, up_t)
    qkv_c_r = chips.swap_core(qkv_send_r)
    up_1 = add(up_l, up_t)
    up_x = chips.scatter_start(up_1, stages[0])
    lead = width // 6
    qkv_y_1 = add(qkv_keep_r[:lead], qkv_c_r[:lead])
    qkv_y_2 = add(qkv_keep_r[lead:], qkv_c_r[lead:])
    qkv_t_1 = swap_tensor(qkv_y_1)
    qkv_g_l, skip_g_l = attend_backward(
        qkv_l, skip_own, key_seg, query_seg, sums_l, turned_l, after(mixed_g_l, up_1, qkv_y_1, qkv_y_2)
    )
    qkv_g_l, skip_g_l, up_x, down_t, qkv_t_1 = together(qkv_g_l, skip_g_l, up_x, down_t, qkv_t_1)
    qkv_t_2 = swap_tensor(qkv_y_2)

    def rest(value):
        for stage in stages[3:]:
            value = chips.scatter(value, stage)
        for stage in reversed(stages[3:]):
            value = chips.gather(value, stage)
        return value

    factor = stages[0][1]
    up_rows = up_1.shape[0] // factor
    feed_2 = jnp.concatenate([add(*up_x), add(*down_lx, down_t)], axis=0)
    feed_x = chips.scatter_start(feed_2, stages[1])
    qkv_keep_l, qkv_send_l, qkv_sums_l = project_grad(
        at, after(normed_ext, feed_2), qkv_g_l, out_g_l
    )
    qkv_keep_l, qkv_send_l, qkv_sums_l, feed_x, qkv_t_2 = together(
        qkv_keep_l, qkv_send_l, qkv_sums_l, feed_x, qkv_t_2
    )
    qkv_c_l = chips.swap_core(qkv_send_l)
    feed_3 = add(*feed_x)
    feed_x = chips.scatter_start(feed_3, stages[2])

    qkv_1 = jnp.concatenate(
        [
            add(qkv_keep_l[:lead], qkv_c_l[:lead], qkv_t_1),
            add(qkv_keep_l[lead:], qkv_c_l[lead:], qkv_t_2),
        ],
        axis=0,
    )
    qkv_x = chips.scatter_start(qkv_1, stages[0])
    skip_back = swap_tensor(after(skip_g_r, qkv_1))
    input_grad, halo_grad, first_sums = first_back(
        where, at, after(qkv_g_l, qkv_1, feed_3), qkv_g_r, qkv_own, qkv_mine, qkv_theirs,
        block_input.reshape(tokens, width), halo, hidden_grad, row_vectors, rows,
    )
    input_grad, halo_grad, first_sums, qkv_x, feed_x = together(
        input_grad, halo_grad, first_sums, qkv_x, feed_x
    )

    qkv_2 = add(*qkv_x)
    qkv_x = chips.scatter_start(qkv_2, stages[1])
    feed_4 = rest(add(*feed_x))
    feed_x = chips.gather_start(after(feed_4, qkv_2), stages[2])
    own_small, other_small = small_step(
        where, at, middle_sums, after(first_sums, qkv_2, feed_4), qkv_sums_l, qkv_sums_r,
        bias_g_l1, bias_g_l2, bias_g_r1, bias_g_r2,
    )
    small_t = swap_tensor(other_small)
    halo_got = lax.ppermute(after(halo_grad, other_small), "tensor", [(1, 0)])
    skip_grad = skip_grad_of(at, after(skip_g_l, own_small), skip_back, rows)
    skip_grad, qkv_x, small_t = together(skip_grad, qkv_x, small_t)
    qkv_3 = add(*qkv_x)
    qkv_x = chips.scatter_start(qkv_3, stages[2])
    small = own_small + small_t
    small_c = chips.swap_core(small)
    block_output = block_half + after(f_r, small, qkv_3)
    block_output, small_c, feed_x = together(block_output, small_c, feed_x)
    feed_5 = chips.gather_finish(feed_x, stages[2])
    feed_x = chips.gather_start(feed_5, stages[1])
    small = small + small_c
    for stage in stages[3:]:
        small = sum(chips.gather_start(small, stage))
    columns = qkv_2.shape[1]
    small_rows = -(-where.size // (8 * columns)) * 8
    small = jnp.pad(small[0], (0, small_rows * columns - where.size)).reshape(small_rows, columns)
    small, qkv_x = together(after(small, feed_5), qkv_x)

    qkv_4 = jnp.concatenate([rest(add(*qkv_x)), small.astype(BF)], axis=0)
    qkv_x = chips.gather_start(qkv_4, stages[0])
    qkv_x, feed_x = together(qkv_x, feed_x)
    feed_6 = chips.gather_finish(feed_x, stages[1])
    up_6, down_6 = feed_6[:up_rows], feed_6[up_rows:]
    up_x = chips.gather_start(up_6, stages[0])
    qkv_5 = chips.gather_finish(qkv_x, stages[0])
    qkv_x = chips.gather_start(after(qkv_5, up_6), stages[2])
    qkv_x, up_x, down_6 = together(qkv_x, up_x, down_6)
    down_x = chips.gather_start(down_6, stages[0])
    up_7 = chips.gather_finish(up_x, stages[0])
    up_c = chips.swap_core(up_7)
    qkv_6 = chips.gather_finish(qkv_x, stages[2])
    qkv_x = chips.gather_start(after(qkv_6, up_7), stages[1])
    input_grad = add_halo(after(input_grad, qkv_6, up_7), halo_got, rows)
    up_weight_grad = up_out(at, after(up_7, input_grad), up_c)
    up_weight_grad, qkv_x, down_x = together(up_weight_grad, qkv_x, down_x)
    qkv_7 = chips.gather_finish(qkv_x, stages[1])
    qkv_other = chips.swap_core(qkv_7)
    down_7 = chips.gather_finish(down_x, stages[0])
    down_c = chips.swap_core(down_7)
    query_weight_grad, key_weight_grad, value_weight_grad, out_weight_grad, small = project_out(
        at, after(qkv_7, down_7), qkv_other, local, width // 2, factor**3
    )
    query_weight_grad, down_c = together(query_weight_grad, down_c)
    down_weight_grad = down_out(at, down_7, down_c)
    small = small.reshape(-1)

    return (
        block_output.reshape(rows, length, width),
        input_grad.reshape(rows, length, width),
        jnp.swapaxes(skip_grad, 1, 2),
        query_weight_grad,
        small[where.query],
        key_weight_grad,
        value_weight_grad.T,
        small[where.value],
        out_weight_grad,
        small[where.out],
        up_weight_grad,
        small[where.up],
        down_weight_grad,
        small[where.down],
        small[where.gain_1],
        small[where.shift_1],
        small[where.gain_2],
        small[where.shift_2],
    )


def solution(mesh):
    in_specs = (
        P("dp", "tensor", None),
        P("dp", None, "tensor"),
        P("dp", None),
        P("dp"),
        P(None, "tensor"),
        P("tensor"),
        P(None, "tensor"),
        P(None, "tensor"),
        P("tensor"),
        P("tensor", None),
        P(),
        P(None, "tensor"),
        P("tensor"),
        P("tensor", None),
        P(),
        P(),
        P(),
        P(),
        P(),
        P("dp", "tensor", None),
    )
    out_specs = (
        P("dp", "tensor", None),
        P("dp", "tensor", None),
        P("dp", None, "tensor"),
        P(None, "tensor"),
        P("tensor"),
        P(None, "tensor"),
        P(None, "tensor"),
        P("tensor"),
        P("tensor", None),
        P(),
        P(None, "tensor"),
        P("tensor"),
        P("tensor", None),
        P(),
        P(),
        P(),
        P(),
        P(),
    )
    return jax.shard_map(
        functools.partial(on_device, mesh.shape["dp"]),
        mesh=mesh,
        in_specs=in_specs,
        out_specs=out_specs,
        check_vma=False,
    )
```
